32 devices in a mesh: wide: 8 (over z, y), narrow: 4 (over x, core).
Axes of the slice: x: 2, y: 2, z: 4, core: 2. Of those that a mesh axis runs over, the one named last changes fastest.
Arguments:
- mobility: float32 [128, 64, 256], P('wide', 'narrow'), may hold values from 0.2 to 5
- sav_vector: float32 [128, 64, 256], P('wide', 'narrow'), may hold values from -8 to 8
- cotangent: float32 [128, 64, 256], P('wide', 'narrow'), may hold values from -8 to 8
Outputs:
- adjoint: float32 [128, 64, 256], P('wide', 'narrow')
The draws below stay inside these ranges and needn't reach their ends.
All inputs are finite; a program needn't handle non-finite values.
Results may differ from the reference program's by a relative error of at most 0.0019.
Values sent between devices are 32-bit elements; how exact they have to be, the bound alone decides.
A program may use at most 128 MiB of HBM per device.

```python
import math
import jax
import jax.numpy as jnp

NZ = 256
LEVELS = 5
NX = 128
NY = 64


def shared_part(key):
    return jax.random.normal(jax.random.fold_in(key, 7), (NX, NY, NZ), jnp.float32)


def draw_sav_vector(key, part):
    own_part = jax.random.normal(jax.random.fold_in(key, 11), (NX, NY, NZ), jnp.float32)
    return jnp.clip(shared_part(key) + 0.7 * own_part, -8.0, 8.0)


def draw_cotangent(key, part):
    own_part = jax.random.normal(jax.random.fold_in(key, 13), (NX, NY, NZ), jnp.float32)
    return jnp.clip(shared_part(key) + 0.7 * own_part, -8.0, 8.0)


def level_of(rng, dims, split, least, high):
    gain = 1.0
    for dim, blocks in split:
        steps = jax.random.uniform(jax.random.fold_in(jax.random.fold_in(rng, 6), dim), (blocks,), jnp.float32, least / len(split), high / len(split))
        gain = gain * jnp.repeat(jnp.exp(steps), dims[dim] // blocks).reshape((-1,) + (1,) * (len(dims) - 1 - dim))
    return gain


def setup_inputs(seed: int = 0) -> dict:
    seeds = jax.random.split(jax.random.key(seed), 4)
    mobility = jnp.clip(jnp.exp(math.log(5.0) - 3.218876 * jax.random.uniform(seeds[0], (NX, NY, NZ), jnp.float32) ** level_of(seeds[0], (NX, NY, NZ), ((0, 8), (1, 4)), -0.2, 0.2)), 0.2, 5.0)
    sav_vector = draw_sav_vector(jax.random.fold_in(seeds[3], 71), 0)
    cotangent = draw_cotangent(jax.random.fold_in(seeds[3], 71), 0)
    return {"mobility": mobility, "sav_vector": sav_vector, "cotangent": cotangent}


DAMPING = 0.8
BASE_TAU = 16.0


def face_terms(padded, tau):
    center = padded[1:-1, 1:-1, 1:-1]
    others = [padded[2:, 1:-1, 1:-1], padded[:-2, 1:-1, 1:-1], padded[1:-1, 2:, 1:-1],
              padded[1:-1, :-2, 1:-1], padded[1:-1, 1:-1, 2:], padded[1:-1, 1:-1, :-2]]
    couplings = jnp.stack([(0.5 * tau) * (center + other) for other in others]).astype(jnp.bfloat16)
    diagonal = jnp.float32(1.0) + couplings[0].astype(jnp.float32)
    for index in range(1, 6):
        diagonal = diagonal + couplings[index].astype(jnp.float32)
    return couplings, diagonal


def coarsen(values):
    count, size_x, size_y, size_z = values.shape
    blocks = values.reshape(count, size_x // 2, 2, size_y // 2, 2, size_z // 2, 2)
    return blocks.mean(axis=(2, 4, 6))


def refine(values):
    return jnp.repeat(jnp.repeat(jnp.repeat(values, 2, axis=1), 2, axis=2), 2, axis=3)


def operate(iterate, couplings, diagonal):
    padded = jnp.pad(iterate, ((0, 0), (1, 1), (1, 1), (1, 1)))
    others = [padded[:, 2:, 1:-1, 1:-1], padded[:, :-2, 1:-1, 1:-1], padded[:, 1:-1, 2:, 1:-1],
              padded[:, 1:-1, :-2, 1:-1], padded[:, 1:-1, 1:-1, 2:], padded[:, 1:-1, 1:-1, :-2]]
    total = couplings[0].astype(jnp.float32)[None] * others[0]
    for index in range(1, 6):
        total = total + couplings[index].astype(jnp.float32)[None] * others[index]
    return diagonal[None] * iterate - total


def relax_once(iterate, source, couplings, diagonal):
    return iterate + DAMPING * (source - operate(iterate, couplings, diagonal)) / diagonal[None]


def multigrid(source, level_index, operators):
    couplings, diagonal = operators[level_index]
    iterate = DAMPING * source / diagonal[None]
    if level_index == LEVELS - 1:
        return relax_once(iterate, source, couplings, diagonal)
    iterate = relax_once(iterate, source, couplings, diagonal)
    residual = source - operate(iterate, couplings, diagonal)
    correction = multigrid(coarsen(residual), level_index + 1, operators)
    iterate = iterate + refine(correction)
    iterate = relax_once(iterate, source, couplings, diagonal)
    return relax_once(iterate, source, couplings, diagonal)


def reference(mobility, sav_vector, cotangent):
    operators = []
    mobile = mobility
    for level_index in range(LEVELS):
        operators.append(face_terms(jnp.pad(mobile, 1), BASE_TAU / 4.0 ** level_index))
        if level_index + 1 < LEVELS:
            mobile = coarsen(mobile[None])[0]
    adjoint_b = multigrid(sav_vector[None], 0, operators)[0]
    numerator = jnp.sum(adjoint_b * cotangent)
    denominator = jnp.sum(sav_vector * adjoint_b)
    sav_ratio = numerator / (1.0 + denominator)
    return multigrid((cotangent - sav_ratio * sav_vector)[None], 0, operators)[0]
```

```python
import functools
import jax
import jax.numpy as jnp
from jax import lax
from jax.experimental import pallas as pl
from jax.experimental.pallas import tpu as pltpu
from jax.sharding import PartitionSpec as P

DAMPING = 0.8
KEEP = 1.0 - DAMPING
BASE_TAU = 16.0
H0 = 4
H1 = 4
PAD = 2
PAD2 = 4
MESH = pl.DeviceIdType.MESH
F32 = jnp.float32
SIDES = [(-1, 0), (1, 0), (0, -1), (0, 1), (-1, -1), (-1, 1), (1, -1), (1, 1)]
OPPOSITE = [1, 0, 3, 2, 7, 6, 5, 4]
TILE = (8, 128)


def iota(shape, dim):
    return lax.broadcasted_iota(jnp.int32, shape, dim)


def shift(value, amount, axis):
    return pltpu.roll(value, amount % value.shape[axis], axis)


def take(value, index, axis):
    return jnp.take_along_axis(value, index, axis=axis)


def z_pairs(tile):
    return take(tile + shift(tile, -1, 1), lax.rem(2 * iota(TILE, 1), 128), 1)


def put_halves(ref, v, at, value):
    for h in range(2):
        ref[v, h, at, :] = value[:, 128 * h : 128 * h + 128]


def yz_pairs(ref, v, at):
    halves = []
    for h in range(2):
        halves.append(z_pairs(ref[v, h, pl.ds(at, 8, stride=2), :] + ref[v, h, pl.ds(at + 1, 8, stride=2), :]))
    return jnp.where(iota(TILE, 1) < 64, halves[0], halves[1])


def z_repeat(tile, start=0):
    return take(tile, start + iota(TILE, 1) // 2, 1)


def y_pairs(tile):
    return take(tile + shift(tile, -1, 0), lax.rem(2 * iota(TILE, 0), 8), 0)


def y_repeat(tile, start=0):
    return take(tile, jnp.clip(start + iota(TILE, 0) // 2, 0, 7), 0)


def top_bottom(top, bottom):
    return jnp.where(iota(TILE, 0) < 4, top, bottom)


def rounded(x):
    return x.astype(jnp.bfloat16).astype(F32)


def slabs(lo, count, chunk, body):
    if count == chunk:
        for k in range(chunk):
            body(lo + k)
        return

    def step(i, _):
        for k in range(chunk):
            body(lo + i * chunk + k)
        return 0

    lax.fori_loop(0, count // chunk, step, 0)


def build(m, cx, cy, cz, rd, d, lo, count, tau, seg, chunk, firsts=()):
    shape = m.shape[1:]
    row = iota(shape, 0)
    lane = lax.rem(iota(shape, 1), seg)
    last_row, first_row = row == shape[0] - 1, row == 0
    last_lane, first_lane = lane == seg - 1, lane == 0
    half = 0.5 * tau

    def body(a):
        own = m[a]
        xp, xm = m[a + 1], m[a - 1]
        yp = jnp.where(last_row, 0.0, shift(own, -1, 0))
        ym = jnp.where(first_row, 0.0, shift(own, 1, 0))
        zp = jnp.where(last_lane, 0.0, shift(own, -1, 1))
        zm = jnp.where(first_lane, 0.0, shift(own, 1, 1))
        total = 1.0
        for other, ref in ((xp, cx), (xm, None), (yp, cy), (ym, None), (zp, cz), (zm, None)):
            face = rounded(half * (own + other))
            total = total + face
            if ref is not None:
                ref[a] = jnp.where(jnp.minimum(own, other) > 0.0, face, 0.0)
        inverse = DAMPING / total
        rd[a] = inverse
        if d is not None:
            d[a] = total
        for r, u in firsts:
            u[a] = inverse * r[a]

    slabs(lo, count, chunk, body)


def neighbours(v, a, cx, cy, cz):
    own = v[a]
    cya, cza = cy[a], cz[a]
    total = cx[a] * v[a + 1] + cx[a - 1] * v[a - 1]
    total = total + (cya * shift(own, -1, 0) + shift(cya * own, 1, 0))
    total = total + (cza * shift(own, -1, 1) + shift(cza * own, 1, 1))
    return own, total


def sweep(vin, vout, r, ops, lo, count, chunk):
    cx, cy, cz, rd, d = ops

    def body(a):
        for vi, vo, ri in zip(vin, vout, r):
            own, t = neighbours(vi, a, cx, cy, cz)
            vo[a] = KEEP * own + rd[a] * (ri[a] + t)

    slabs(lo, count, chunk, body)


def residual(vi, ri, a, ops):
    cx, cy, cz, rd, d = ops
    own, t = neighbours(vi, a, cx, cy, cz)
    diag = d[a] if d is not None else DAMPING / rd[a]
    return own, ri[a] + t - diag * own


def fold(x):
    total = None
    for i in range(x.shape[0] // 8):
        for j in range(x.shape[1] // 128):
            part = x[8 * i : 8 * i + 8, 128 * j : 128 * j + 128]
            total = part if total is None else total + part
    return total


def fold_own(x):
    total = None
    for j in range(x.shape[1] // 128):
        lanes = slice(128 * j, 128 * j + 128)
        part = x[8:16, lanes] + top_bottom(x[16:24, lanes], x[0:8, lanes])
        total = part if total is None else total + part
    return total


def kernel(nw, nn, bx, by, nz, m_hbm, s_hbm, c_hbm, out_ref,
           m_ref, s_ref, c_ref,
           m0, cx0, cy0, cz0, rd0, d0, rs0, rc0, us0, uc0, vs0, vc0,
           rx, yp, ry, cp, rcn, xv, hx, yv, hy,
           m1, cx1, cy1, cz1, rd1, d1, r1, u1, v1, w1, h1,
           cx2, cy2, cz2, rd2, r2, u2, v2,
           cx3, cy3, cz3, rd3, r3, u3, v3,
           cx4, cy4, cz4, rd4, r4, u4, v4,
           t0, sm2, sr2, sp2, gm, gr, gp, pb, pbs, f1p, tok,
           ins, ss, gs, gq, e0r, m1r, r1r, v0r, v1r):
    iw, ino = lax.axis_index("wide"), lax.axis_index("narrow")
    b1x, b1y, z1 = bx // 2, by // 2, nz // 2
    b2x, b2y, z2 = bx // 4, by // 4, nz // 4
    x2, x3, x4 = nw * b2x, nw * b2x // 2, nw * b2x // 4
    there = []
    for dx, dy in SIDES:
        ok = None
        for cond, on in ((iw > 0, dx < 0), (iw < nw - 1, dx > 0), (ino > 0, dy < 0), (ino < nn - 1, dy > 0)):
            if on:
                ok = cond if ok is None else jnp.logical_and(ok, cond)
        there.append(ok)

    def peer(side):
        return (iw + SIDES[side][0], ino + SIDES[side][1])

    inputs = [pltpu.make_async_copy(src, dst, ins.at[i])
              for i, (src, dst) in enumerate(((m_hbm, m_ref), (s_hbm, s_ref), (c_hbm, c_ref)))]
    for copy in inputs:
        copy.start()

    def clear(ref, index):
        ref[index] = jnp.zeros(ref[index].shape, F32)

    for k in range(2):
        for ref in (rx, ry, hx, hy):
            for i in range(ref.shape[1]):
                clear(ref, (k, i))
    for k in range(4):
        clear(rcn, k)
    for k in range(2):
        for i in range(h1.shape[1]):
            clear(h1, (k, i))
    side_rows = (slice(0, b1y), slice(2 * b1y, 3 * b1y))
    for a in (0, 1, 2, 3, H1 + b1x, H1 + b1x + 1, H1 + b1x + 2, H1 + b1x + 3):
        clear(m1, (0, a))
    for a in (H1 - 2, H1 - 1, H1 + b1x, H1 + b1x + 1):
        for v in range(2):
            clear(r1, (v, a))
    for a in range(H1, H1 + b1x):
        for rows in side_rows:
            clear(m1, (0, a, rows))
            for v in range(2):
                clear(r1, (v, a, rows))

    barrier = pltpu.get_barrier_semaphore()

    def greet(j, _):
        pl.semaphore_signal(barrier, inc=1, device_id=(lax.rem(iw + j, nw), ino), device_id_type=MESH)
        return 0

    lax.fori_loop(1, nw, greet, 0)
    for j in range(1, nn):
        pl.semaphore_signal(barrier, inc=1, device_id=(iw, lax.rem(ino + j, nn)), device_id_type=MESH)
    for k in range(4, 8):
        @pl.when(there[k])
        def _():
            pl.semaphore_signal(barrier, inc=1, device_id=peer(k), device_id_type=MESH)

    for copy in inputs:
        copy.wait()
    for side, (m_lo, r_lo) in enumerate(((0, 0), (by - 3, by - 2))):
        for k in range(3):
            yp[side, k] = m_ref[:, m_lo + k, :]
        for k in range(2):
            yp[side, 3 + k] = s_ref[:, r_lo + k, :]
            yp[side, 5 + k] = c_ref[:, r_lo + k, :]
    for k in range(4, 8):
        dx, dy = SIDES[k]
        xa, xb = (0, 1) if dx < 0 else (bx - 1, bx - 2)
        ya, yb = (0, 1) if dy < 0 else (by - 1, by - 2)
        for i, (ref, x, y) in enumerate(((m_ref, xa, ya), (m_ref, xa, yb), (m_ref, xb, ya),
                                         (s_ref, xa, ya), (c_ref, xa, ya))):
            cp[k - 4, i : i + 1, :] = ref[x, y : y + 1, :]

    beside_x = jnp.minimum(iw, 1) + jnp.minimum(nw - 1 - iw, 1)
    beside_y = jnp.minimum(ino, 1) + jnp.minimum(nn - 1 - ino, 1)
    pl.semaphore_wait(barrier, nw + nn - 2 + beside_x * beside_y)

    def remote(src, dst, ssem, rsem, dev):
        return pltpu.make_async_remote_copy(src_ref=src, dst_ref=dst, send_sem=ssem, recv_sem=rsem,
                                            device_id=dev, device_id_type=MESH)

    def to_side(side, pairs, rsem):
        return [remote(src, dst, ss.at[side], rsem.at[OPPOSITE[side]], peer(side)) for src, dst in pairs]

    def e0_sends(side):
        land = OPPOSITE[side]
        if side < 2:
            pairs = []
            at = 0
            for ref, width in ((m_ref, 3), (s_ref, 2), (c_ref, 2)):
                lo = 0 if side == 0 else bx - width
                pairs.append((ref.at[lo : lo + width], rx.at[land, at : at + width]))
                at += width
            return to_side(side, pairs, e0r)
        if side < 4:
            return to_side(side, [(yp.at[side - 2], ry.at[land - 2])], e0r)
        return to_side(side, [(cp.at[side - 4], rcn.at[land - 4])], e0r)

    def box1(side, sending, width, corner):
        dx, dy = SIDES[side]
        w = corner if dx and dy else width
        if sending:
            xlo, w = (H1, w) if dx < 0 else ((H1 + b1x - w, w) if dx > 0 else (H1, b1x))
            ylo = b1y
        else:
            xlo, w = (H1 - w, w) if dx < 0 else ((H1 + b1x, w) if dx > 0 else (H1, b1x))
            ylo = b1y * (1 + dy)
        return xlo, w, ylo

    def level1_sends(ref, rsem, side, width, corner):
        sx, w, sy = box1(side, True, width, corner)
        tx, _, ty = box1(OPPOSITE[side], False, width, corner)
        return to_side(side, [(ref.at[:, sx : sx + w, sy : sy + b1y], ref.at[:, tx : tx + w, ty : ty + b1y])], rsem)

    def level1_landed(ref, rsem, width, corner):
        def fn(side):
            tx, w, ty = box1(side, False, width, corner)
            view = ref.at[:, tx : tx + w, ty : ty + b1y]
            pltpu.make_async_copy(view, view, rsem.at[side]).wait()
        return fn

    def each(fn, sides=range(8)):
        for side in sides:
            @pl.when(there[side])
            def _():
                fn(side)

    def start(copies):
        for copy in copies:
            copy.start()

    def e0_landed(side):
        view = rx.at[side] if side < 2 else (ry.at[side - 2] if side < 4 else rcn.at[side - 4])
        pltpu.make_async_copy(view, view, e0r.at[side]).wait()

    each(lambda k: start(e0_sends(k)), (0, 1, 2, 3, 4, 5, 6, 7))

    own_y = slice(b1y, 2 * b1y)
    for i in range(b1x):
        put_halves(t0, 0, slice(i * by, (i + 1) * by), m_ref[2 * i] + m_ref[2 * i + 1])
    for i in range(b1x):
        m1[0, H1 + i, own_y, :] = 0.125 * yz_pairs(t0, 0, i * by)
    for i in range(0, b2x, 2):
        quads = [y_pairs(m1[0, H1 + 2 * k, own_y, :] + m1[0, H1 + 2 * k + 1, own_y, :]) for k in (i, i + 1)]
        mob2 = 0.125 * z_pairs(top_bottom(quads[0], quads[1]))
        sm2[i * b2y : (i + 2) * b2y, :] = mob2
        gm[ino, iw, i * b2y : (i + 2) * b2y, :] = mob2

    def over_wide(src, dst, kind):
        def step(j, _):
            to = lax.rem(iw + j, nw)
            remote(src, dst(iw), gs.at[kind], gq.at[kind], (to, ino)).start()
            return 0

        lax.fori_loop(1, nw, step, 0)

    def over_narrow(src, dst, kind):
        for j in range(1, nn):
            to = lax.rem(ino + j, nn)
            remote(src, dst(ino), gs.at[kind], gq.at[kind], (iw, to)).start()

    def landed(view, kind):
        pltpu.make_async_copy(view, view, gq.at[kind]).wait()

    wide_m = lambda: landed(gm.at[0, 0 : nw - 1], 0)
    narrow_m = lambda: landed(gm.at[0 : nn - 1], 1)
    wide_r = lambda: landed(gr.at[0, 0 : nw - 1], 2)
    narrow_r = lambda: landed(gr.at[0 : nn - 1], 3)
    wide_p = lambda: landed(gp.at[0 : nw - 1], 4)
    narrow_p = lambda: landed(pbs.at[0 : nn - 1], 5)

    for ref, src, width in ((m0, m_ref, 3), (rs0, s_ref, 2), (rc0, c_ref, 2)):
        blank = jnp.zeros(m0.shape[1:], F32)
        for i in range(width):
            ref[H0 - 1 - i] = blank
            ref[H0 + bx + i] = blank

        def put(i, _):
            ref[H0 + i, H0 : H0 + by, :] = src[i]
            return 0

        lax.fori_loop(0, bx, put, 0)
    for ref in (u3, v3, u4, v4):
        zero = jnp.zeros(ref.shape[1:], F32)
        for a in (0, 1, ref.shape[0] - 2, ref.shape[0] - 1):
            ref[a] = zero
    for ref in (u2, v2, r2, cx2, cy2, cz2, rd2):
        zero = jnp.zeros(ref.shape[1:], F32)
        for a in range(PAD2):
            ref[a] = zero
            ref[ref.shape[0] - 1 - a] = zero
    for ref in (cx3, cx4):
        ref[PAD - 1] = jnp.zeros(ref.shape[1:], F32)

    each(e0_landed, (2, 3))
    fields = ((m0, 0, 3), (rs0, 3, 2), (rc0, 5, 2))
    for ref, at, width in fields:
        for i in range(width):
            ref[H0 : H0 + bx, H0 - width + i, :] = ry[0, at + i]
            ref[H0 : H0 + bx, H0 + by + i, :] = ry[1, at + i]

    ops0 = (cx0, cy0, cz0, rd0, d0)
    firsts0 = ((rs0, us0), (rc0, uc0))

    build(m0, cx0, cy0, cz0, rd0, d0, H0 + 1, bx - 2, BASE_TAU, nz, 2, firsts0)
    sweep((us0, uc0), (vs0, vc0), (rs0, rc0), ops0, H0 + 2, bx - 4, 2)
    each(lambda k: start(level1_sends(m1, m1r, k, 3, 3)))
    over_wide(sm2, lambda w: gm.at[ino, w], 0)

    def down0(i, carry):
        num, den = carry
        sums = []
        for k in range(2):
            a = H0 + 2 * i + k
            vs, es = residual(vs0, rs0, a, ops0)
            vc, ec = residual(vc0, rc0, a, ops0)
            both = es + rs0[a]
            num = num + fold_own(both * vc)
            den = den + fold_own(both * vs)
            sums.append((es, ec))
        at = pl.ds(pl.multiple_of(i * m0.shape[1], 8), m0.shape[1])
        put_halves(t0, 0, at, sums[0][0] + sums[1][0])
        put_halves(t0, 1, at, sums[0][1] + sums[1][1])
        return num, den

    zero8 = jnp.zeros(TILE, F32)
    part0 = lax.fori_loop(2, b1x - 2, down0, (zero8, zero8))

    each(e0_landed, (0, 1, 4, 5, 6, 7))
    for ref, at, width in fields:
        for i in range(width):
            ref[H0 - width + i, H0 : H0 + by, :] = rx[0, at + i]
            ref[H0 + bx + i, H0 : H0 + by, :] = rx[1, at + i]
    for k in range(4):
        dx, dy = SIDES[4 + k]
        xa, xb = (H0 - 1, H0 - 2) if dx < 0 else (H0 + bx, H0 + bx + 1)
        ya, yb = (H0 - 1, H0 - 2) if dy < 0 else (H0 + by, H0 + by + 1)
        for i, (ref, x, y) in enumerate(((m0, xa, ya), (m0, xa, yb), (m0, xb, ya), (rs0, xa, ya), (rc0, xa, ya))):
            ref[x, y : y + 1, :] = rcn[k, i : i + 1, :]
    for lo, v_lo in ((H0 - 2, H0 - 1), (H0 + bx - 1, H0 + bx - 2)):
        build(m0, cx0, cy0, cz0, rd0, d0, lo, 3, BASE_TAU, nz, 1, firsts0)
        sweep((us0, uc0), (vs0, vc0), (rs0, rc0), ops0, v_lo, 3, 1)
    part0 = lax.fori_loop(0, 2, down0, part0)
    num0, den0 = lax.fori_loop(b1x - 2, b1x, down0, part0)
    for v in range(2):
        for i in range(b1x):
            r1[v, H1 + i, own_y, :] = 0.125 * yz_pairs(t0, v, i * m0.shape[1] + H0)
    each(lambda k: start(level1_sends(r1, r1r, k, 2, 1)))
    wide_m()
    over_narrow(gm.at[ino], lambda n: gm.at[n], 1)
    for side, (x_far, x_near) in enumerate(((H0 + 1, H0), (H0 + bx - 2, H0 + bx - 1))):
        for v, ref in enumerate((vs0, vc0)):
            xv[side, v, 0:by, :] = ref[x_far, H0 : H0 + by, :]
            xv[side, v, by : by + 1, :] = ref[x_near, H0 - 1 : H0, :]
            xv[side, v, by + 1 : by + 2, :] = ref[x_near, H0 + by : H0 + by + 1, :]
    for side, col in enumerate((H0 + 1, H0 + by - 2)):
        for v, ref in enumerate((vs0, vc0)):
            yv[side, v] = ref[H0 : H0 + bx, col, :]

    def v0_sends(side):
        land = OPPOSITE[side]
        src, dst = (xv.at[side], hx.at[land]) if side < 2 else (yv.at[side - 2], hy.at[land - 2])
        return to_side(side, [(src, dst)], v0r)

    each(lambda k: start(v0_sends(k)), range(4))
    each(level1_landed(m1, m1r, 3, 3))
    ops1 = (cx1, cy1, cz1, rd1, d1)
    build(m1.at[0], cx1, cy1, cz1, rd1, d1, H1 - 3, b1x + 6, BASE_TAU / 4, z1, 2)
    each(level1_landed(r1, r1r, 2, 1))
    rr1 = (r1.at[0], r1.at[1])
    uu1 = (u1.at[0], u1.at[1])
    vv1 = (v1.at[0], v1.at[1])

    def first1(a):
        for v in range(2):
            u1[v, a] = rd1[a] * r1[v, a]

    slabs(H1 - 2, b1x + 4, 2, first1)
    sweep(uu1, vv1, rr1, ops1, H1 - 1, b1x + 2, 2)
    num1, den1 = zero8, zero8
    quads = []
    for i in range(b2x):
        pair = []
        for k in range(2):
            a = H1 + 2 * i + k
            vs, es = residual(vv1[0], rr1[0], a, ops1)
            vc, ec = residual(vv1[1], rr1[1], a, ops1)
            both = (es + r1[0, a])[own_y]
            num1 = num1 + both * vc[own_y]
            den1 = den1 + both * vs[own_y]
            pair.append((es[own_y], ec[own_y]))
        quads.append([y_pairs(pair[0][v] + pair[1][v]) for v in range(2)])
        if i % 2:
            packed = [z_pairs(top_bottom(quads[i - 1][v], quads[i][v])) for v in range(2)]
            own2 = 0.125 * jnp.where(iota(TILE, 1) < z2, packed[0], packed[1])
            sr2[(i - 1) * b2y : (i + 1) * b2y, :] = own2
            gr[ino, iw, (i - 1) * b2y : (i + 1) * b2y, :] = own2
    over_wide(sr2, lambda w: gr.at[ino, w], 2)
    num_row = jnp.sum(num0 + 8.0 * num1, axis=0, keepdims=True)
    den_row = jnp.sum(den0 + 8.0 * den1, axis=0, keepdims=True)
    row8 = iota(TILE, 0)
    part = jnp.where(row8 == 0, num_row, jnp.where(row8 == 1, den_row, 0.0))
    sp2[...] = part
    gp[iw] = part
    over_wide(sp2, lambda w: gp.at[w], 4)

    narrow_m()

    def unpack(src, dst):
        def step(w, _):
            for n in range(nn):
                for i in range(b2x):
                    dst[PAD2 + w * b2x + i, n * b2y : (n + 1) * b2y, :] = src[n, w, i * b2y : (i + 1) * b2y, :]
            return 0

        lax.fori_loop(0, nw, step, 0)

    unpack(gm, v2)
    build(v2, cx2, cy2, cz2, rd2, None, PAD2, x2, BASE_TAU / 16, z2, 8)

    def coarsen(x):
        if x.shape[0] == 16:
            return 0.125 * z_pairs(top_bottom(y_pairs(x[0:8]), y_pairs(x[8:16])))
        return 0.125 * z_pairs(top_bottom(y_pairs(x), 0.0))

    def coarsen_pairs(get, xc, pad, dst):
        def step(g, _):
            for k in range(4):
                a = pad + 2 * (4 * g + k)
                dst[PAD + 4 * g + k] = coarsen(get(a) + get(a + 1))
            return 0

        lax.fori_loop(0, xc // 4, step, 0)

    coarsen_pairs(lambda a: v2[a], x3, PAD2, v3)
    build(v3, cx3, cy3, cz3, rd3, None, PAD, x3, BASE_TAU / 64, z2 // 2, 4)
    coarsen_pairs(lambda a: v3[a], x4, PAD, v4)
    build(v4, cx4, cy4, cz4, rd4, None, PAD, x4, BASE_TAU / 256, z2 // 4, 4)

    wide_r()
    over_narrow(gr.at[ino], lambda n: gr.at[n], 3)

    def v1_sends(side):
        land = OPPOSITE[side]
        pairs = []
        for v in range(2):
            lo = H1 if side == 0 else H1 + b1x - 3
            pairs.append((v1.at[v, lo : lo + 3], h1.at[land, 3 * v : 3 * v + 3]))
        for v in range(2):
            lo = H1 if side == 0 else H1 + b1x - 2
            pairs.append((r1.at[v, lo : lo + 2], h1.at[land, 6 + 2 * v : 8 + 2 * v]))
        return to_side(side, pairs, v1r)

    each(lambda k: start(v1_sends(k)), range(2))

    def v0_landed(side):
        view = hx.at[side] if side < 2 else hy.at[side - 2]
        pltpu.make_async_copy(view, view, v0r.at[side]).wait()

    each(v0_landed, range(4))
    for side, (x_far, x_near) in enumerate(((H0 - 2, H0 - 1), (H0 + bx + 1, H0 + bx))):
        for v, ref in enumerate((vs0, vc0)):
            ref[x_far, H0 : H0 + by, :] = hx[side, v, 0:by, :]
            ref[x_near, H0 - 1 : H0, :] = hx[side, v, by : by + 1, :]
            ref[x_near, H0 + by : H0 + by + 1, :] = hx[side, v, by + 1 : by + 2, :]
    for side, col in enumerate((H0 - 2, H0 + by + 1)):
        for v, ref in enumerate((vs0, vc0)):
            ref[H0 : H0 + bx, col, :] = hy[side, v]
    narrow_r()
    unpack(gr, r2)

    ops2 = (cx2, cy2, cz2, rd2, None)
    ops3 = (cx3, cy3, cz3, rd3, None)
    ops4 = (cx4, cy4, cz4, rd4, None)

    def down(u, v, r, ops, pad, xc):
        def first(a):
            u[a] = ops[3][a] * r[a]

        slabs(pad, xc, 4, first)
        sweep((u,), (v,), (r,), ops, pad, xc, 8)

    down(u2, v2, r2, ops2, PAD2, x2)
    low2 = iota(v2.shape[1:], 1) < z2

    def coarsen2(g, carry):
        num, den = carry
        for k in range(2):
            pair = []
            for j in range(2):
                a = PAD2 + 2 * (2 * g + k) + j
                v, e = residual(v2, r2, a, ops2)
                both = jnp.where(low2, e + r2[a], 0.0)
                num = num + fold(both * shift(v, z2, 1))
                den = den + fold(both * v)
                pair.append(e)
            r3[PAD + 2 * g + k] = coarsen(pair[0] + pair[1])
        return num, den

    num2, den2 = lax.fori_loop(0, x3 // 2, coarsen2, (zero8, zero8))
    wide_p()
    total = gp[0]
    if nw <= 16:
        for w in range(1, nw):
            total = total + gp[w]
    else:
        total = lax.fori_loop(1, nw, lambda w, acc: acc + gp[w], total)
    pb[...] = total
    over_narrow(pb, lambda n: pbs.at[n], 5)
    down(u3, v3, r3, ops3, PAD, x3)
    coarsen_pairs(lambda a: residual(v3, r3, a, ops3)[1], x4, PAD, r4)
    down(u4, v4, r4, ops4, PAD, x4)

    def up3(g, _):
        for k in range(4):
            add = y_repeat(z_repeat(v4[PAD + 4 * g + k]))
            a = PAD + 2 * (4 * g + k)
            v3[a] = v3[a] + add
            v3[a + 1] = v3[a + 1] + add
        return 0

    lax.fori_loop(0, x4 // 4, up3, 0)
    sweep((v3,), (u3,), (r3,), ops3, PAD, x3, 8)
    sweep((u3,), (v3,), (r3,), ops3, PAD, x3, 8)
    low3 = iota(TILE, 1) < z2 // 2

    def dots(i, carry):
        num, den = carry
        for k in range(4):
            a = PAD + 4 * i + k
            both = jnp.where(low3, v3[a], 0.0)
            den = den + both * r3[a]
            num = num + both * shift(r3[a], -(z2 // 2), 1)
        return num, den

    num3, den3 = lax.fori_loop(0, x3 // 4, dots, (zero8, zero8))
    base = PAD2 + iw * b2x
    for i in range(b2x // 2 + 4):
        wide_tile = z_repeat(v3[PAD + iw * (b2x // 2) - 2 + i])
        for j in range(2):
            a = base - 4 + 2 * i + j
            v2[a, 0:8, :] = v2[a, 0:8, :] + y_repeat(wide_tile)
            v2[a, 8:16, :] = v2[a, 8:16, :] + y_repeat(wide_tile, 4)
    sweep((v2,), (u2,), (r2,), ops2, base - 3, b2x + 6, b2x + 6)
    sweep((u2,), (v2,), (r2,), ops2, base - 2, b2x + 4, b2x + 4)

    narrow_p()
    whole = total
    for j in range(1, nn):
        whole = whole + pbs[lax.rem(ino + j, nn)]
    num = jnp.sum(jnp.where(row8 == 0, whole, 0.0) + 64.0 * num2 + 512.0 * num3)
    den = jnp.sum(jnp.where(row8 == 1, whole, 0.0) + 64.0 * den2 + 512.0 * den3)
    ratio = (jnp.full(TILE, num) / (1.0 + jnp.full(TILE, den)))[0:1, :]

    def v1_landed(side):
        pltpu.make_async_copy(h1.at[side], h1.at[side], v1r.at[side]).wait()

    each(v1_landed, range(2))
    rows2 = v2.shape[1]
    full_y = 2 * rows2
    for i in range(b2x + 4):
        f1p[i, 0:b1y, :] = jnp.zeros((b1y, z1), F32)
        f1p[i, b1y + full_y : 2 * b1y + full_y, :] = jnp.zeros((b1y, z1), F32)
        for j in range(rows2 // 8):
            e = v2[base - 2 + i, 8 * j : 8 * j + 8, :]
            part = z_repeat(shift(e, z2, 1) - ratio * e)
            f1p[i, pl.ds(b1y + 16 * j, 8, stride=2), :] = part
            f1p[i, pl.ds(b1y + 16 * j + 1, 8, stride=2), :] = part
    window = pl.ds(pl.multiple_of(ino * b1y, 8), 3 * b1y)
    for x in range(-3, b1x + 3):
        a = H1 + x
        side, at = (0, x + 3) if x < 0 else (1, x - b1x)
        far = x < 0 or x >= b1x
        vs, vc = (h1[side, at], h1[side, 3 + at]) if far else (v1[0, a], v1[1, a])
        u1[0, a] = vc - ratio * vs + f1p[x // 2 + 2, window, :]
        if -2 <= x < b1x + 2:
            at = x + 2 if x < 0 else x - b1x
            rs, rc = (h1[side, 6 + at], h1[side, 8 + at]) if far else (r1[0, a], r1[1, a])
            w1[a] = rc - ratio * rs
    sweep((u1.at[0],), (u1.at[1],), (w1,), ops1, H1 - 2, b1x + 4, 2)
    sweep((u1.at[1],), (u1.at[0],), (w1,), ops1, H1 - 1, b1x + 2, 2)

    ratio0 = jnp.concatenate([ratio] * (nz // 128), axis=1)

    def up0(i, _):
        tiles = [u1[0, H1 - 1 + i, 8 * j : 8 * j + 8, :] for j in range(3)]
        rows = [top_bottom(y_repeat(tiles[0], 6), y_repeat(tiles[1], -2)),
                y_repeat(tiles[1], 2),
                top_bottom(y_repeat(tiles[1], 6), y_repeat(tiles[2], -2))]
        add = jnp.concatenate([jnp.concatenate([z_repeat(t), z_repeat(t, 64)], axis=1) for t in rows], axis=0)
        for k in range(2):
            a = H0 - 2 + 2 * i + k
            us0[a] = vc0[a] - ratio0 * vs0[a] + add
            rc0[a] = rc0[a] - ratio0 * rs0[a]
        return 0

    lax.fori_loop(0, b1x + 2, up0, 0)
    sweep((us0,), (uc0,), (rc0,), ops0, H0 - 1, bx + 2, 2)

    def last(a):
        own, t = neighbours(uc0, a, cx0, cy0, cz0)
        out_ref[a - H0] = (KEEP * own + rd0[a] * (rc0[a] + t))[H0 : H0 + by]

    slabs(H0, bx, 2, last)

    def sent(side):
        dx, dy = SIDES[side]
        if dy == 0:
            tiles = 7 * by * nz // 1024 + 3 + 4 + 2 * (by + 8) * nz // 1024 + 30
        elif dx == 0:
            tiles = 7 * bx * nz // 1024 + b1x + 2 * b1x + 2 * bx * nz // 1024
        else:
            tiles = 2 + 3 + 2
        view = tok.at[0:tiles]
        pltpu.make_async_copy(view, view, ss.at[side]).wait()

    each(sent)
    for kind, view in enumerate((gm.at[0, 0 : nw - 1], gm.at[0 : nn - 1], gr.at[0, 0 : nw - 1],
                                 gr.at[0 : nn - 1], gp.at[0 : nw - 1], pbs.at[0 : nn - 1])):
        pltpu.make_async_copy(view, view, gs.at[kind]).wait()


def solution(mesh):
    nw, nn = mesh.shape["wide"], mesh.shape["narrow"]

    def per_device(mobility, sav_vector, cotangent):
        bx, by, nz = mobility.shape
        b1x, b1y, z1 = bx // 2, by // 2, nz // 2
        x2, y2 = nw * bx // 4, nn * by // 4
        own = (bx, by, nz)
        l0 = (bx + 2 * H0, by + 2 * H0, nz)
        l1 = (b1x + 2 * H1, 3 * b1y, z1)
        l2 = (x2 + 2 * PAD2, y2, z1)
        l3 = (x2 // 2 + 2 * PAD, y2 // 2, z1)
        l4 = (x2 // 4 + 2 * PAD, 8, z1)
        own2 = (bx // 4 * (by // 4), z1)
        buffers = (
            [own] * 3 + [l0] * 12
            + [(2, 7, by, nz), (2, 7, bx, nz), (2, 7, bx, nz), (4, 8, nz), (4, 8, nz)]
            + [(2, 2, by + 8, nz)] * 2 + [(2, 2, bx, nz)] * 2
            + [(1, *l1)] + [l1] * 5 + [(2, *l1)] * 3 + [l1] + [(2, 10, 3 * b1y, z1)]
            + [l2] * 7 + [l3] * 7 + [l4] * 7
            + [(2, 2, b1x * l0[1], nz // 2)]
            + [own2, own2, TILE, (nn, nw, *own2), (nn, nw, *own2), (nw, *TILE), TILE, (nn, *TILE)]
            + [(bx // 4 + 4, 2 * y2 + 2 * b1y, z1), (128, *TILE)]
        )
        size = sum(4 * functools.reduce(lambda p, q: p * q, shape) for shape in buffers)
        dma = lambda n: pltpu.SemaphoreType.DMA((n,))
        scratch = [pltpu.VMEM(shape, F32) for shape in buffers]
        scratch += [dma(n) for n in (3, 8, 6, 6, 8, 8, 8, 4, 2)]
        return pl.pallas_call(
            functools.partial(kernel, nw, nn, bx, by, nz),
            out_shape=jax.ShapeDtypeStruct((bx, by, nz), F32),
            in_specs=[pl.BlockSpec(memory_space=pltpu.HBM)] * 3,
            out_specs=pl.BlockSpec(memory_space=pltpu.VMEM),
            scratch_shapes=scratch,
            compiler_params=pltpu.CompilerParams(
                collective_id=0, has_side_effects=True, vmem_limit_bytes=min(67043328, size + (8 << 20))
            ),
        )(mobility, sav_vector, cotangent)

    spec = P("wide", "narrow", None)
    return jax.shard_map(per_device, mesh=mesh, in_specs=(spec,) * 3, out_specs=spec, check_vma=False)
```

```python
import functools
import jax
import jax.numpy as jnp
from jax import lax
from jax.experimental import pallas as pl
from jax.experimental.pallas import tpu as pltpu
from jax.sharding import PartitionSpec as P

DAMPING = 0.8
KEEP = 1.0 - DAMPING
BASE_TAU = 16.0
H0 = 4
H1 = 4
PAD = 2
PAD2 = 4
GRANT = 56200000
MESH = pl.DeviceIdType.MESH
F32 = jnp.float32
SIDES = [(-1, 0), (1, 0), (0, -1), (0, 1), (-1, -1), (-1, 1), (1, -1), (1, 1)]
OPPOSITE = [1, 0, 3, 2, 7, 6, 5, 4]
TILE = (8, 128)


def iota(shape, dim):
    return lax.broadcasted_iota(jnp.int32, shape, dim)


def shift(value, amount, axis):
    return pltpu.roll(value, amount % value.shape[axis], axis)


def take(value, index, axis):
    return jnp.take_along_axis(value, index, axis=axis)


def z_pairs(tile):
    return take(tile + shift(tile, -1, 1), lax.rem(2 * iota(TILE, 1), 128), 1)


def put_halves(ref, v, at, value):
    for h in range(2):
        ref[v, h, at, :] = value[:, 128 * h : 128 * h + 128]


def yz_pairs(ref, v, at):
    halves = []
    for h in range(2):
        halves.append(z_pairs(ref[v, h, pl.ds(at, 8, stride=2), :] + ref[v, h, pl.ds(at + 1, 8, stride=2), :]))
    return jnp.where(iota(TILE, 1) < 64, halves[0], halves[1])


def z_repeat(tile, start=0):
    return take(tile, start + iota(TILE, 1) // 2, 1)


def y_pairs(tile):
    return take(tile + shift(tile, -1, 0), lax.rem(2 * iota(TILE, 0), 8), 0)


def y_repeat(tile, start=0):
    return take(tile, jnp.clip(start + iota(TILE, 0) // 2, 0, 7), 0)


def top_bottom(top, bottom):
    return jnp.where(iota(TILE, 0) < 4, top, bottom)


def rounded(x):
    return x.astype(jnp.bfloat16).astype(F32)


def slabs(lo, count, chunk, body):
    if count == chunk:
        for k in range(chunk):
            body(lo + k)
        return

    def step(i, _):
        for k in range(chunk):
            body(lo + i * chunk + k)
        return 0

    lax.fori_loop(0, count // chunk, step, 0)


def build(m, cx, cy, cz, rd, d, lo, count, tau, seg, chunk, firsts=()):
    shape = m.shape[1:]
    row = iota(shape, 0)
    lane = lax.rem(iota(shape, 1), seg)
    last_row, first_row = row == shape[0] - 1, row == 0
    last_lane, first_lane = lane == seg - 1, lane == 0
    half = 0.5 * tau

    def body(a):
        own = m[a]
        xp, xm = m[a + 1], m[a - 1]
        yp = jnp.where(last_row, 0.0, shift(own, -1, 0))
        ym = jnp.where(first_row, 0.0, shift(own, 1, 0))
        zp = jnp.where(last_lane, 0.0, shift(own, -1, 1))
        zm = jnp.where(first_lane, 0.0, shift(own, 1, 1))
        total = 1.0
        for other, ref in ((xp, cx), (xm, None), (yp, cy), (ym, None), (zp, cz), (zm, None)):
            face = rounded(half * (own + other))
            total = total + face
            if ref is not None:
                ref[a] = jnp.where(jnp.minimum(own, other) > 0.0, face, 0.0)
        inverse = DAMPING / total
        rd[a] = inverse
        if d is not None:
            d[a] = total
        for r, u in firsts:
            u[a] = inverse * r[a]

    slabs(lo, count, chunk, body)


def neighbours(v, a, cx, cy, cz):
    own = v[a]
    cya, cza = cy[a], cz[a]
    total = cx[a] * v[a + 1] + cx[a - 1] * v[a - 1]
    total = total + (cya * shift(own, -1, 0) + shift(cya * own, 1, 0))
    total = total + (cza * shift(own, -1, 1) + shift(cza * own, 1, 1))
    return own, total


def sweep(vin, vout, r, ops, lo, count, chunk):
    cx, cy, cz, rd, d = ops

    def body(a):
        for vi, vo, ri in zip(vin, vout, r):
            own, t = neighbours(vi, a, cx, cy, cz)
            vo[a] = KEEP * own + rd[a] * (ri[a] + t)

    slabs(lo, count, chunk, body)


def residual(vi, ri, a, ops):
    cx, cy, cz, rd, d = ops
    own, t = neighbours(vi, a, cx, cy, cz)
    diag = d[a] if d is not None else DAMPING / rd[a]
    return own, ri[a] + t - diag * own


def fold(x):
    total = None
    for i in range(x.shape[0] // 8):
        for j in range(x.shape[1] // 128):
            part = x[8 * i : 8 * i + 8, 128 * j : 128 * j + 128]
            total = part if total is None else total + part
    return total


def fold_own(x):
    total = None
    for j in range(x.shape[1] // 128):
        lanes = slice(128 * j, 128 * j + 128)
        part = x[8:16, lanes] + top_bottom(x[16:24, lanes], x[0:8, lanes])
        total = part if total is None else total + part
    return total


def kernel(nw, nn, bx, by, nz, m_hbm, s_hbm, c_hbm, out_ref,
           m_ref, s_ref, c_ref,
           m0, cx0, cy0, cz0, rd0, d0, rs0, rc0, us0, uc0, vs0, vc0,
           rx, yp, ry, cp, rcn, xv, hx, yv, hy,
           m1, cx1, cy1, cz1, rd1, d1, r1, u1, v1, w1, h1, hc,
           cx2, cy2, cz2, rd2, r2, u2, v2,
           cx3, cy3, cz3, rd3, r3, u3, v3,
           cx4, cy4, cz4, rd4, r4, u4, v4,
           t0, sm2, sr2, sp2, gm, gr, gp, pb, pbs, f1p, tok,
           ins, ss, gs, gq, e0r, m1r, r1r, v0r, v1r):
    iw, ino = lax.axis_index("wide"), lax.axis_index("narrow")
    b1x, b1y, z1 = bx // 2, by // 2, nz // 2
    b2x, b2y, z2 = bx // 4, by // 4, nz // 4
    x2, x3, x4 = nw * b2x, nw * b2x // 2, nw * b2x // 4
    there = []
    for dx, dy in SIDES:
        ok = None
        for cond, on in ((iw > 0, dx < 0), (iw < nw - 1, dx > 0), (ino > 0, dy < 0), (ino < nn - 1, dy > 0)):
            if on:
                ok = cond if ok is None else jnp.logical_and(ok, cond)
        there.append(ok)

    def peer(side):
        return (iw + SIDES[side][0], ino + SIDES[side][1])

    inputs = [pltpu.make_async_copy(src, dst, ins.at[i])
              for i, (src, dst) in enumerate(((m_hbm, m_ref), (s_hbm, s_ref), (c_hbm, c_ref)))]
    for copy in inputs:
        copy.start()

    def clear(ref, index):
        ref[index] = jnp.zeros(ref[index].shape, F32)

    for k in range(2):
        for ref in (rx, ry, hx, hy):
            for i in range(ref.shape[1]):
                clear(ref, (k, i))
    for k in range(4):
        clear(rcn, k)
    for k in range(2):
        for i in range(h1.shape[1]):
            clear(h1, (k, i))
        for i in range(2):
            clear(hc, (k, i))
    side_rows = (slice(0, b1y), slice(2 * b1y, 3 * b1y))
    for a in (0, 1, 2, 3, H1 + b1x, H1 + b1x + 1, H1 + b1x + 2, H1 + b1x + 3):
        clear(m1, (0, a))
    for a in (H1 - 2, H1 - 1, H1 + b1x, H1 + b1x + 1):
        for v in range(2):
            clear(r1, (v, a))
    for a in range(H1, H1 + b1x):
        for rows in side_rows:
            clear(m1, (0, a, rows))
            for v in range(2):
                clear(r1, (v, a, rows))

    barrier = pltpu.get_barrier_semaphore()

    nb = nn // 2 * nw
    me, odd = ino // 2 * nw + iw, lax.rem(ino, 2)
    twin = ino + 1 - 2 * odd

    def fellow(j):
        to = lax.rem(me + j, nb)
        return lax.rem(to, nw), 2 * (to // nw) + odd

    def greet(j, _):
        pl.semaphore_signal(barrier, inc=1, device_id=fellow(j), device_id_type=MESH)
        return 0

    lax.fori_loop(1, nb, greet, 0)
    for j in range(1, nn, 2):
        pl.semaphore_signal(barrier, inc=1, device_id=(iw, lax.rem(ino + j, nn)), device_id_type=MESH)
    for k in range(4, 8):
        @pl.when(there[k])
        def _():
            pl.semaphore_signal(barrier, inc=1, device_id=peer(k), device_id_type=MESH)

    beside_x = jnp.minimum(iw, 1) + jnp.minimum(nw - 1 - iw, 1)
    beside_y = jnp.minimum(ino, 1) + jnp.minimum(nn - 1 - ino, 1)
    pl.semaphore_wait(barrier, nb - 1 + nn // 2 + beside_x * beside_y)

    def remote(src, dst, ssem, rsem, dev):
        return pltpu.make_async_remote_copy(src_ref=src, dst_ref=dst, send_sem=ssem, recv_sem=rsem,
                                            device_id=dev, device_id_type=MESH)

    def to_side(side, pairs, rsem):
        return [remote(src, dst, ss.at[side], rsem.at[OPPOSITE[side]], peer(side)) for src, dst in pairs]

    def e0_sends(side):
        land = OPPOSITE[side]
        if side < 2:
            pairs = []
            at = 0
            for ref, width in ((m_hbm, 3), (s_hbm, 2), (c_hbm, 2)):
                lo = 0 if side == 0 else bx - width
                pairs.append((ref.at[lo : lo + width], rx.at[land, at : at + width]))
                at += width
            return to_side(side, pairs, e0r)
        if side < 4:
            return to_side(side, [(yp.at[side - 2], ry.at[land - 2])], e0r)
        return to_side(side, [(cp.at[side - 4], rcn.at[land - 4])], e0r)

    def each(fn, sides=range(8)):
        for side in sides:
            @pl.when(there[side])
            def _():
                fn(side)

    def start(copies):
        for copy in copies:
            copy.start()

    each(lambda k: start(e0_sends(k)), (0, 1))
    for copy in inputs:
        copy.wait()
    for side, (m_lo, r_lo) in enumerate(((0, 0), (by - 3, by - 2))):
        for k in range(3):
            yp[side, k] = m_ref[:, m_lo + k, :]
        for k in range(2):
            yp[side, 3 + k] = s_ref[:, r_lo + k, :]
            yp[side, 5 + k] = c_ref[:, r_lo + k, :]
    for k in range(4, 8):
        dx, dy = SIDES[k]
        xa, xb = (0, 1) if dx < 0 else (bx - 1, bx - 2)
        ya, yb = (0, 1) if dy < 0 else (by - 1, by - 2)
        for i, (ref, x, y) in enumerate(((m_ref, xa, ya), (m_ref, xa, yb), (m_ref, xb, ya),
                                         (s_ref, xa, ya), (c_ref, xa, ya))):
            cp[k - 4, i : i + 1, :] = ref[x, y : y + 1, :]

    each(lambda k: start(e0_sends(k)), (2, 3, 4, 5, 6, 7))

    def box1(side, sending, width, corner):
        dx, dy = SIDES[side]
        w = corner if dx and dy else width
        if sending:
            xlo, w = (H1, w) if dx < 0 else ((H1 + b1x - w, w) if dx > 0 else (H1, b1x))
            ylo = b1y
        else:
            xlo, w = (H1 - w, w) if dx < 0 else ((H1 + b1x, w) if dx > 0 else (H1, b1x))
            ylo = b1y * (1 + dy)
        return xlo, w, ylo

    def level1_sends(ref, rsem, side, width, corner):
        sx, w, sy = box1(side, True, width, corner)
        tx, _, ty = box1(OPPOSITE[side], False, width, corner)
        return to_side(side, [(ref.at[:, sx : sx + w, sy : sy + b1y], ref.at[:, tx : tx + w, ty : ty + b1y])], rsem)

    def level1_landed(ref, rsem, width, corner):
        def fn(side):
            tx, w, ty = box1(side, False, width, corner)
            view = ref.at[:, tx : tx + w, ty : ty + b1y]
            pltpu.make_async_copy(view, view, rsem.at[side]).wait()
        return fn

    def e0_landed(side):
        view = rx.at[side] if side < 2 else (ry.at[side - 2] if side < 4 else rcn.at[side - 4])
        pltpu.make_async_copy(view, view, e0r.at[side]).wait()

    own_y = slice(b1y, 2 * b1y)
    for i in range(b1x):
        put_halves(t0, 0, slice(i * by, (i + 1) * by), m_ref[2 * i] + m_ref[2 * i + 1])
    for i in range(b1x):
        m1[0, H1 + i, own_y, :] = 0.125 * yz_pairs(t0, 0, i * by)
    for i in range(0, b2x, 2):
        quads = [y_pairs(m1[0, H1 + 2 * k, own_y, :] + m1[0, H1 + 2 * k + 1, own_y, :]) for k in (i, i + 1)]
        mob2 = 0.125 * z_pairs(top_bottom(quads[0], quads[1]))
        sm2[i * b2y : (i + 2) * b2y, :] = mob2
        gm[odd, me, i * b2y : (i + 2) * b2y, :] = mob2

    def to_fellows(src, dst, kind):
        def step(j, _):
            remote(src, dst, gs.at[kind], gq.at[kind], fellow(j)).start()
            return 0

        lax.fori_loop(1, nb, step, 0)

    def to_twin(src, dst, kind):
        remote(src, dst, gs.at[kind], gq.at[kind], (iw, twin)).start()

    def landed(view, kind):
        pltpu.make_async_copy(view, view, gq.at[kind]).wait()

    for ref, src, width in ((m0, m_ref, 3), (rs0, s_ref, 2), (rc0, c_ref, 2)):
        blank = jnp.zeros(m0.shape[1:], F32)
        for i in range(width):
            ref[H0 - 1 - i] = blank
            ref[H0 + bx + i] = blank

        def put(i, _):
            ref[H0 + i, H0 : H0 + by, :] = src[i]
            return 0

        lax.fori_loop(0, bx, put, 0)
    for ref in (u3, v3, u4, v4):
        zero = jnp.zeros(ref.shape[1:], F32)
        for a in (0, 1, ref.shape[0] - 2, ref.shape[0] - 1):
            ref[a] = zero
    for ref in (u2, v2, r2, cx2, cy2, cz2, rd2):
        zero = jnp.zeros(ref.shape[1:], F32)
        for a in range(PAD2):
            ref[a] = zero
            ref[ref.shape[0] - 1 - a] = zero
    for ref in (cx3, cx4):
        ref[PAD - 1] = jnp.zeros(ref.shape[1:], F32)

    each(e0_landed, (2, 3))
    fields = ((m0, 0, 3), (rs0, 3, 2), (rc0, 5, 2))
    for ref, at, width in fields:
        for i in range(width):
            ref[H0 : H0 + bx, H0 - width + i, :] = ry[0, at + i]
            ref[H0 : H0 + bx, H0 + by + i, :] = ry[1, at + i]

    ops0 = (cx0, cy0, cz0, rd0, d0)
    firsts0 = ((rs0, us0), (rc0, uc0))

    build(m0, cx0, cy0, cz0, rd0, d0, H0 + 1, bx - 2, BASE_TAU, nz, 2, firsts0)
    sweep((us0, uc0), (vs0, vc0), (rs0, rc0), ops0, H0 + 2, bx - 4, 2)

    def down0(i, carry):
        num, den = carry
        sums = []
        for k in range(2):
            a = H0 + 2 * i + k
            vs, es = residual(vs0, rs0, a, ops0)
            vc, ec = residual(vc0, rc0, a, ops0)
            both = es + rs0[a]
            num = num + fold_own(both * vc)
            den = den + fold_own(both * vs)
            sums.append((es, ec))
        at = pl.ds(pl.multiple_of(i * m0.shape[1], 8), m0.shape[1])
        put_halves(t0, 0, at, sums[0][0] + sums[1][0])
        put_halves(t0, 1, at, sums[0][1] + sums[1][1])
        return num, den

    zero8 = jnp.zeros(TILE, F32)
    part0 = lax.fori_loop(2, b1x - 2, down0, (zero8, zero8))

    each(e0_landed, (0, 1, 4, 5, 6, 7))
    each(lambda k: start(level1_sends(m1, m1r, k, 3, 3)))
    for ref, at, width in fields:
        for i in range(width):
            ref[H0 - width + i, H0 : H0 + by, :] = rx[0, at + i]
            ref[H0 + bx + i, H0 : H0 + by, :] = rx[1, at + i]
    for k in range(4):
        dx, dy = SIDES[4 + k]
        xa, xb = (H0 - 1, H0 - 2) if dx < 0 else (H0 + bx, H0 + bx + 1)
        ya, yb = (H0 - 1, H0 - 2) if dy < 0 else (H0 + by, H0 + by + 1)
        for i, (ref, x, y) in enumerate(((m0, xa, ya), (m0, xa, yb), (m0, xb, ya), (rs0, xa, ya), (rc0, xa, ya))):
            ref[x, y : y + 1, :] = rcn[k, i : i + 1, :]
    for lo, v_lo in ((H0 - 2, H0 - 1), (H0 + bx - 1, H0 + bx - 2)):
        build(m0, cx0, cy0, cz0, rd0, d0, lo, 3, BASE_TAU, nz, 3, firsts0)
        sweep((us0, uc0), (vs0, vc0), (rs0, rc0), ops0, v_lo, 3, 3)
    part0 = lax.fori_loop(0, 2, down0, part0)
    num0, den0 = lax.fori_loop(b1x - 2, b1x, down0, part0)
    for v in range(2):
        for i in range(b1x):
            r1[v, H1 + i, own_y, :] = 0.125 * yz_pairs(t0, v, i * m0.shape[1] + H0)
    each(lambda k: start(level1_sends(r1, r1r, k, 2, 1)))
    to_fellows(sm2, gm.at[odd, me], 0)
    for side, (x_far, x_near) in enumerate(((H0 + 1, H0), (H0 + bx - 2, H0 + bx - 1))):
        for v, ref in enumerate((vs0, vc0)):
            xv[side, v, 0:by, :] = ref[x_far, H0 : H0 + by, :]
            xv[side, v, by : by + 1, :] = ref[x_near, H0 - 1 : H0, :]
            xv[side, v, by + 1 : by + 2, :] = ref[x_near, H0 + by : H0 + by + 1, :]
    for side, col in enumerate((H0 + 1, H0 + by - 2)):
        for v, ref in enumerate((vs0, vc0)):
            yv[side, v] = ref[H0 : H0 + bx, col, :]

    def v0_sends(side):
        land = OPPOSITE[side]
        src, dst = (xv.at[side], hx.at[land]) if side < 2 else (yv.at[side - 2], hy.at[land - 2])
        return to_side(side, [(src, dst)], v0r)

    each(level1_landed(m1, m1r, 3, 3))
    ops1 = (cx1, cy1, cz1, rd1, d1)
    build(m1.at[0], cx1, cy1, cz1, rd1, d1, H1 - 3, b1x + 6, BASE_TAU / 4, z1, b1x // 2 + 3)
    each(level1_landed(r1, r1r, 2, 1))
    rr1 = (r1.at[0], r1.at[1])
    uu1 = (u1.at[0], u1.at[1])
    vv1 = (v1.at[0], v1.at[1])

    def first1(a):
        for v in range(2):
            u1[v, a] = rd1[a] * r1[v, a]

    slabs(H1 - 2, b1x + 4, b1x + 4, first1)
    sweep(uu1, vv1, rr1, ops1, H1 - 1, b1x + 2, b1x // 2 + 1)
    num1, den1 = zero8, zero8
    quads = []
    for i in range(b2x):
        pair = []
        for k in range(2):
            a = H1 + 2 * i + k
            vs, es = residual(vv1[0], rr1[0], a, ops1)
            vc, ec = residual(vv1[1], rr1[1], a, ops1)
            both = (es + r1[0, a])[own_y]
            num1 = num1 + both * vc[own_y]
            den1 = den1 + both * vs[own_y]
            pair.append((es[own_y], ec[own_y]))
        quads.append([y_pairs(pair[0][v] + pair[1][v]) for v in range(2)])
        if i % 2:
            packed = [z_pairs(top_bottom(quads[i - 1][v], quads[i][v])) for v in range(2)]
            own2 = 0.125 * jnp.where(iota(TILE, 1) < z2, packed[0], packed[1])
            sr2[(i - 1) * b2y : (i + 1) * b2y, :] = own2
            gr[odd, me, (i - 1) * b2y : (i + 1) * b2y, :] = own2
    to_fellows(sr2, gr.at[odd, me], 2)
    num_row = jnp.sum(num0 + 8.0 * num1, axis=0, keepdims=True)
    den_row = jnp.sum(den0 + 8.0 * den1, axis=0, keepdims=True)
    row8 = iota(TILE, 0)
    part = jnp.where(row8 == 0, num_row, jnp.where(row8 == 1, den_row, 0.0))
    sp2[...] = part
    gp[me] = part
    to_fellows(sp2, gp.at[me], 4)

    landed(gm.at[0, 0 : nb - 1], 0)
    to_twin(gm.at[odd], gm.at[odd], 1)
    landed(gm.at[0], 1)

    def unpack(src, dst):
        def step(w, _):
            for n in range(nn):
                for i in range(b2x):
                    dst[PAD2 + w * b2x + i, n * b2y : (n + 1) * b2y, :] = src[n % 2, n // 2 * nw + w, i * b2y : (i + 1) * b2y, :]
            return 0

        lax.fori_loop(0, nw, step, 0)

    unpack(gm, v2)
    build(v2, cx2, cy2, cz2, rd2, None, PAD2, x2, BASE_TAU / 16, z2, 8)

    def coarsen(x):
        if x.shape[0] == 16:
            return 0.125 * z_pairs(top_bottom(y_pairs(x[0:8]), y_pairs(x[8:16])))
        return 0.125 * z_pairs(top_bottom(y_pairs(x), 0.0))

    def coarsen_pairs(get, xc, pad, dst):
        def step(g, _):
            for k in range(4):
                a = pad + 2 * (4 * g + k)
                dst[PAD + 4 * g + k] = coarsen(get(a) + get(a + 1))
            return 0

        lax.fori_loop(0, xc // 4, step, 0)

    coarsen_pairs(lambda a: v2[a], x3, PAD2, v3)
    build(v3, cx3, cy3, cz3, rd3, None, PAD, x3, BASE_TAU / 64, z2 // 2, 4)
    coarsen_pairs(lambda a: v3[a], x4, PAD, v4)
    build(v4, cx4, cy4, cz4, rd4, None, PAD, x4, BASE_TAU / 256, z2 // 4, 4)

    landed(gr.at[0, 0 : nb - 1], 2)
    to_twin(gr.at[odd], gr.at[odd], 3)

    def v1_sends(side):
        land = OPPOSITE[side]
        pairs = []
        for v in range(2):
            lo = H1 if side == 0 else H1 + b1x - 3
            pairs.append((v1.at[v, lo : lo + 3], h1.at[land, 3 * v : 3 * v + 3]))
        far = H1 + 1 if side == 0 else H1 + b1x - 2
        for i, rows in enumerate(side_rows):
            pairs.append((r1.at[:, far, rows], hc.at[land, i]))
        return to_side(side, pairs, v1r)

    each(lambda k: start(v1_sends(k)), range(2))
    each(lambda k: start(v0_sends(k)), range(4))

    def v0_landed(side):
        view = hx.at[side] if side < 2 else hy.at[side - 2]
        pltpu.make_async_copy(view, view, v0r.at[side]).wait()

    landed(gr.at[0], 3)
    unpack(gr, r2)

    ops2 = (cx2, cy2, cz2, rd2, None)
    ops3 = (cx3, cy3, cz3, rd3, None)
    ops4 = (cx4, cy4, cz4, rd4, None)

    def down(u, v, r, ops, pad, xc):
        def first(a):
            u[a] = ops[3][a] * r[a]

        slabs(pad, xc, 8, first)
        sweep((u,), (v,), (r,), ops, pad, xc, min(xc, 16) if u.shape[1] == 8 else 8)

    down(u2, v2, r2, ops2, PAD2, x2)
    low2 = iota(v2.shape[1:], 1) < z2

    def coarsen2(g, carry):
        num, den = carry
        for k in range(4):
            pair = []
            for j in range(2):
                a = PAD2 + 2 * (4 * g + k) + j
                v, e = residual(v2, r2, a, ops2)
                both = jnp.where(low2, e + r2[a], 0.0)
                num = num + fold(both * shift(v, z2, 1))
                den = den + fold(both * v)
                pair.append(e)
            r3[PAD + 4 * g + k] = coarsen(pair[0] + pair[1])
        return num, den

    num2, den2 = lax.fori_loop(0, x3 // 4, coarsen2, (zero8, zero8))
    landed(gp.at[0 : nb - 1], 4)
    total = gp[0]
    if nb <= 32:
        for w in range(1, nb):
            total = total + gp[w]
    else:
        total = lax.fori_loop(1, nb, lambda w, acc: acc + gp[w], total)
    pb[...] = total
    to_twin(pb, pbs, 5)
    down(u3, v3, r3, ops3, PAD, x3)
    coarsen_pairs(lambda a: residual(v3, r3, a, ops3)[1], x4, PAD, r4)
    down(u4, v4, r4, ops4, PAD, x4)

    def up3(g, _):
        for k in range(4):
            add = y_repeat(z_repeat(v4[PAD + 4 * g + k]))
            a = PAD + 2 * (4 * g + k)
            v3[a] = v3[a] + add
            v3[a + 1] = v3[a + 1] + add
        return 0

    lax.fori_loop(0, x4 // 4, up3, 0)
    sweep((v3,), (u3,), (r3,), ops3, PAD, x3, 16)
    sweep((u3,), (v3,), (r3,), ops3, PAD, x3, 16)
    low3 = iota(TILE, 1) < z2 // 2

    def dots(i, carry):
        num, den = carry
        for k in range(4):
            a = PAD + 4 * i + k
            both = jnp.where(low3, v3[a], 0.0)
            den = den + both * r3[a]
            num = num + both * shift(r3[a], -(z2 // 2), 1)
        return num, den

    num3, den3 = lax.fori_loop(0, x3 // 4, dots, (zero8, zero8))
    base = PAD2 + iw * b2x
    for i in range(b2x // 2 + 4):
        wide_tile = z_repeat(v3[PAD + iw * (b2x // 2) - 2 + i])
        for j in range(2):
            a = base - 4 + 2 * i + j
            v2[a, 0:8, :] = v2[a, 0:8, :] + y_repeat(wide_tile)
            v2[a, 8:16, :] = v2[a, 8:16, :] + y_repeat(wide_tile, 4)
    sweep((v2,), (u2,), (r2,), ops2, base - 3, b2x + 6, b2x + 6)
    sweep((u2,), (v2,), (r2,), ops2, base - 2, b2x + 4, b2x + 4)

    landed(pbs, 5)
    whole = total + pbs[...]
    num = jnp.sum(jnp.where(row8 == 0, whole, 0.0) + 64.0 * num2 + 512.0 * num3)
    den = jnp.sum(jnp.where(row8 == 1, whole, 0.0) + 64.0 * den2 + 512.0 * den3)
    ratio = (jnp.full(TILE, num) / (1.0 + jnp.full(TILE, den)))[0:1, :]

    def v1_landed(side):
        view = tok.at[0 : 6 * 3 * b1y // 8 + 4 * b1y // 8]
        pltpu.make_async_copy(view, view, v1r.at[side]).wait()

    each(v1_landed, range(2))
    for side, a in enumerate((H1 - 2, H1 + b1x + 1)):
        for i, rows in enumerate(side_rows):
            r1[:, a, rows] = hc[side, i]
    rows2 = v2.shape[1]
    full_y = 2 * rows2
    for i in range(b2x + 4):
        f1p[i, 0:b1y, :] = jnp.zeros((b1y, z1), F32)
        f1p[i, b1y + full_y : 2 * b1y + full_y, :] = jnp.zeros((b1y, z1), F32)
        for j in range(rows2 // 8):
            e = v2[base - 2 + i, 8 * j : 8 * j + 8, :]
            part = z_repeat(shift(e, z2, 1) - ratio * e)
            f1p[i, pl.ds(b1y + 16 * j, 8, stride=2), :] = part
            f1p[i, pl.ds(b1y + 16 * j + 1, 8, stride=2), :] = part
    window = pl.ds(pl.multiple_of(ino * b1y, 8), 3 * b1y)
    for x in range(-3, b1x + 3):
        a = H1 + x
        side, at = (0, x + 3) if x < 0 else (1, x - b1x)
        far = x < 0 or x >= b1x
        vs, vc = (h1[side, at], h1[side, 3 + at]) if far else (v1[0, a], v1[1, a])
        u1[0, a] = vc - ratio * vs + f1p[x // 2 + 2, window, :]
        if -2 <= x < b1x + 2:
            w1[a] = r1[1, a] - ratio * r1[0, a]
    sweep((u1.at[0],), (u1.at[1],), (w1,), ops1, H1 - 2, b1x + 4, b1x // 2 + 2)
    sweep((u1.at[1],), (u1.at[0],), (w1,), ops1, H1 - 1, b1x + 2, b1x // 2 + 1)

    each(v0_landed, range(4))
    for side, (x_far, x_near) in enumerate(((H0 - 2, H0 - 1), (H0 + bx + 1, H0 + bx))):
        for v, ref in enumerate((vs0, vc0)):
            ref[x_far, H0 : H0 + by, :] = hx[side, v, 0:by, :]
            ref[x_near, H0 - 1 : H0, :] = hx[side, v, by : by + 1, :]
            ref[x_near, H0 + by : H0 + by + 1, :] = hx[side, v, by + 1 : by + 2, :]
    for side, col in enumerate((H0 - 2, H0 + by + 1)):
        for v, ref in enumerate((vs0, vc0)):
            ref[H0 : H0 + bx, col, :] = hy[side, v]
    ratio0 = jnp.concatenate([ratio] * (nz // 128), axis=1)

    def up0(i):
        tiles = [u1[0, H1 - 1 + i, 8 * j : 8 * j + 8, :] for j in range(3)]
        rows = [top_bottom(y_repeat(tiles[0], 6), y_repeat(tiles[1], -2)),
                y_repeat(tiles[1], 2),
                top_bottom(y_repeat(tiles[1], 6), y_repeat(tiles[2], -2))]
        add = jnp.concatenate([jnp.concatenate([z_repeat(t), z_repeat(t, 64)], axis=1) for t in rows], axis=0)
        for k in range(2):
            a = H0 - 2 + 2 * i + k
            us0[a] = vc0[a] - ratio0 * vs0[a] + add
            rc0[a] = rc0[a] - ratio0 * rs0[a]

    slabs(0, b1x + 2, 2, up0)
    sweep((us0,), (uc0,), (rc0,), ops0, H0 - 1, bx + 2, 3)

    def last(a):
        own, t = neighbours(uc0, a, cx0, cy0, cz0)
        out_ref[a - H0] = (KEEP * own + rd0[a] * (rc0[a] + t))[H0 : H0 + by]

    slabs(H0, bx, 4, last)

    def sent(side):
        dx, dy = SIDES[side]
        if dy == 0:
            tiles = 7 * by * nz // 1024 + 3 + 4 + 2 * (by + 8) * nz // 1024 + 18 + 4
        elif dx == 0:
            tiles = 7 * bx * nz // 1024 + b1x + 2 * b1x + 2 * bx * nz // 1024
        else:
            tiles = 2 + 3 + 2
        view = tok.at[0:tiles]
        pltpu.make_async_copy(view, view, ss.at[side]).wait()

    each(sent)
    for kind, view in enumerate((gm.at[0, 0 : nb - 1], gm.at[0], gr.at[0, 0 : nb - 1], gr.at[0],
                                 gp.at[0 : nb - 1], pbs)):
        pltpu.make_async_copy(view, view, gs.at[kind]).wait()


def solution(mesh):
    nw, nn = mesh.shape["wide"], mesh.shape["narrow"]

    def per_device(mobility, sav_vector, cotangent):
        bx, by, nz = mobility.shape
        b1x, b1y, z1 = bx // 2, by // 2, nz // 2
        x2, y2 = nw * bx // 4, nn * by // 4
        own = (bx, by, nz)
        l0 = (bx + 2 * H0, by + 2 * H0, nz)
        l1 = (b1x + 2 * H1, 3 * b1y, z1)
        l2 = (x2 + 2 * PAD2, y2, z1)
        l3 = (x2 // 2 + 2 * PAD, y2 // 2, z1)
        l4 = (x2 // 4 + 2 * PAD, 8, z1)
        own2 = (bx // 4 * (by // 4), z1)
        buffers = (
            [own] * 3 + [l0] * 12
            + [(2, 7, by, nz), (2, 7, bx, nz), (2, 7, bx, nz), (4, 8, nz), (4, 8, nz)]
            + [(2, 2, by + 8, nz)] * 2 + [(2, 2, bx, nz)] * 2
            + [(1, *l1)] + [l1] * 5 + [(2, *l1)] * 3 + [l1] + [(2, 6, 3 * b1y, z1), (2, 2, 2, b1y, z1)]
            + [l2] * 7 + [l3] * 7 + [l4] * 7
            + [(2, 2, b1x * l0[1], nz // 2)]
            + [own2, own2, TILE, (2, nn // 2 * nw, *own2), (2, nn // 2 * nw, *own2), (nn // 2 * nw, *TILE), TILE, TILE]
            + [(bx // 4 + 4, 2 * y2 + 2 * b1y, z1), (128, *TILE)]
        )
        size = sum(4 * functools.reduce(lambda p, q: p * q, shape) for shape in buffers)
        dma = lambda n: pltpu.SemaphoreType.DMA((n,))
        scratch = [pltpu.VMEM(shape, F32) for shape in buffers]
        scratch += [dma(n) for n in (3, 8, 6, 6, 8, 8, 8, 4, 2)]
        return pl.pallas_call(
            functools.partial(kernel, nw, nn, bx, by, nz),
            out_shape=jax.ShapeDtypeStruct((bx, by, nz), F32),
            in_specs=[pl.BlockSpec(memory_space=pltpu.HBM)] * 3,
            out_specs=pl.BlockSpec(memory_space=pltpu.VMEM),
            scratch_shapes=scratch,
            compiler_params=pltpu.CompilerParams(
                collective_id=0, has_side_effects=True, vmem_limit_bytes=GRANT if size < GRANT else 67043328
            ),
        )(mobility, sav_vector, cotangent)

    spec = P("wide", "narrow", None)
    return jax.shard_map(per_device, mesh=mesh, in_specs=(spec,) * 3, out_specs=spec, check_vma=False)
```

```python
import functools
import jax
import jax.numpy as jnp
from jax import lax
from jax.experimental import pallas as pl
from jax.experimental.pallas import tpu as pltpu
from jax.sharding import PartitionSpec as P

DAMPING = 0.8
KEEP = 1.0 - DAMPING
BASE_TAU = 16.0
H0 = 4
H1 = 4
PAD = 2
PAD2 = 4
GRANT = 56200000
MESH = pl.DeviceIdType.MESH
F32 = jnp.float32
SIDES = [(-1, 0), (1, 0), (0, -1), (0, 1), (-1, -1), (-1, 1), (1, -1), (1, 1)]
OPPOSITE = [1, 0, 3, 2, 7, 6, 5, 4]
TILE = (8, 128)


def iota(shape, dim):
    return lax.broadcasted_iota(jnp.int32, shape, dim)


def shift(value, amount, axis):
    return pltpu.roll(value, amount % value.shape[axis], axis)


def take(value, index, axis):
    return jnp.take_along_axis(value, index, axis=axis)


def z_pairs(tile):
    return take(tile + shift(tile, -1, 1), lax.rem(2 * iota(TILE, 1), 128), 1)


def put_halves(ref, v, at, value):
    for h in range(2):
        ref[v, h, at, :] = value[:, 128 * h : 128 * h + 128]


def yz_pairs(ref, v, at):
    halves = []
    for h in range(2):
        halves.append(z_pairs(ref[v, h, pl.ds(at, 8, stride=2), :] + ref[v, h, pl.ds(at + 1, 8, stride=2), :]))
    return jnp.where(iota(TILE, 1) < 64, halves[0], halves[1])


def z_repeat(tile, start=0):
    return take(tile, start + iota(TILE, 1) // 2, 1)


def y_pairs(tile):
    return take(tile + shift(tile, -1, 0), lax.rem(2 * iota(TILE, 0), 8), 0)


def y_repeat(tile, start=0):
    return take(tile, jnp.clip(start + iota(TILE, 0) // 2, 0, 7), 0)


def top_bottom(top, bottom):
    return jnp.where(iota(TILE, 0) < 4, top, bottom)


def rounded(x):
    return x.astype(jnp.bfloat16).astype(F32)


def slabs(lo, count, chunk, body):
    if count == chunk:
        for k in range(chunk):
            body(lo + k)
        return

    def step(i, _):
        for k in range(chunk):
            body(lo + i * chunk + k)
        return 0

    lax.fori_loop(0, count // chunk, step, 0)


def build(m, cx, cy, cz, rd, d, lo, count, tau, seg, chunk, firsts=()):
    shape = m.shape[1:]
    row = iota(shape, 0)
    lane = lax.rem(iota(shape, 1), seg)
    last_row, first_row = row == shape[0] - 1, row == 0
    last_lane, first_lane = lane == seg - 1, lane == 0
    half = 0.5 * tau

    def body(a):
        own = m[a]
        xp, xm = m[a + 1], m[a - 1]
        yp = jnp.where(last_row, 0.0, shift(own, -1, 0))
        ym = jnp.where(first_row, 0.0, shift(own, 1, 0))
        zp = jnp.where(last_lane, 0.0, shift(own, -1, 1))
        zm = jnp.where(first_lane, 0.0, shift(own, 1, 1))
        total = 1.0
        for other, ref in ((xp, cx), (xm, None), (yp, cy), (ym, None), (zp, cz), (zm, None)):
            face = rounded(half * (own + other))
            total = total + face
            if ref is not None:
                ref[a] = jnp.where(jnp.minimum(own, other) > 0.0, face, 0.0)
        inverse = DAMPING / total
        rd[a] = inverse
        if d is not None:
            d[a] = total
        for r, u in firsts:
            u[a] = inverse * r[a]

    slabs(lo, count, chunk, body)


def neighbours(v, a, cx, cy, cz):
    own = v[a]
    cya, cza = cy[a], cz[a]
    total = cx[a] * v[a + 1] + cx[a - 1] * v[a - 1]
    total = total + (cya * shift(own, -1, 0) + shift(cya * own, 1, 0))
    total = total + (cza * shift(own, -1, 1) + shift(cza * own, 1, 1))
    return own, total


def sweep(vin, vout, r, ops, lo, count, chunk):
    cx, cy, cz, rd, d = ops

    def body(a):
        for vi, vo, ri in zip(vin, vout, r):
            own, t = neighbours(vi, a, cx, cy, cz)
            vo[a] = KEEP * own + rd[a] * (ri[a] + t)

    slabs(lo, count, chunk, body)


def residual(vi, ri, a, ops):
    cx, cy, cz, rd, d = ops
    own, t = neighbours(vi, a, cx, cy, cz)
    diag = d[a] if d is not None else DAMPING / rd[a]
    return own, ri[a] + t - diag * own


def fold(x):
    total = None
    for i in range(x.shape[0] // 8):
        for j in range(x.shape[1] // 128):
            part = x[8 * i : 8 * i + 8, 128 * j : 128 * j + 128]
            total = part if total is None else total + part
    return total


def fold_own(x):
    total = None
    for j in range(x.shape[1] // 128):
        lanes = slice(128 * j, 128 * j + 128)
        part = x[8:16, lanes] + top_bottom(x[16:24, lanes], x[0:8, lanes])
        total = part if total is None else total + part
    return total


def kernel(nw, nn, bx, by, nz, m_hbm, s_hbm, c_hbm, out_ref,
           m_ref, s_ref, c_ref,
           m0, cx0, cy0, cz0, rd0, d0, rs0, rc0, us0, uc0, vs0, vc0,
           rx, yp, ry, cp, rcn, xv, hx, yv, hy, xu, hu,
           m1, cx1, cy1, cz1, rd1, d1, r1, u1, v1, w1, h1, hc, cv1, cs1, cr1,
           cx2, cy2, cz2, rd2, r2, u2, v2,
           cx3, cy3, cz3, rd3, r3, u3, v3,
           cx4, cy4, cz4, rd4, r4, u4, v4,
           t0, sm2, sr2, sp2, gm, gr, gp, pb, pbs, f1p, tok,
           ins, ss, gs, gq, e0r, m1r, r1r, v0r, v1r, u0r):
    iw, ino = lax.axis_index("wide"), lax.axis_index("narrow")
    b1x, b1y, z1 = bx // 2, by // 2, nz // 2
    b2x, b2y, z2 = bx // 4, by // 4, nz // 4
    x2, x3, x4 = nw * b2x, nw * b2x // 2, nw * b2x // 4
    there = []
    for dx, dy in SIDES:
        ok = None
        for cond, on in ((iw > 0, dx < 0), (iw < nw - 1, dx > 0), (ino > 0, dy < 0), (ino < nn - 1, dy > 0)):
            if on:
                ok = cond if ok is None else jnp.logical_and(ok, cond)
        there.append(ok)

    def peer(side):
        return (iw + SIDES[side][0], ino + SIDES[side][1])

    inputs = [pltpu.make_async_copy(src, dst, ins.at[i])
              for i, (src, dst) in enumerate(((m_hbm, m_ref), (s_hbm, s_ref), (c_hbm, c_ref)))]
    for copy in inputs:
        copy.start()

    def clear(ref, index):
        ref[index] = jnp.zeros(ref[index].shape, F32)

    for k in range(2):
        for ref in (rx, ry, hx, hy, hu):
            for i in range(ref.shape[1]):
                clear(ref, (k, i))
    for k in range(4):
        clear(rcn, k)
    for k in range(2):
        clear(h1, k)
        clear(hc, k)
        clear(cr1, k)
    side_rows = (slice(0, b1y), slice(2 * b1y, 3 * b1y))
    for a in (0, 1, 2, 3, H1 + b1x, H1 + b1x + 1, H1 + b1x + 2, H1 + b1x + 3):
        clear(m1, (0, a))
    for a in (H1 - 2, H1 - 1, H1 + b1x, H1 + b1x + 1):
        for v in range(2):
            clear(r1, (v, a))
    for a in range(H1, H1 + b1x):
        for rows in side_rows:
            clear(m1, (0, a, rows))
            for v in range(2):
                clear(r1, (v, a, rows))

    barrier = pltpu.get_barrier_semaphore()

    nb = nn // 2 * nw
    me, odd = ino // 2 * nw + iw, lax.rem(ino, 2)
    twin = ino + 1 - 2 * odd

    def fellow(j):
        to = me + j
        to = jnp.where(to >= nb, to - nb, to)
        row = to // nw
        return to - row * nw, 2 * row + odd

    def over_fellows(fn):
        if nb <= 16:
            for j in range(1, nb):
                fn(j)
        else:
            def step(j, _):
                fn(j)
                return 0

            lax.fori_loop(1, nb, step, 0)

    over_fellows(lambda j: pl.semaphore_signal(barrier, inc=1, device_id=fellow(j), device_id_type=MESH))
    for j in range(1, nn, 2):
        pl.semaphore_signal(barrier, inc=1, device_id=(iw, lax.rem(ino + j, nn)), device_id_type=MESH)
    for k in range(4, 8):
        @pl.when(there[k])
        def _():
            pl.semaphore_signal(barrier, inc=1, device_id=peer(k), device_id_type=MESH)

    beside_x = jnp.minimum(iw, 1) + jnp.minimum(nw - 1 - iw, 1)
    beside_y = jnp.minimum(ino, 1) + jnp.minimum(nn - 1 - ino, 1)
    pl.semaphore_wait(barrier, nb - 1 + nn // 2 + beside_x * beside_y)

    def remote(src, dst, ssem, rsem, dev):
        return pltpu.make_async_remote_copy(src_ref=src, dst_ref=dst, send_sem=ssem, recv_sem=rsem,
                                            device_id=dev, device_id_type=MESH)

    def to_side(side, pairs, rsem):
        return [remote(src, dst, ss.at[side], rsem.at[OPPOSITE[side]], peer(side)) for src, dst in pairs]

    def e0_sends(side):
        land = OPPOSITE[side]
        if side < 2:
            pairs = []
            at = 0
            for ref, width in ((m_hbm, 2), (s_hbm, 1), (c_hbm, 1)):
                lo = 0 if side == 0 else bx - width
                pairs.append((ref.at[lo : lo + width], rx.at[land, at : at + width]))
                at += width
            return to_side(side, pairs, e0r)
        if side < 4:
            return to_side(side, [(yp.at[side - 2], ry.at[land - 2])], e0r)
        return to_side(side, [(cp.at[side - 4], rcn.at[land - 4])], e0r)

    def each(fn, sides=range(8)):
        for side in sides:
            @pl.when(there[side])
            def _():
                fn(side)

    def start(copies):
        for copy in copies:
            copy.start()

    each(lambda k: start(e0_sends(k)), (0, 1))
    for copy in inputs:
        copy.wait()
    for side, (m_lo, r_lo) in enumerate(((0, 0), (by - 3, by - 2))):
        for k in range(3):
            yp[side, k] = m_ref[:, m_lo + k, :]
        for k in range(2):
            yp[side, 3 + k] = s_ref[:, r_lo + k, :]
            yp[side, 5 + k] = c_ref[:, r_lo + k, :]
    for k in range(4, 8):
        dx, dy = SIDES[k]
        xa, xb = (0, 1) if dx < 0 else (bx - 1, bx - 2)
        ya, yb = (0, 1) if dy < 0 else (by - 1, by - 2)
        for i, (ref, x, y) in enumerate(((m_ref, xa, ya), (m_ref, xa, yb), (m_ref, xb, ya),
                                         (s_ref, xa, ya), (c_ref, xa, ya))):
            cp[k - 4, i : i + 1, :] = ref[x, y : y + 1, :]

    each(lambda k: start(e0_sends(k)), (2, 3, 4, 5, 6, 7))

    near1 = ((1, 1), (1, 2), (1, 3), (2, 1), (2, 2), (3, 1))
    near_m1 = near1 + ((2, 3), (1, 4))

    def inside1(side, i, j):
        dx, dy = SIDES[side]
        return H1 + i - 1 if dx < 0 else H1 + b1x - i, b1y + j - 1 if dy < 0 else 2 * b1y - j

    def outside1(side, i, j):
        dx, dy = SIDES[side]
        return H1 - i if dx < 0 else H1 + b1x + i - 1, b1y - j if dy < 0 else 2 * b1y + j - 1

    def box1(side, sending, width):
        dx, dy = SIDES[side]
        w = width
        if sending:
            xlo, w = (H1, w) if dx < 0 else ((H1 + b1x - w, w) if dx > 0 else (H1, b1x))
            ylo = b1y
        else:
            xlo, w = (H1 - w, w) if dx < 0 else ((H1 + b1x, w) if dx > 0 else (H1, b1x))
            ylo = b1y * (1 + dy)
        return xlo, w, ylo

    def level1_sends(ref, rsem, side, width, kc):
        if side > 3:
            return to_side(side, [(cs1.at[kc, side - 4], cr1.at[kc, OPPOSITE[side] - 4])], rsem)
        sx, w, sy = box1(side, True, width)
        tx, _, ty = box1(OPPOSITE[side], False, width)
        return to_side(side, [(ref.at[:, sx : sx + w, sy : sy + b1y], ref.at[:, tx : tx + w, ty : ty + b1y])], rsem)

    def level1_landed(ref, rsem, width, kc):
        def fn(side):
            if side > 3:
                view = cr1.at[kc, side - 4]
            else:
                tx, w, ty = box1(side, False, width)
                view = ref.at[:, tx : tx + w, ty : ty + b1y]
            pltpu.make_async_copy(view, view, rsem.at[side]).wait()
        return fn

    def e0_landed(side):
        view = rx.at[side] if side < 2 else (ry.at[side - 2] if side < 4 else rcn.at[side - 4])
        pltpu.make_async_copy(view, view, e0r.at[side]).wait()

    own_y = slice(b1y, 2 * b1y)
    for i in range(b1x):
        put_halves(t0, 0, slice(i * by, (i + 1) * by), m_ref[2 * i] + m_ref[2 * i + 1])
    for i in range(b1x):
        m1[0, H1 + i, own_y, :] = 0.125 * yz_pairs(t0, 0, i * by)
    for k in range(4, 8):
        for n, (i, j) in enumerate(near_m1):
            x, y = inside1(k, i, j)
            cs1[0, k - 4, n : n + 1, :] = m1[0, x, y : y + 1, :]
    for i in range(0, b2x, 2):
        quads = [y_pairs(m1[0, H1 + 2 * k, own_y, :] + m1[0, H1 + 2 * k + 1, own_y, :]) for k in (i, i + 1)]
        mob2 = 0.125 * z_pairs(top_bottom(quads[0], quads[1]))
        sm2[i * b2y : (i + 2) * b2y, :] = mob2
        gm[odd, me, i * b2y : (i + 2) * b2y, :] = mob2

    def to_fellows(src, dst, kind):
        over_fellows(lambda j: remote(src, dst, gs.at[kind], gq.at[kind], fellow(j)).start())

    def to_twin(src, dst, kind):
        remote(src, dst, gs.at[kind], gq.at[kind], (iw, twin)).start()

    def landed(view, kind):
        pltpu.make_async_copy(view, view, gq.at[kind]).wait()

    for ref, src, width in ((m0, m_ref, 2), (rs0, s_ref, 1), (rc0, c_ref, 1)):
        blank = jnp.zeros(m0.shape[1:], F32)
        for i in range(width):
            ref[H0 - 1 - i] = blank
            ref[H0 + bx + i] = blank

        def put(i):
            ref[H0 + i, H0 : H0 + by, :] = src[i]

        slabs(0, bx, 4, put)
    for ref in (us0, uc0):
        ref[H0 - 2] = jnp.zeros(m0.shape[1:], F32)
        ref[H0 + bx + 1] = jnp.zeros(m0.shape[1:], F32)
    for a in (0, 1, 2, 3, H1 + b1x, H1 + b1x + 1, H1 + b1x + 2, H1 + b1x + 3):
        for v in range(2):
            v1[v, a] = jnp.zeros(v1.shape[2:], F32)
    for ref in (u3, v3, u4, v4):
        zero = jnp.zeros(ref.shape[1:], F32)
        for a in (0, 1, ref.shape[0] - 2, ref.shape[0] - 1):
            ref[a] = zero
    for ref in (u2, v2, r2, cx2, cy2, cz2, rd2):
        zero = jnp.zeros(ref.shape[1:], F32)
        for a in range(PAD2):
            ref[a] = zero
            ref[ref.shape[0] - 1 - a] = zero
    for ref in (cx3, cx4):
        ref[PAD - 1] = jnp.zeros(ref.shape[1:], F32)

    each(e0_landed, (2, 3))
    fields = ((m0, 0, 3), (rs0, 3, 2), (rc0, 5, 2))
    for ref, at, width in fields:
        for i in range(width):
            ref[H0 : H0 + bx, H0 - width + i, :] = ry[0, at + i]
            ref[H0 : H0 + bx, H0 + by + i, :] = ry[1, at + i]

    ops0 = (cx0, cy0, cz0, rd0, d0)
    firsts0 = ((rs0, us0), (rc0, uc0))

    for side, a in enumerate((H0 + 1, H0 + bx - 2)):
        build(m0, cx0, cy0, cz0, rd0, d0, a, 1, BASE_TAU, nz, 1, firsts0)
        for v, ref in enumerate((us0, uc0)):
            xu[side, v] = ref[a, H0 : H0 + by, :]
    each(lambda k: start(to_side(k, [(xu.at[k], hu.at[OPPOSITE[k]])], u0r)), (0, 1))
    each(lambda k: start(level1_sends(m1, m1r, k, 3, 0)))
    build(m0, cx0, cy0, cz0, rd0, d0, H0 + 2, bx - 4, BASE_TAU, nz, 2, firsts0)
    sweep((us0, uc0), (vs0, vc0), (rs0, rc0), ops0, H0 + 2, bx - 4, 2)

    def down0(i, carry):
        num, den = carry
        sums = []
        for k in range(2):
            a = H0 + 2 * i + k
            vs, es = residual(vs0, rs0, a, ops0)
            vc, ec = residual(vc0, rc0, a, ops0)
            both = es + rs0[a]
            num = num + fold_own(both * vc)
            den = den + fold_own(both * vs)
            sums.append((es, ec))
        at = pl.ds(pl.multiple_of(i * m0.shape[1], 8), m0.shape[1])
        put_halves(t0, 0, at, sums[0][0] + sums[1][0])
        put_halves(t0, 1, at, sums[0][1] + sums[1][1])
        return num, den

    zero8 = jnp.zeros(TILE, F32)
    part0 = lax.fori_loop(2, b1x - 2, down0, (zero8, zero8))

    def u0_landed(side):
        pltpu.make_async_copy(hu.at[side], hu.at[side], u0r.at[side]).wait()

    each(e0_landed, (0, 1, 4, 5, 6, 7))
    each(u0_landed, (0, 1))
    for ref, at, width in ((m0, 0, 2), (rs0, 2, 1), (rc0, 3, 1)):
        for i in range(width):
            ref[H0 - width + i, H0 : H0 + by, :] = rx[0, at + i]
            ref[H0 + bx + i, H0 : H0 + by, :] = rx[1, at + i]
    for v, ref in enumerate((us0, uc0)):
        ref[H0 - 2, H0 : H0 + by, :] = hu[0, v]
        ref[H0 + bx + 1, H0 : H0 + by, :] = hu[1, v]
    for k in range(4):
        dx, dy = SIDES[4 + k]
        xa, xb = (H0 - 1, H0 - 2) if dx < 0 else (H0 + bx, H0 + bx + 1)
        ya, yb = (H0 - 1, H0 - 2) if dy < 0 else (H0 + by, H0 + by + 1)
        for i, (ref, x, y) in enumerate(((m0, xa, ya), (m0, xa, yb), (m0, xb, ya), (rs0, xa, ya), (rc0, xa, ya))):
            ref[x, y : y + 1, :] = rcn[k, i : i + 1, :]
    beyond = m0[H0 - 2]
    own = m0[H0 - 1]
    cx0[H0 - 2] = jnp.where(jnp.minimum(own, beyond) > 0.0, rounded(0.5 * BASE_TAU * (own + beyond)), 0.0)
    for lo, v_lo in ((H0 - 1, H0 - 1), (H0 + bx - 1, H0 + bx - 2)):
        build(m0, cx0, cy0, cz0, rd0, d0, lo, 2, BASE_TAU, nz, 2, firsts0)
        sweep((us0, uc0), (vs0, vc0), (rs0, rc0), ops0, v_lo, 3, 3)
    part0 = lax.fori_loop(0, 2, down0, part0)
    num0, den0 = lax.fori_loop(b1x - 2, b1x, down0, part0)
    for v in range(2):
        for i in range(b1x):
            r1[v, H1 + i, own_y, :] = 0.125 * yz_pairs(t0, v, i * m0.shape[1] + H0)
    for k in range(4, 8):
        for n in range(6):
            x, y = inside1(k, 1, 1 + n // 2)
            cs1[1, k - 4, n : n + 1, :] = r1[n % 2, x, y : y + 1, :]
    each(lambda k: start(level1_sends(r1, r1r, k, 2, 1)))
    to_fellows(sm2, gm.at[odd, me], 0)
    for side, (x_far, x_near) in enumerate(((H0 + 1, H0), (H0 + bx - 2, H0 + bx - 1))):
        for v, ref in enumerate((vs0, vc0)):
            xv[side, v, 0:by, :] = ref[x_far, H0 : H0 + by, :]
            xv[side, v, by : by + 1, :] = ref[x_near, H0 - 1 : H0, :]
            xv[side, v, by + 1 : by + 2, :] = ref[x_near, H0 + by : H0 + by + 1, :]
    for side, col in enumerate((H0 + 1, H0 + by - 2)):
        for v, ref in enumerate((vs0, vc0)):
            yv[side, v] = ref[H0 : H0 + bx, col, :]

    def v0_sends(side):
        land = OPPOSITE[side]
        src, dst = (xv.at[side], hx.at[land]) if side < 2 else (yv.at[side - 2], hy.at[land - 2])
        return to_side(side, [(src, dst)], v0r)

    each(level1_landed(m1, m1r, 3, 0))
    for k in range(4, 8):
        for n, (i, j) in enumerate(near_m1):
            x, y = outside1(k, i, j)
            m1[0, x, y : y + 1, :] = cr1[0, k - 4, n : n + 1, :]
    ops1 = (cx1, cy1, cz1, rd1, d1)
    build(m1.at[0], cx1, cy1, cz1, rd1, d1, H1 - 3, b1x + 6, BASE_TAU / 4, z1, b1x // 2 + 3)
    each(level1_landed(r1, r1r, 2, 1))
    for k in range(4, 8):
        for n in range(6):
            x, y = outside1(k, 1, 1 + n // 2)
            r1[n % 2, x, y : y + 1, :] = cr1[1, k - 4, n : n + 1, :]
    rr1 = (r1.at[0], r1.at[1])
    uu1 = (u1.at[0], u1.at[1])
    vv1 = (v1.at[0], v1.at[1])

    def first1(a):
        for v in range(2):
            u1[v, a] = rd1[a] * r1[v, a]

    slabs(H1 - 2, b1x + 4, b1x + 4, first1)
    sweep(uu1, vv1, rr1, ops1, H1 - 1, b1x + 2, b1x // 2 + 1)
    num1, den1 = zero8, zero8
    quads = []
    for i in range(b2x):
        pair = []
        for k in range(2):
            a = H1 + 2 * i + k
            vs, es = residual(vv1[0], rr1[0], a, ops1)
            vc, ec = residual(vv1[1], rr1[1], a, ops1)
            both = (es + r1[0, a])[own_y]
            num1 = num1 + both * vc[own_y]
            den1 = den1 + both * vs[own_y]
            pair.append((es[own_y], ec[own_y]))
        quads.append([y_pairs(pair[0][v] + pair[1][v]) for v in range(2)])
        if i % 2:
            packed = [z_pairs(top_bottom(quads[i - 1][v], quads[i][v])) for v in range(2)]
            own2 = 0.125 * jnp.where(iota(TILE, 1) < z2, packed[0], packed[1])
            sr2[(i - 1) * b2y : (i + 1) * b2y, :] = own2
            gr[odd, me, (i - 1) * b2y : (i + 1) * b2y, :] = own2
    to_fellows(sr2, gr.at[odd, me], 2)
    num_row = jnp.sum(num0 + 8.0 * num1, axis=0, keepdims=True)
    den_row = jnp.sum(den0 + 8.0 * den1, axis=0, keepdims=True)
    row8 = iota(TILE, 0)
    part = jnp.where(row8 == 0, num_row, jnp.where(row8 == 1, den_row, 0.0))
    sp2[...] = part
    gp[me] = part
    to_fellows(sp2, gp.at[me], 4)

    def v1_corners(side, ref_v, ref_r, tiles, outward):
        for d in range(2):
            corner = 4 + 2 * side + d
            for n, (i, j) in enumerate(near1 + ((1, 2), (2, 1))):
                x = (outside1 if outward else inside1)(corner, i, j)[0]
                y = outside1(corner, i, j)[1]
                ref = ref_v if n < 6 else ref_r
                for v in range(2):
                    if outward:
                        ref[v, x, y : y + 1, :] = tiles[side, v, d, n : n + 1, :]
                    else:
                        tiles[side, v, d, n : n + 1, :] = ref[v, x, y : y + 1, :]

    for side in range(2):
        v1_corners(side, v1, r1, cv1, False)
    landed(gm.at[0, 0 : nb - 1], 0)
    to_twin(gm.at[odd], gm.at[odd], 1)
    landed(gm.at[0], 1)

    def unpack(src, dst):
        def step(w, _):
            for n in range(nn):
                for i in range(b2x):
                    dst[PAD2 + w * b2x + i, n * b2y : (n + 1) * b2y, :] = src[n % 2, n // 2 * nw + w, i * b2y : (i + 1) * b2y, :]
            return 0

        lax.fori_loop(0, nw, step, 0)

    unpack(gm, v2)
    build(v2, cx2, cy2, cz2, rd2, None, PAD2, x2, BASE_TAU / 16, z2, 8)

    def coarsen(x):
        if x.shape[0] == 16:
            return 0.125 * z_pairs(top_bottom(y_pairs(x[0:8]), y_pairs(x[8:16])))
        return 0.125 * z_pairs(top_bottom(y_pairs(x), 0.0))

    def coarsen_pairs(get, xc, pad, dst):
        def step(g, _):
            for k in range(4):
                a = pad + 2 * (4 * g + k)
                dst[PAD + 4 * g + k] = coarsen(get(a) + get(a + 1))
            return 0

        lax.fori_loop(0, xc // 4, step, 0)

    coarsen_pairs(lambda a: v2[a], x3, PAD2, v3)
    build(v3, cx3, cy3, cz3, rd3, None, PAD, x3, BASE_TAU / 64, z2 // 2, 4)
    coarsen_pairs(lambda a: v3[a], x4, PAD, v4)
    build(v4, cx4, cy4, cz4, rd4, None, PAD, x4, BASE_TAU / 256, z2 // 4, 4)

    landed(gr.at[0, 0 : nb - 1], 2)
    to_twin(gr.at[odd], gr.at[odd], 3)

    def v1_sends(side):
        land = OPPOSITE[side]
        lo = H1 if side == 0 else H1 + b1x - 3
        return to_side(side, [(v1.at[:, lo : lo + 3, own_y], h1.at[land]), (cv1.at[side], hc.at[land])], v1r)

    each(lambda k: start(v1_sends(k)), range(2))
    each(lambda k: start(v0_sends(k)), range(4))

    def v0_landed(side):
        view = hx.at[side] if side < 2 else hy.at[side - 2]
        pltpu.make_async_copy(view, view, v0r.at[side]).wait()

    landed(gr.at[0], 3)
    unpack(gr, r2)

    ops2 = (cx2, cy2, cz2, rd2, None)
    ops3 = (cx3, cy3, cz3, rd3, None)
    ops4 = (cx4, cy4, cz4, rd4, None)

    def down(u, v, r, ops, pad, xc):
        def first(a):
            u[a] = ops[3][a] * r[a]

        slabs(pad, xc, 8, first)
        sweep((u,), (v,), (r,), ops, pad, xc, min(xc, 16) if u.shape[1] == 8 else 8)

    down(u2, v2, r2, ops2, PAD2, x2)
    low2 = iota(v2.shape[1:], 1) < z2

    def coarsen2(g, carry):
        num, den = carry
        for k in range(4):
            pair = []
            for j in range(2):
                a = PAD2 + 2 * (4 * g + k) + j
                v, e = residual(v2, r2, a, ops2)
                both = jnp.where(low2, e + r2[a], 0.0)
                num = num + fold(both * shift(v, z2, 1))
                den = den + fold(both * v)
                pair.append(e)
            r3[PAD + 4 * g + k] = coarsen(pair[0] + pair[1])
        return num, den

    num2, den2 = lax.fori_loop(0, x3 // 4, coarsen2, (zero8, zero8))
    landed(gp.at[0 : nb - 1], 4)
    total = gp[0]
    if nb <= 32:
        for w in range(1, nb):
            total = total + gp[w]
    else:
        total = lax.fori_loop(1, nb, lambda w, acc: acc + gp[w], total)
    pb[...] = total
    to_twin(pb, pbs, 5)
    down(u3, v3, r3, ops3, PAD, x3)
    coarsen_pairs(lambda a: residual(v3, r3, a, ops3)[1], x4, PAD, r4)
    down(u4, v4, r4, ops4, PAD, x4)

    def up3(g, _):
        for k in range(4):
            add = y_repeat(z_repeat(v4[PAD + 4 * g + k]))
            a = PAD + 2 * (4 * g + k)
            v3[a] = v3[a] + add
            v3[a + 1] = v3[a + 1] + add
        return 0

    lax.fori_loop(0, x4 // 4, up3, 0)
    sweep((v3,), (u3,), (r3,), ops3, PAD, x3, 16)
    sweep((u3,), (v3,), (r3,), ops3, PAD, x3, 16)
    low3 = iota(TILE, 1) < z2 // 2

    def dots(i, carry):
        num, den = carry
        for k in range(4):
            a = PAD + 4 * i + k
            both = jnp.where(low3, v3[a], 0.0)
            den = den + both * r3[a]
            num = num + both * shift(r3[a], -(z2 // 2), 1)
        return num, den

    num3, den3 = lax.fori_loop(0, x3 // 4, dots, (zero8, zero8))
    base = PAD2 + iw * b2x
    for i in range(b2x // 2 + 4):
        wide_tile = z_repeat(v3[PAD + iw * (b2x // 2) - 2 + i])
        for j in range(2):
            a = base - 4 + 2 * i + j
            v2[a, 0:8, :] = v2[a, 0:8, :] + y_repeat(wide_tile)
            v2[a, 8:16, :] = v2[a, 8:16, :] + y_repeat(wide_tile, 4)
    sweep((v2,), (u2,), (r2,), ops2, base - 3, b2x + 6, b2x + 6)
    sweep((u2,), (v2,), (r2,), ops2, base - 2, b2x + 4, b2x + 4)

    landed(pbs, 5)
    whole = total + pbs[...]
    num = jnp.sum(jnp.where(row8 == 0, whole, 0.0) + 64.0 * num2 + 512.0 * num3)
    den = jnp.sum(jnp.where(row8 == 1, whole, 0.0) + 64.0 * den2 + 512.0 * den3)
    ratio = (jnp.full(TILE, num) / (1.0 + jnp.full(TILE, den)))[0:1, :]

    def v1_landed(side):
        view = tok.at[0 : 10]
        pltpu.make_async_copy(view, view, v1r.at[side]).wait()

    each(v1_landed, range(2))
    for side, a in enumerate((H1 - 3, H1 + b1x)):
        v1[:, a : a + 3, own_y] = h1[side]
        v1_corners(side, v1, r1, hc, True)
    rows2 = v2.shape[1]
    full_y = 2 * rows2
    for i in range(b2x + 4):
        f1p[i, 0:b1y, :] = jnp.zeros((b1y, z1), F32)
        f1p[i, b1y + full_y : 2 * b1y + full_y, :] = jnp.zeros((b1y, z1), F32)
        for j in range(rows2 // 8):
            e = v2[base - 2 + i, 8 * j : 8 * j + 8, :]
            part = z_repeat(shift(e, z2, 1) - ratio * e)
            f1p[i, pl.ds(b1y + 16 * j, 8, stride=2), :] = part
            f1p[i, pl.ds(b1y + 16 * j + 1, 8, stride=2), :] = part
    window = pl.ds(pl.multiple_of(ino * b1y, 8), 3 * b1y)
    for x in range(-3, b1x + 3):
        a = H1 + x
        u1[0, a] = v1[1, a] - ratio * v1[0, a] + f1p[x // 2 + 2, window, :]
        if -2 <= x < b1x + 2:
            w1[a] = r1[1, a] - ratio * r1[0, a]
    sweep((u1.at[0],), (u1.at[1],), (w1,), ops1, H1 - 2, b1x + 4, b1x // 2 + 2)
    sweep((u1.at[1],), (u1.at[0],), (w1,), ops1, H1 - 1, b1x + 2, b1x // 2 + 1)

    each(v0_landed, range(4))
    for side, (x_far, x_near) in enumerate(((H0 - 2, H0 - 1), (H0 + bx + 1, H0 + bx))):
        for v, ref in enumerate((vs0, vc0)):
            ref[x_far, H0 : H0 + by, :] = hx[side, v, 0:by, :]
            ref[x_near, H0 - 1 : H0, :] = hx[side, v, by : by + 1, :]
            ref[x_near, H0 + by : H0 + by + 1, :] = hx[side, v, by + 1 : by + 2, :]
    for side, col in enumerate((H0 - 2, H0 + by + 1)):
        for v, ref in enumerate((vs0, vc0)):
            ref[H0 : H0 + bx, col, :] = hy[side, v]
    ratio0 = jnp.concatenate([ratio] * (nz // 128), axis=1)

    def up0(i):
        tiles = [u1[0, H1 - 1 + i, 8 * j : 8 * j + 8, :] for j in range(3)]
        rows = [top_bottom(y_repeat(tiles[0], 6), y_repeat(tiles[1], -2)),
                y_repeat(tiles[1], 2),
                top_bottom(y_repeat(tiles[1], 6), y_repeat(tiles[2], -2))]
        add = jnp.concatenate([jnp.concatenate([z_repeat(t), z_repeat(t, 64)], axis=1) for t in rows], axis=0)
        for k in range(2):
            a = H0 - 2 + 2 * i + k
            us0[a] = vc0[a] - ratio0 * vs0[a] + add
            rc0[a] = rc0[a] - ratio0 * rs0[a]

    slabs(0, b1x + 2, 2, up0)
    sweep((us0,), (uc0,), (rc0,), ops0, H0 - 1, bx + 2, 3)

    def last(a):
        own, t = neighbours(uc0, a, cx0, cy0, cz0)
        out_ref[a - H0] = (KEEP * own + rd0[a] * (rc0[a] + t))[H0 : H0 + by]

    slabs(H0, bx, 4, last)

    def sent(side):
        dx, dy = SIDES[side]
        if dy == 0:
            tiles = 6 * by * nz // 1024 + 3 + 4 + 2 * (by + 8) * nz // 1024 + 10
        elif dx == 0:
            tiles = 7 * bx * nz // 1024 + b1x + 2 * b1x + 2 * bx * nz // 1024
        else:
            tiles = 2 + 1 + 1
        view = tok.at[0:tiles]
        pltpu.make_async_copy(view, view, ss.at[side]).wait()

    each(sent)
    for kind, view in enumerate((gm.at[0, 0 : nb - 1], gm.at[0], gr.at[0, 0 : nb - 1], gr.at[0],
                                 gp.at[0 : nb - 1], pbs)):
        pltpu.make_async_copy(view, view, gs.at[kind]).wait()


def solution(mesh):
    nw, nn = mesh.shape["wide"], mesh.shape["narrow"]

    def per_device(mobility, sav_vector, cotangent):
        bx, by, nz = mobility.shape
        b1x, b1y, z1 = bx // 2, by // 2, nz // 2
        x2, y2 = nw * bx // 4, nn * by // 4
        own = (bx, by, nz)
        l0 = (bx + 2 * H0, by + 2 * H0, nz)
        l1 = (b1x + 2 * H1, 3 * b1y, z1)
        l2 = (x2 + 2 * PAD2, y2, z1)
        l3 = (x2 // 2 + 2 * PAD, y2 // 2, z1)
        l4 = (x2 // 4 + 2 * PAD, 8, z1)
        own2 = (bx // 4 * (by // 4), z1)
        buffers = (
            [own] * 3 + [l0] * 12
            + [(2, 4, by, nz), (2, 7, bx, nz), (2, 7, bx, nz), (4, 8, nz), (4, 8, nz)]
            + [(2, 2, by + 8, nz)] * 2 + [(2, 2, bx, nz)] * 2 + [(2, 2, by, nz)] * 2
            + [(1, *l1)] + [l1] * 5 + [(2, *l1)] * 3 + [l1] + [(2, 2, 3, b1y, z1), (2, 2, 2, b1y, z1), (2, 2, 2, b1y, z1), (2, 4, *TILE), (2, 4, *TILE)]
            + [l2] * 7 + [l3] * 7 + [l4] * 7
            + [(2, 2, b1x * l0[1], nz // 2)]
            + [own2, own2, TILE, (2, nn // 2 * nw, *own2), (2, nn // 2 * nw, *own2), (nn // 2 * nw, *TILE), TILE, TILE]
            + [(bx // 4 + 4, 2 * y2 + 2 * b1y, z1), (128, *TILE)]
        )
        size = sum(4 * functools.reduce(lambda p, q: p * q, shape) for shape in buffers)
        dma = lambda n: pltpu.SemaphoreType.DMA((n,))
        scratch = [pltpu.VMEM(shape, F32) for shape in buffers]
        scratch += [dma(n) for n in (3, 8, 6, 6, 8, 8, 8, 4, 2, 2)]
        return pl.pallas_call(
            functools.partial(kernel, nw, nn, bx, by, nz),
            out_shape=jax.ShapeDtypeStruct((bx, by, nz), F32),
            in_specs=[pl.BlockSpec(memory_space=pltpu.HBM)] * 3,
            out_specs=pl.BlockSpec(memory_space=pltpu.VMEM),
            scratch_shapes=scratch,
            compiler_params=pltpu.CompilerParams(
                collective_id=0, has_side_effects=True, vmem_limit_bytes=GRANT if size < GRANT else 67043328
            ),
        )(mobility, sav_vector, cotangent)

    spec = P("wide", "narrow", None)
    return jax.shard_map(per_device, mesh=mesh, in_specs=(spec,) * 3, out_specs=spec, check_vma=False)
```

```python
import functools
import jax
import jax.numpy as jnp
from jax import lax
from jax.experimental import pallas as pl
from jax.experimental.pallas import tpu as pltpu
from jax.sharding import PartitionSpec as P

DAMPING = 0.8
KEEP = 1.0 - DAMPING
BASE_TAU = 16.0
H0 = 4
H1 = 4
PAD = 2
PAD2 = 4
GRANT = 56200000
MESH = pl.DeviceIdType.MESH
F32 = jnp.float32
SIDES = [(-1, 0), (1, 0), (0, -1), (0, 1), (-1, -1), (-1, 1), (1, -1), (1, 1)]
OPPOSITE = [1, 0, 3, 2, 7, 6, 5, 4]
TILE = (8, 128)


def iota(shape, dim):
    return lax.broadcasted_iota(jnp.int32, shape, dim)


def shift(value, amount, axis):
    return pltpu.roll(value, amount % value.shape[axis], axis)


def take(value, index, axis):
    return jnp.take_along_axis(value, index, axis=axis, mode="promise_in_bounds")


def z_pairs(tile):
    return take(tile + shift(tile, -1, 1), lax.rem(2 * iota(TILE, 1), 128), 1)


def put_halves(ref, v, at, value):
    for h in range(2):
        ref[v, h, at, :] = value[:, 128 * h : 128 * h + 128]


def yz_pairs(ref, v, at):
    halves = []
    for h in range(2):
        halves.append(z_pairs(ref[v, h, pl.ds(at, 8, stride=2), :] + ref[v, h, pl.ds(at + 1, 8, stride=2), :]))
    return jnp.where(iota(TILE, 1) < 64, halves[0], halves[1])


def z_repeat(tile, start=0):
    return take(tile, start + iota(TILE, 1) // 2, 1)


def y_pairs(tile):
    return take(tile + shift(tile, -1, 0), lax.rem(2 * iota(TILE, 0), 8), 0)


def y_repeat(tile, start=0):
    return take(tile, jnp.clip(start + iota(TILE, 0) // 2, 0, 7), 0)


def top_bottom(top, bottom):
    return jnp.where(iota(TILE, 0) < 4, top, bottom)


def rounded(x):
    return x.astype(jnp.bfloat16).astype(F32)


def loop(count, chunk, body, carry):
    if count <= chunk:
        for i in range(count):
            carry = body(i, carry)
        return carry

    def step(g, carry):
        for k in range(chunk):
            carry = body(g * chunk + k, carry)
        return carry

    return lax.fori_loop(0, count // chunk, step, carry)


def slabs(lo, count, chunk, body):
    if count <= chunk:
        for k in range(count):
            body(lo + k)
        return

    def step(i, _):
        for k in range(chunk):
            body(lo + i * chunk + k)
        return 0

    lax.fori_loop(0, count // chunk, step, 0)


def build(m, cx, cy, cz, rd, d, lo, count, tau, seg, chunk, firsts=()):
    shape = m.shape[1:]
    row = iota(shape, 0)
    lane = lax.rem(iota(shape, 1), seg)
    last_row, first_row = row == shape[0] - 1, row == 0
    last_lane, first_lane = lane == seg - 1, lane == 0
    half = 0.5 * tau

    def body(a):
        own = m[a]
        xp, xm = m[a + 1], m[a - 1]
        yp = jnp.where(last_row, 0.0, shift(own, -1, 0))
        ym = jnp.where(first_row, 0.0, shift(own, 1, 0))
        zp = jnp.where(last_lane, 0.0, shift(own, -1, 1))
        zm = jnp.where(first_lane, 0.0, shift(own, 1, 1))
        total = 1.0
        for other, ref in ((xp, cx), (xm, None), (yp, cy), (ym, None), (zp, cz), (zm, None)):
            face = rounded(half * (own + other))
            total = total + face
            if ref is not None:
                ref[a] = jnp.where(jnp.minimum(own, other) > 0.0, face, 0.0)
        inverse = DAMPING / total
        rd[a] = inverse
        if d is not None:
            d[a] = total
        for r, u in firsts:
            u[a] = inverse * r[a]

    slabs(lo, count, chunk, body)


def neighbours(v, a, cx, cy, cz):
    own = v[a]
    cya, cza = cy[a], cz[a]
    total = cx[a] * v[a + 1] + cx[a - 1] * v[a - 1]
    total = total + (cya * shift(own, -1, 0) + shift(cya * own, 1, 0))
    total = total + (cza * shift(own, -1, 1) + shift(cza * own, 1, 1))
    return own, total


def sweep(vin, vout, r, ops, lo, count, chunk):
    cx, cy, cz, rd, d = ops

    def body(a):
        for vi, vo, ri in zip(vin, vout, r):
            own, t = neighbours(vi, a, cx, cy, cz)
            vo[a] = KEEP * own + rd[a] * (ri[a] + t)

    slabs(lo, count, chunk, body)


def residual(vi, ri, a, ops):
    cx, cy, cz, rd, d = ops
    own, t = neighbours(vi, a, cx, cy, cz)
    diag = d[a] if d is not None else DAMPING / rd[a]
    return own, ri[a] + t - diag * own


def fold(x):
    total = None
    for i in range(x.shape[0] // 8):
        for j in range(x.shape[1] // 128):
            part = x[8 * i : 8 * i + 8, 128 * j : 128 * j + 128]
            total = part if total is None else total + part
    return total


def fold_own(x):
    total = None
    for j in range(x.shape[1] // 128):
        lanes = slice(128 * j, 128 * j + 128)
        part = x[8:16, lanes] + top_bottom(x[16:24, lanes], x[0:8, lanes])
        total = part if total is None else total + part
    return total


def kernel(nw, nn, bx, by, nz, m_hbm, s_hbm, c_hbm, out_ref,
           m_ref, s_ref, c_ref,
           m0, cx0, cy0, cz0, rd0, d0, rs0, rc0, us0, uc0, vs0, vc0,
           rx, yp, ry, cp, rcn, xv, hx, yv, hy, xu, hu,
           m1, cx1, cy1, cz1, rd1, d1, r1, u1, v1, w1, h1, hc, cv1, cs1, cr1,
           cx2, cy2, cz2, rd2, r2, u2, v2, d2,
           cx3, cy3, cz3, rd3, r3, u3, v3, d3,
           cx4, cy4, cz4, rd4, r4, u4, v4,
           t0, sm2, sr2, sp2, gm, gr, gp, pb, pbs, f1p, tok,
           ins, ss, gs, gq, e0r, m1r, r1r, v0r, v1r, u0r):
    iw, ino = lax.axis_index("wide"), lax.axis_index("narrow")
    b1x, b1y, z1 = bx // 2, by // 2, nz // 2
    b2x, b2y, z2 = bx // 4, by // 4, nz // 4
    x2, x3, x4 = nw * b2x, nw * b2x // 2, nw * b2x // 4
    there = []
    for dx, dy in SIDES:
        ok = None
        for cond, on in ((iw > 0, dx < 0), (iw < nw - 1, dx > 0), (ino > 0, dy < 0), (ino < nn - 1, dy > 0)):
            if on:
                ok = cond if ok is None else jnp.logical_and(ok, cond)
        there.append(ok)

    def peer(side):
        return (iw + SIDES[side][0], ino + SIDES[side][1])

    inputs = [pltpu.make_async_copy(src, dst, ins.at[0])
              for src, dst in ((m_hbm, m_ref), (s_hbm, s_ref), (c_hbm, c_ref))]
    for copy in inputs:
        copy.start()

    def clear(ref, index):
        ref[index] = jnp.zeros(ref[index].shape, F32)

    barrier = pltpu.get_barrier_semaphore()

    nb = nn // 2 * nw
    me, odd = ino // 2 * nw + iw, lax.rem(ino, 2)
    twin = ino + 1 - 2 * odd

    def fellow(j):
        to = me + j
        to = jnp.where(to >= nb, to - nb, to)
        row = to // nw
        return to - row * nw, 2 * row + odd

    def over_fellows(fn):
        if nb <= 16:
            for j in range(1, nb):
                fn(j)
        else:
            def step(j, _):
                fn(j)
                return 0

            lax.fori_loop(1, nb, step, 0)

    over_fellows(lambda j: pl.semaphore_signal(barrier, inc=1, device_id=fellow(j), device_id_type=MESH))
    for j in range(1, nn, 2):
        pl.semaphore_signal(barrier, inc=1, device_id=(iw, lax.rem(ino + j, nn)), device_id_type=MESH)
    for k in range(4, 8):
        @pl.when(there[k])
        def _():
            pl.semaphore_signal(barrier, inc=1, device_id=peer(k), device_id_type=MESH)

    beside_x = jnp.minimum(iw, 1) + jnp.minimum(nw - 1 - iw, 1)
    beside_y = jnp.minimum(ino, 1) + jnp.minimum(nn - 1 - ino, 1)
    pl.semaphore_wait(barrier, nb - 1 + nn // 2 + beside_x * beside_y)

    def remote(src, dst, ssem, rsem, dev):
        return pltpu.make_async_remote_copy(src_ref=src, dst_ref=dst, send_sem=ssem, recv_sem=rsem,
                                            device_id=dev, device_id_type=MESH)

    def to_side(side, pairs, rsem):
        return [remote(src, dst, ss.at[side], rsem.at[OPPOSITE[side]], peer(side)) for src, dst in pairs]

    def e0_sends(side):
        land = OPPOSITE[side]
        if side < 2:
            pairs = []
            at = 0
            for ref, width in ((m_hbm, 2), (s_hbm, 1), (c_hbm, 1)):
                lo = 0 if side == 0 else bx - width
                pairs.append((ref.at[lo : lo + width], rx.at[land, at : at + width]))
                at += width
            return to_side(side, pairs, e0r)
        if side < 4:
            return to_side(side, [(yp.at[side - 2], ry.at[land - 2])], e0r)
        return to_side(side, [(cp.at[side - 4], rcn.at[land - 4])], e0r)

    def each(fn, sides=range(8)):
        for side in sides:
            @pl.when(there[side])
            def _():
                fn(side)

    def start(copies):
        for copy in copies:
            copy.start()

    each(lambda k: start(e0_sends(k)), (0, 1))
    view = tok.at[0 : 3 * bx * by * nz // 1024]
    pltpu.make_async_copy(view, view, ins.at[0]).wait()
    for side, (m_lo, r_lo) in enumerate(((0, 0), (by - 3, by - 2))):
        for k in range(3):
            yp[side, k] = m_ref[:, m_lo + k, :]
        for k in range(2):
            yp[side, 3 + k] = s_ref[:, r_lo + k, :]
            yp[side, 5 + k] = c_ref[:, r_lo + k, :]
    for k in range(4, 8):
        dx, dy = SIDES[k]
        xa, xb = (0, 1) if dx < 0 else (bx - 1, bx - 2)
        ya, yb = (0, 1) if dy < 0 else (by - 1, by - 2)
        for i, (ref, x, y) in enumerate(((m_ref, xa, ya), (m_ref, xa, yb), (m_ref, xb, ya),
                                         (s_ref, xa, ya), (c_ref, xa, ya))):
            cp[k - 4, i : i + 1, :] = ref[x, y : y + 1, :]

    each(lambda k: start(e0_sends(k)), (2, 3, 4, 5, 6, 7))

    near1 = ((1, 1), (1, 2), (1, 3), (2, 1), (2, 2), (3, 1))
    near_m1 = near1 + ((2, 3), (1, 4))

    def inside1(side, i, j):
        dx, dy = SIDES[side]
        return H1 + i - 1 if dx < 0 else H1 + b1x - i, b1y + j - 1 if dy < 0 else 2 * b1y - j

    def outside1(side, i, j):
        dx, dy = SIDES[side]
        return H1 - i if dx < 0 else H1 + b1x + i - 1, b1y - j if dy < 0 else 2 * b1y + j - 1

    def box1(side, sending, width):
        dx, dy = SIDES[side]
        w = width
        if sending:
            xlo, w = (H1, w) if dx < 0 else ((H1 + b1x - w, w) if dx > 0 else (H1, b1x))
            ylo = b1y
        else:
            xlo, w = (H1 - w, w) if dx < 0 else ((H1 + b1x, w) if dx > 0 else (H1, b1x))
            ylo = b1y * (1 + dy)
        return xlo, w, ylo

    def level1_sends(ref, rsem, side, width, kc):
        if side > 3:
            return to_side(side, [(cs1.at[kc, side - 4], cr1.at[kc, OPPOSITE[side] - 4])], rsem)
        sx, w, sy = box1(side, True, width)
        tx, _, ty = box1(OPPOSITE[side], False, width)
        return to_side(side, [(ref.at[:, sx : sx + w, sy : sy + b1y], ref.at[:, tx : tx + w, ty : ty + b1y])], rsem)

    def level1_landed(ref, rsem, width, kc):
        def fn(side):
            if side > 3:
                view = cr1.at[kc, side - 4]
            else:
                tx, w, ty = box1(side, False, width)
                view = ref.at[:, tx : tx + w, ty : ty + b1y]
            pltpu.make_async_copy(view, view, rsem.at[side]).wait()
        return fn

    def e0_landed(side):
        view = rx.at[side] if side < 2 else (ry.at[side - 2] if side < 4 else rcn.at[side - 4])
        pltpu.make_async_copy(view, view, e0r.at[side]).wait()

    own_y = slice(b1y, 2 * b1y)
    for i in range(b1x):
        put_halves(t0, 0, slice(i * by, (i + 1) * by), m_ref[2 * i] + m_ref[2 * i + 1])
    for i in range(b1x):
        m1[0, H1 + i, own_y, :] = 0.125 * yz_pairs(t0, 0, i * by)
    for k in range(4, 8):
        for n, (i, j) in enumerate(near_m1):
            x, y = inside1(k, i, j)
            cs1[0, k - 4, n : n + 1, :] = m1[0, x, y : y + 1, :]
    for i in range(0, b2x, 2):
        quads = [y_pairs(m1[0, H1 + 2 * k, own_y, :] + m1[0, H1 + 2 * k + 1, own_y, :]) for k in (i, i + 1)]
        mob2 = 0.125 * z_pairs(top_bottom(quads[0], quads[1]))
        sm2[i * b2y : (i + 2) * b2y, :] = mob2
        gm[odd, me, i * b2y : (i + 2) * b2y, :] = mob2

    def to_fellows(src, dst, kind):
        over_fellows(lambda j: remote(src, dst, gs.at[2 if kind > 3 else kind % 2], gq.at[kind], fellow(j)).start())

    def to_twin(src, dst, kind):
        remote(src, dst, gs.at[2 if kind > 3 else kind % 2], gq.at[kind], (iw, twin)).start()

    def landed(view, kind):
        pltpu.make_async_copy(view, view, gq.at[kind]).wait()

    for ref, src, width in ((m0, m_ref, 2), (rs0, s_ref, 1), (rc0, c_ref, 1)):
        blank = jnp.zeros(m0.shape[1:], F32)
        for i in range(width):
            ref[H0 - 1 - i] = blank
            ref[H0 + bx + i] = blank

        def put(i):
            ref[H0 + i, H0 : H0 + by, :] = src[i]

        slabs(0, bx, bx, put)
    side_rows = (slice(0, b1y), slice(2 * b1y, 3 * b1y))
    for k in range(8):
        @pl.when(jnp.logical_not(there[k]))
        def _():
            if k > 3:
                clear(rcn, k - 4)
                clear(cr1, (0, k - 4))
                clear(cr1, (1, k - 4))
                return
            lands = ((rx, hx, hu, h1, hc) if k < 2 else (ry, hy))
            for ref in lands:
                clear(ref, k % 2)
            for ref, width in ((m1, 3), (r1, 2)):
                xlo, w, ylo = box1(k, False, width)
                clear(ref, (slice(None), slice(xlo, xlo + w), slice(ylo, ylo + b1y)))
    for a in (0, H1 + b1x + 3):
        clear(m1, (0, a))
    for a in (1, 2, 3, H1 + b1x, H1 + b1x + 1, H1 + b1x + 2):
        for rows in side_rows:
            clear(m1, (0, a, rows))
            for v in range(2):
                clear(r1, (v, a, rows))
    for ref in (us0, uc0):
        ref[H0 - 2] = jnp.zeros(m0.shape[1:], F32)
        ref[H0 + bx + 1] = jnp.zeros(m0.shape[1:], F32)
    for a in (0, 1, 2, 3, H1 + b1x, H1 + b1x + 1, H1 + b1x + 2, H1 + b1x + 3):
        for v in range(2):
            v1[v, a] = jnp.zeros(v1.shape[2:], F32)
    for ref in (u4, v4):
        zero = jnp.zeros(ref.shape[1:], F32)
        for a in (0, 1, ref.shape[0] - 2, ref.shape[0] - 1):
            ref[a] = zero
    for ref in (u2, v2, r2, cx2, cy2, cz2, rd2, u3, v3, r3, cx3, cy3, cz3, rd3):
        zero = jnp.zeros(ref.shape[1:], F32)
        for a in range(PAD2):
            ref[a] = zero
            ref[ref.shape[0] - 1 - a] = zero
    cx4[PAD - 1] = jnp.zeros(cx4.shape[1:], F32)

    each(e0_landed, (2, 3))
    fields = ((m0, 0, 3), (rs0, 3, 2), (rc0, 5, 2))
    for ref, at, width in fields:
        for i in range(width):
            ref[H0 : H0 + bx, H0 - width + i, :] = ry[0, at + i]
            ref[H0 : H0 + bx, H0 + by + i, :] = ry[1, at + i]

    ops0 = (cx0, cy0, cz0, rd0, d0)
    firsts0 = ((rs0, us0), (rc0, uc0))

    for side, a in enumerate((H0 + 1, H0 + bx - 2)):
        build(m0, cx0, cy0, cz0, rd0, d0, a, 1, BASE_TAU, nz, 1, firsts0)
        for v, ref in enumerate((us0, uc0)):
            xu[side, v] = ref[a, H0 : H0 + by, :]
    each(lambda k: start(to_side(k, [(xu.at[k], hu.at[OPPOSITE[k]])], u0r)), (0, 1))
    each(lambda k: start(level1_sends(m1, m1r, k, 3, 0)))
    build(m0, cx0, cy0, cz0, rd0, d0, H0 + 2, bx - 4, BASE_TAU, nz, bx - 4, firsts0)
    sweep((us0, uc0), (vs0, vc0), (rs0, rc0), ops0, H0 + 2, bx - 4, bx - 4)

    def down0(i, carry):
        num, den = carry
        sums = []
        for k in range(2):
            a = H0 + 2 * i + k
            vs, es = residual(vs0, rs0, a, ops0)
            vc, ec = residual(vc0, rc0, a, ops0)
            both = es + rs0[a]
            num = num + fold_own(both * vc)
            den = den + fold_own(both * vs)
            sums.append((es, ec))
        at = slice(i * m0.shape[1], (i + 1) * m0.shape[1])
        put_halves(t0, 0, at, sums[0][0] + sums[1][0])
        put_halves(t0, 1, at, sums[0][1] + sums[1][1])
        return num, den

    zero8 = jnp.zeros(TILE, F32)
    part0 = loop(b1x - 4, b1x - 4, lambda i, c: down0(2 + i, c), (zero8, zero8))

    def u0_landed(side):
        pltpu.make_async_copy(hu.at[side], hu.at[side], u0r.at[side]).wait()

    each(e0_landed, (0, 1, 4, 5, 6, 7))
    each(u0_landed, (0, 1))
    for ref, at, width in ((m0, 0, 2), (rs0, 2, 1), (rc0, 3, 1)):
        for i in range(width):
            ref[H0 - width + i, H0 : H0 + by, :] = rx[0, at + i]
            ref[H0 + bx + i, H0 : H0 + by, :] = rx[1, at + i]
    for v, ref in enumerate((us0, uc0)):
        ref[H0 - 2, H0 : H0 + by, :] = hu[0, v]
        ref[H0 + bx + 1, H0 : H0 + by, :] = hu[1, v]
    for k in range(4):
        dx, dy = SIDES[4 + k]
        xa, xb = (H0 - 1, H0 - 2) if dx < 0 else (H0 + bx, H0 + bx + 1)
        ya, yb = (H0 - 1, H0 - 2) if dy < 0 else (H0 + by, H0 + by + 1)
        for i, (ref, x, y) in enumerate(((m0, xa, ya), (m0, xa, yb), (m0, xb, ya), (rs0, xa, ya), (rc0, xa, ya))):
            ref[x, y : y + 1, :] = rcn[k, i : i + 1, :]
    beyond = m0[H0 - 2]
    own = m0[H0 - 1]
    cx0[H0 - 2] = jnp.where(jnp.minimum(own, beyond) > 0.0, rounded(0.5 * BASE_TAU * (own + beyond)), 0.0)
    for lo, v_lo in ((H0 - 1, H0 - 1), (H0 + bx - 1, H0 + bx - 2)):
        build(m0, cx0, cy0, cz0, rd0, d0, lo, 2, BASE_TAU, nz, 2, firsts0)
        sweep((us0, uc0), (vs0, vc0), (rs0, rc0), ops0, v_lo, 3, 3)
    num0, den0 = loop(2, 2, lambda i, c: down0(b1x - 2 + i, down0(i, c)), part0)
    for v in range(2):
        for i in range(b1x):
            r1[v, H1 + i, own_y, :] = 0.125 * yz_pairs(t0, v, i * m0.shape[1] + H0)
    for k in range(4, 8):
        for n in range(6):
            x, y = inside1(k, 1, 1 + n // 2)
            cs1[1, k - 4, n : n + 1, :] = r1[n % 2, x, y : y + 1, :]
    each(lambda k: start(level1_sends(r1, r1r, k, 2, 1)))
    to_fellows(sm2, gm.at[odd, me], 0)
    for side, (x_far, x_near) in enumerate(((H0 + 1, H0), (H0 + bx - 2, H0 + bx - 1))):
        for v, ref in enumerate((vs0, vc0)):
            xv[side, v, 0:by, :] = ref[x_far, H0 : H0 + by, :]
            xv[side, v, by : by + 1, :] = ref[x_near, H0 - 1 : H0, :]
            xv[side, v, by + 1 : by + 2, :] = ref[x_near, H0 + by : H0 + by + 1, :]
    for side, col in enumerate((H0 + 1, H0 + by - 2)):
        for v, ref in enumerate((vs0, vc0)):
            yv[side, v] = ref[H0 : H0 + bx, col, :]

    def v0_sends(side):
        land = OPPOSITE[side]
        src, dst = (xv.at[side], hx.at[land]) if side < 2 else (yv.at[side - 2], hy.at[land - 2])
        return to_side(side, [(src, dst)], v0r)

    each(level1_landed(m1, m1r, 3, 0))
    for k in range(4, 8):
        for n, (i, j) in enumerate(near_m1):
            x, y = outside1(k, i, j)
            m1[0, x, y : y + 1, :] = cr1[0, k - 4, n : n + 1, :]
    ops1 = (cx1, cy1, cz1, rd1, d1)
    build(m1.at[0], cx1, cy1, cz1, rd1, d1, H1 - 3, b1x + 6, BASE_TAU / 4, z1, b1x + 6)
    each(level1_landed(r1, r1r, 2, 1))
    for k in range(4, 8):
        for n in range(6):
            x, y = outside1(k, 1, 1 + n // 2)
            r1[n % 2, x, y : y + 1, :] = cr1[1, k - 4, n : n + 1, :]
    rr1 = (r1.at[0], r1.at[1])
    uu1 = (u1.at[0], u1.at[1])
    vv1 = (v1.at[0], v1.at[1])

    def first1(a):
        for v in range(2):
            u1[v, a] = rd1[a] * r1[v, a]

    slabs(H1 - 2, b1x + 4, b1x + 4, first1)
    sweep(uu1, vv1, rr1, ops1, H1 - 1, b1x + 2, b1x + 2)
    num1, den1 = zero8, zero8
    quads = []
    for i in range(b2x):
        pair = []
        for k in range(2):
            a = H1 + 2 * i + k
            vs, es = residual(vv1[0], rr1[0], a, ops1)
            vc, ec = residual(vv1[1], rr1[1], a, ops1)
            both = (es + r1[0, a])[own_y]
            num1 = num1 + both * vc[own_y]
            den1 = den1 + both * vs[own_y]
            pair.append((es[own_y], ec[own_y]))
        quads.append([y_pairs(pair[0][v] + pair[1][v]) for v in range(2)])
        if i % 2:
            packed = [z_pairs(top_bottom(quads[i - 1][v], quads[i][v])) for v in range(2)]
            own2 = 0.125 * jnp.where(iota(TILE, 1) < z2, packed[0], packed[1])
            sr2[(i - 1) * b2y : (i + 1) * b2y, :] = own2
            gr[odd, me, (i - 1) * b2y : (i + 1) * b2y, :] = own2
    to_fellows(sr2, gr.at[odd, me], 2)
    num_row = jnp.sum(num0 + 8.0 * num1, axis=0, keepdims=True)
    den_row = jnp.sum(den0 + 8.0 * den1, axis=0, keepdims=True)
    low1 = iota((1, 128), 1) < 64
    part = jnp.where(low1, num_row + shift(num_row, 64, 1), den_row + shift(den_row, 64, 1))
    sp2[...] = part
    gp[me] = part
    to_fellows(sp2, gp.at[me], 4)

    def v1_corners(side, ref_v, ref_r, tiles, outward):
        for d in range(2):
            corner = 4 + 2 * side + d
            for n, (i, j) in enumerate(near1 + ((1, 2), (2, 1))):
                x = (outside1 if outward else inside1)(corner, i, j)[0]
                y = outside1(corner, i, j)[1]
                ref = ref_v if n < 6 else ref_r
                for v in range(2):
                    if outward:
                        ref[v, x, y : y + 1, :] = tiles[side, v, d, n : n + 1, :]
                    else:
                        tiles[side, v, d, n : n + 1, :] = ref[v, x, y : y + 1, :]

    for side in range(2):
        v1_corners(side, v1, r1, cv1, False)
    landed(gm.at[0, 0 : nb - 1], 0)
    to_twin(gm.at[odd], gm.at[odd], 1)
    landed(gm.at[0], 1)
    def v1_sends(side):
        land = OPPOSITE[side]
        lo = H1 if side == 0 else H1 + b1x - 3
        return to_side(side, [(v1.at[:, lo : lo + 3, own_y], h1.at[land]), (cv1.at[side], hc.at[land])], v1r)

    each(lambda k: start(v1_sends(k)), range(2))

    def unpack(src, dst, u=None):
        def step(w, carry):
            for i in range(b2x):
                a = PAD2 + w * b2x + i
                for n in range(nn):
                    dst[a, n * b2y : (n + 1) * b2y, :] = src[n % 2, n // 2 * nw + w, i * b2y : (i + 1) * b2y, :]
                if u is not None:
                    u[a] = rd2[a] * dst[a]
            return carry

        loop(nw, 8, step, 0)

    unpack(gm, v2)
    kept2 = d2 if d2.shape == v2.shape else None
    build(v2, cx2, cy2, cz2, rd2, kept2, PAD2, x2, BASE_TAU / 16, z2, 16)

    def coarsen_y(x):
        if x.shape[0] == 16:
            return top_bottom(y_pairs(x[0:8]), y_pairs(x[8:16]))
        return top_bottom(y_pairs(x), 0.0)

    def coarsen_z(dst, lo, count):
        def body(a):
            dst[a] = 0.125 * z_pairs(dst[a])

        slabs(lo, count, min(count, 16), body)

    def coarsen_pairs(src, dst, xc, pad):
        def body(i, carry):
            a = PAD2 + 2 * i
            dst[pad + i] = coarsen_y(src[a] + src[a + 1])
            return carry

        loop(xc, 16, body, 0)
        coarsen_z(dst, pad, xc)

    coarsen_pairs(v2, v3, x3, PAD2)
    build(v3, cx3, cy3, cz3, rd3, d3, PAD2, x3, BASE_TAU / 64, z2 // 2, 16)
    coarsen_pairs(v3, v4, x4, PAD)
    build(v4, cx4, cy4, cz4, rd4, None, PAD, x4, BASE_TAU / 256, z2 // 4, 8)

    landed(gr.at[0, 0 : nb - 1], 2)
    to_twin(gr.at[odd], gr.at[odd], 3)

    each(lambda k: start(v0_sends(k)), range(4))

    def v0_landed(side):
        view = hx.at[side] if side < 2 else hy.at[side - 2]
        pltpu.make_async_copy(view, view, v0r.at[side]).wait()

    landed(gr.at[0], 3)
    unpack(gr, r2, u2)

    ops2 = (cx2, cy2, cz2, rd2, kept2)
    ops3 = (cx3, cy3, cz3, rd3, d3)
    ops4 = (cx4, cy4, cz4, rd4, None)

    def coarsen_residual(v, r, ops, dst, xc, pad, seg):
        low = iota(v.shape[1:], 1) < seg

        def step(i, carry):
            num, den = carry
            pair = []
            for j in range(2):
                a = PAD2 + 2 * i + j
                own, e = residual(v, r, a, ops)
                both = jnp.where(low, e + r[a], 0.0)
                num = num + fold(both * shift(own, -seg, 1))
                den = den + fold(both * own)
                pair.append(e)
            dst[pad + i] = coarsen_y(pair[0] + pair[1])
            return num, den

        sums = loop(xc, 16, step, (zero8, zero8))
        coarsen_z(dst, pad, xc)
        return sums

    sweep((u2,), (v2,), (r2,), ops2, PAD2, x2, 32)
    landed(gp.at[0 : nb - 1], 4)
    total = gp[0]
    if nb <= 32:
        for w in range(1, nb):
            total = total + gp[w]
    else:
        total = lax.fori_loop(1, nb, lambda w, acc: acc + gp[w], total)
    pb[...] = total
    to_twin(pb, pbs, 5)
    num2, den2 = coarsen_residual(v2, r2, ops2, r3, x3, PAD2, z2)
    def first3(a):
        u3[a] = rd3[a] * r3[a]

    slabs(PAD2, x3, 16, first3)
    sweep((u3,), (v3,), (r3,), ops3, PAD2, x3, 16)
    num3, den3 = coarsen_residual(v3, r3, ops3, r4, x4, PAD, z2 // 2)

    def first4(a):
        u4[a] = rd4[a] * r4[a]

    slabs(PAD, x4, 8, first4)
    sweep((u4,), (v4,), (r4,), ops4, PAD, x4, 8)
    low4 = iota(TILE, 1) < z2 // 4

    def dots(i, carry):
        num, den = carry
        for k in range(8):
            a = PAD + 8 * i + k
            both = jnp.where(low4, r4[a], 0.0)
            den = den + both * v4[a]
            num = num + both * shift(v4[a], -(z2 // 4), 1)
        return num, den

    num4, den4 = dots(0, (zero8, zero8)) if x4 == 8 else lax.fori_loop(0, x4 // 8, dots, (zero8, zero8))
    b3x = b2x // 2
    base3 = PAD2 + iw * b3x
    for i in range(b3x // 2 + 4):
        add = y_repeat(z_repeat(v4[PAD + iw * (b3x // 2) - 2 + i]))
        for j in range(2):
            a = base3 - 4 + 2 * i + j
            v3[a] = v3[a] + add
    sweep((v3,), (u3,), (r3,), ops3, base3 - 3, b3x + 6, b3x + 6)
    sweep((u3,), (v3,), (r3,), ops3, base3 - 2, b3x + 4, b3x + 4)
    landed(pbs, 5)
    whole = total + pbs[...]

    def total_of(mask, n2, n3, n4):
        x = jnp.sum(64.0 * n2 + 512.0 * n3 + 4096.0 * n4, axis=0, keepdims=True)
        return jnp.sum(x + jnp.where(mask, whole, 0.0), axis=1, keepdims=True)

    ratio = total_of(low1, num2, num3, num4) / (1.0 + total_of(jnp.logical_not(low1), den2, den3, den4))
    ratio = jnp.broadcast_to(ratio, (1, 128))
    base = PAD2 + iw * b2x
    for i in range(b2x // 2 + 4):
        wide_tile = z_repeat(v3[base3 - 2 + i])
        for j in range(2):
            a = base - 4 + 2 * i + j
            v2[a, 0:8, :] = v2[a, 0:8, :] + y_repeat(wide_tile)
            v2[a, 8:16, :] = v2[a, 8:16, :] + y_repeat(wide_tile, 4)
    sweep((v2,), (u2,), (r2,), ops2, base - 3, b2x + 6, b2x + 6)
    sweep((u2,), (v2,), (r2,), ops2, base - 2, b2x + 4, b2x + 4)

    def v1_landed(side):
        view = tok.at[0 : 10]
        pltpu.make_async_copy(view, view, v1r.at[side]).wait()

    each(v1_landed, range(2))
    for side, a in enumerate((H1 - 3, H1 + b1x)):
        v1[:, a : a + 3, own_y] = h1[side]
        v1_corners(side, v1, r1, hc, True)
    rows2 = v2.shape[1]
    full_y = 2 * rows2
    for i in range(b2x + 4):
        f1p[i, 0:b1y, :] = jnp.zeros((b1y, z1), F32)
        f1p[i, b1y + full_y : 2 * b1y + full_y, :] = jnp.zeros((b1y, z1), F32)
        for j in range(rows2 // 8):
            e = v2[base - 2 + i, 8 * j : 8 * j + 8, :]
            part = z_repeat(shift(e, z2, 1) - ratio * e)
            f1p[i, pl.ds(b1y + 16 * j, 8, stride=2), :] = part
            f1p[i, pl.ds(b1y + 16 * j + 1, 8, stride=2), :] = part
    window = pl.ds(pl.multiple_of(ino * b1y, 8), 3 * b1y)
    for x in range(-3, b1x + 3):
        a = H1 + x
        u1[0, a] = v1[1, a] - ratio * v1[0, a] + f1p[x // 2 + 2, window, :]
        if -2 <= x < b1x + 2:
            w1[a] = r1[1, a] - ratio * r1[0, a]
    sweep((u1.at[0],), (u1.at[1],), (w1,), ops1, H1 - 2, b1x + 4, b1x + 4)
    sweep((u1.at[1],), (u1.at[0],), (w1,), ops1, H1 - 1, b1x + 2, b1x + 2)

    each(v0_landed, range(4))
    for side, (x_far, x_near) in enumerate(((H0 - 2, H0 - 1), (H0 + bx + 1, H0 + bx))):
        for v, ref in enumerate((vs0, vc0)):
            ref[x_far, H0 : H0 + by, :] = hx[side, v, 0:by, :]
            ref[x_near, H0 - 1 : H0, :] = hx[side, v, by : by + 1, :]
            ref[x_near, H0 + by : H0 + by + 1, :] = hx[side, v, by + 1 : by + 2, :]
    for side, col in enumerate((H0 - 2, H0 + by + 1)):
        for v, ref in enumerate((vs0, vc0)):
            ref[H0 : H0 + bx, col, :] = hy[side, v]
    ratio0 = jnp.concatenate([ratio] * (nz // 128), axis=1)

    def up0(g):
        tiles = [[u1[0, H1 - 1 + 2 * g + k, 8 * j : 8 * j + 8, :] for j in range(3)] for k in range(2)]
        sub = iota(TILE, 0)
        ends = [top_bottom(jnp.where(sub < 2, shift(t[0], 2, 0), shift(t[2], 2, 0)), 0.0) for t in tiles]
        ends = top_bottom(ends[0], shift(ends[1], 4, 0))
        halves = [[z_repeat(t, start) for t in (ends, tiles[0][1], tiles[1][1])] for start in (0, 64)]
        for k in range(2):
            adds = []
            for end, mid in ((h[0], h[1 + k]) for h in halves):
                end = shift(end, -4 * k, 0) if k else end
                adds.append((top_bottom(y_repeat(end), y_repeat(mid, -2)), y_repeat(mid, 2),
                             top_bottom(y_repeat(mid, 6), y_repeat(end))))
            add = jnp.concatenate([jnp.concatenate([adds[0][j], adds[1][j]], axis=1) for j in range(3)], axis=0)
            for i in range(2):
                a = H0 - 2 + 4 * g + 2 * k + i
                us0[a] = vc0[a] - ratio0 * vs0[a] + add
                rc0[a] = rc0[a] - ratio0 * rs0[a]

    slabs(0, b1x // 2 + 1, b1x // 2 + 1, up0)
    sweep((us0,), (uc0,), (rc0,), ops0, H0 - 1, bx + 2, bx + 2)

    def last(a):
        own, t = neighbours(uc0, a, cx0, cy0, cz0)
        out_ref[a - H0] = (KEEP * own + rd0[a] * (rc0[a] + t))[H0 : H0 + by]

    slabs(H0, bx, bx, last)

    def sent(side):
        dx, dy = SIDES[side]
        if dy == 0:
            tiles = 6 * by * nz // 1024 + 3 + 4 + 2 * (by + 8) * nz // 1024 + 10
        elif dx == 0:
            tiles = 7 * bx * nz // 1024 + b1x + 2 * b1x + 2 * bx * nz // 1024
        else:
            tiles = 2 + 1 + 1
        view = tok.at[0:tiles]
        pltpu.make_async_copy(view, view, ss.at[side]).wait()

    each(sent)
    for i, view in enumerate((gr.at[:, 0 : nb - 1], gr, gp)):
        pltpu.make_async_copy(view, view, gs.at[i]).wait()


def solution(mesh):
    nw, nn = mesh.shape["wide"], mesh.shape["narrow"]

    def per_device(mobility, sav_vector, cotangent):
        bx, by, nz = mobility.shape
        b1x, b1y, z1 = bx // 2, by // 2, nz // 2
        x2, y2 = nw * bx // 4, nn * by // 4
        own = (bx, by, nz)
        l0 = (bx + 2 * H0, by + 2 * H0, nz)
        l1 = (b1x + 2 * H1, 3 * b1y, z1)
        l2 = (x2 + 2 * PAD2, y2, z1)
        l3 = (x2 // 2 + 2 * PAD2, y2 // 2, z1)
        l4 = (x2 // 4 + 2 * PAD, 8, z1)
        own2 = (bx // 4 * (by // 4), z1)
        buffers = (
            [own] * 3 + [l0] * 12
            + [(2, 4, by, nz), (2, 7, bx, nz), (2, 7, bx, nz), (4, 8, nz), (4, 8, nz)]
            + [(2, 2, by + 8, nz)] * 2 + [(2, 2, bx, nz)] * 2 + [(2, 2, by, nz)] * 2
            + [(1, *l1)] + [l1] * 5 + [(2, *l1)] * 3 + [l1] + [(2, 2, 3, b1y, z1), (2, 2, 2, b1y, z1), (2, 2, 2, b1y, z1), (2, 4, *TILE), (2, 4, *TILE)]
            + [l2] * 7 + [l2 if nw <= 16 else (1, *TILE)] + [l3] * 8 + [l4] * 7
            + [(2, 2, b1x * l0[1], nz // 2)]
            + [own2, own2, (1, 128), (2, nn // 2 * nw, *own2), (2, nn // 2 * nw, *own2), (nn // 2 * nw, 1, 128), (1, 128), (1, 128)]
            + [(bx // 4 + 4, 2 * y2 + 2 * b1y, z1), (3 * bx * by * nz // 1024, *TILE)]
        )
        size = sum(4 * functools.reduce(lambda p, q: p * q, shape) for shape in buffers)
        dma = lambda n: pltpu.SemaphoreType.DMA((n,))
        scratch = [pltpu.VMEM(shape, F32) for shape in buffers]
        scratch += [dma(n) for n in (1, 8, 3, 6, 8, 8, 8, 4, 2, 2)]
        return pl.pallas_call(
            functools.partial(kernel, nw, nn, bx, by, nz),
            out_shape=jax.ShapeDtypeStruct((bx, by, nz), F32),
            in_specs=[pl.BlockSpec(memory_space=pltpu.HBM)] * 3,
            out_specs=pl.BlockSpec(memory_space=pltpu.VMEM),
            scratch_shapes=scratch,
            compiler_params=pltpu.CompilerParams(
                collective_id=0, has_side_effects=True, vmem_limit_bytes=GRANT if size < GRANT else 67043328
            ),
        )(mobility, sav_vector, cotangent)

    spec = P("wide", "narrow", None)
    return jax.shard_map(per_device, mesh=mesh, in_specs=(spec,) * 3, out_specs=spec, check_vma=False)
```

```python
import functools
import jax
import jax.numpy as jnp
from jax import lax
from jax.experimental import pallas as pl
from jax.experimental.pallas import tpu as pltpu
from jax.sharding import PartitionSpec as P

DAMPING = 0.8
KEEP = 1.0 - DAMPING
BASE_TAU = 16.0
H0 = 4
H1 = 4
PAD = 2
PAD2 = 4
GRANT = 56200000
MESH = pl.DeviceIdType.MESH
F32 = jnp.float32
SIDES = [(-1, 0), (1, 0), (0, -1), (0, 1), (-1, -1), (-1, 1), (1, -1), (1, 1)]
OPPOSITE = [1, 0, 3, 2, 7, 6, 5, 4]
TILE = (8, 128)


def iota(shape, dim):
    return lax.broadcasted_iota(jnp.int32, shape, dim)


def shift(value, amount, axis):
    return pltpu.roll(value, amount % value.shape[axis], axis)


def take(value, index, axis):
    return jnp.take_along_axis(value, index, axis=axis, mode="promise_in_bounds")


def z_pairs(tile):
    return take(tile + shift(tile, -1, 1), lax.rem(2 * iota(TILE, 1), 128), 1)


def put_halves(ref, v, at, value):
    for h in range(2):
        ref[v, h, at, :] = value[:, 128 * h : 128 * h + 128]


def yz_pairs(ref, v, at):
    halves = []
    for h in range(2):
        halves.append(z_pairs(ref[v, h, pl.ds(at, 8, stride=2), :] + ref[v, h, pl.ds(at + 1, 8, stride=2), :]))
    return jnp.where(iota(TILE, 1) < 64, halves[0], halves[1])


def z_repeat(tile, start=0):
    return take(tile, start + iota(TILE, 1) // 2, 1)


def y_pairs(tile):
    return take(tile + shift(tile, -1, 0), lax.rem(2 * iota(TILE, 0), 8), 0)


def y_repeat(tile, start=0):
    return take(tile, jnp.clip(start + iota(TILE, 0) // 2, 0, 7), 0)


def top_bottom(top, bottom):
    return jnp.where(iota(TILE, 0) < 4, top, bottom)


def rounded(x):
    return x.astype(jnp.bfloat16).astype(F32)


def loop(count, chunk, body, carry):
    if count <= chunk:
        for i in range(count):
            carry = body(i, carry)
        return carry

    def step(g, carry):
        for k in range(chunk):
            carry = body(g * chunk + k, carry)
        return carry

    return lax.fori_loop(0, count // chunk, step, carry)


def slabs(lo, count, chunk, body):
    if count <= chunk:
        for k in range(count):
            body(lo + k)
        return

    def step(i, _):
        for k in range(chunk):
            body(lo + i * chunk + k)
        return 0

    lax.fori_loop(0, count // chunk, step, 0)


def build(m, cx, cy, cz, rd, d, lo, count, tau, seg, chunk, firsts=()):
    shape = m.shape[1:]
    row = iota(shape, 0)
    lane = lax.rem(iota(shape, 1), seg)
    last_row, first_row = row == shape[0] - 1, row == 0
    last_lane, first_lane = lane == seg - 1, lane == 0
    half = 0.5 * tau

    def body(a):
        own = m[a]
        xp, xm = m[a + 1], m[a - 1]
        yp = jnp.where(last_row, 0.0, shift(own, -1, 0))
        ym = jnp.where(first_row, 0.0, shift(own, 1, 0))
        zp = jnp.where(last_lane, 0.0, shift(own, -1, 1))
        zm = jnp.where(first_lane, 0.0, shift(own, 1, 1))
        total = 1.0
        for other, ref in ((xp, cx), (xm, None), (yp, cy), (ym, None), (zp, cz), (zm, None)):
            face = rounded(half * (own + other))
            total = total + face
            if ref is not None:
                ref[a] = jnp.where(jnp.minimum(own, other) > 0.0, face, 0.0)
        inverse = DAMPING / total
        rd[a] = inverse
        if d is not None:
            d[a] = total
        for r, u in firsts:
            u[a] = inverse * r[a]

    slabs(lo, count, chunk, body)


def neighbours(v, a, cx, cy, cz):
    own = v[a]
    cya, cza = cy[a], cz[a]
    total = cx[a] * v[a + 1] + cx[a - 1] * v[a - 1]
    total = total + (cya * shift(own, -1, 0) + shift(cya * own, 1, 0))
    total = total + (cza * shift(own, -1, 1) + shift(cza * own, 1, 1))
    return own, total


def sweep(vin, vout, r, ops, lo, count, chunk):
    cx, cy, cz, rd, d = ops

    def body(a):
        for vi, vo, ri in zip(vin, vout, r):
            own, t = neighbours(vi, a, cx, cy, cz)
            vo[a] = KEEP * own + rd[a] * (ri[a] + t)

    slabs(lo, count, chunk, body)


def residual(vi, ri, a, ops):
    cx, cy, cz, rd, d = ops
    own, t = neighbours(vi, a, cx, cy, cz)
    diag = d[a] if d is not None else DAMPING / rd[a]
    return own, ri[a] + t - diag * own


def fold(x):
    total = None
    for i in range(x.shape[0] // 8):
        for j in range(x.shape[1] // 128):
            part = x[8 * i : 8 * i + 8, 128 * j : 128 * j + 128]
            total = part if total is None else total + part
    return total


def fold_own(x):
    total = None
    for j in range(x.shape[1] // 128):
        lanes = slice(128 * j, 128 * j + 128)
        part = x[8:16, lanes] + top_bottom(x[16:24, lanes], x[0:8, lanes])
        total = part if total is None else total + part
    return total


def kernel(nw, nn, bx, by, nz, m_hbm, s_hbm, c_hbm, out_ref,
           m_ref, s_ref, c_ref,
           m0, cx0, cy0, cz0, rd0, d0, rs0, rc0, us0, uc0, vs0, vc0,
           rx, yp, ry, cp, rcn, xv, hx, yv, hy, xu, hu,
           m1, cx1, cy1, cz1, rd1, d1, r1, u1, v1, w1, h1, hc, cv1, cs1, cr1, cs2, cr2,
           cx2, cy2, cz2, rd2, r2, u2, v2, d2,
           cx3, cy3, cz3, rd3, r3, u3, v3, d3,
           cx4, cy4, cz4, rd4, r4, u4, v4,
           t0, sm2, sr2, sp2, gm, gr, gp, pb, pbs, f1p, tok,
           ins, ss, gs, gq, e0r, y0r, m1r, r1r, v0r, v1r, u0r):
    iw, ino = lax.axis_index("wide"), lax.axis_index("narrow")
    b1x, b1y, z1 = bx // 2, by // 2, nz // 2
    b2x, b2y, z2 = bx // 4, by // 4, nz // 4
    x2, x3, x4 = nw * b2x, nw * b2x // 2, nw * b2x // 4
    there = []
    for dx, dy in SIDES:
        ok = None
        for cond, on in ((iw > 0, dx < 0), (iw < nw - 1, dx > 0), (ino > 0, dy < 0), (ino < nn - 1, dy > 0)):
            if on:
                ok = cond if ok is None else jnp.logical_and(ok, cond)
        there.append(ok)

    def peer(side):
        return (iw + SIDES[side][0], ino + SIDES[side][1])

    inputs = [pltpu.make_async_copy(src, dst, ins.at[0])
              for src, dst in ((m_hbm, m_ref), (s_hbm, s_ref), (c_hbm, c_ref))]
    for copy in inputs:
        copy.start()

    def clear(ref, index):
        ref[index] = jnp.zeros(ref[index].shape, F32)

    barrier = pltpu.get_barrier_semaphore()

    nb = nn // 2 * nw
    me, odd = ino // 2 * nw + iw, lax.rem(ino, 2)
    twin = ino + 1 - 2 * odd

    def fellow(j):
        to = me + j
        to = jnp.where(to >= nb, to - nb, to)
        row = to // nw
        return to - row * nw, 2 * row + odd

    def over_fellows(fn):
        if nb <= 16:
            for j in range(1, nb):
                fn(j)
        else:
            def step(j, _):
                fn(j)
                return 0

            lax.fori_loop(1, nb, step, 0)

    over_fellows(lambda j: pl.semaphore_signal(barrier, inc=1, device_id=fellow(j), device_id_type=MESH))
    for j in range(1, nn, 2):
        pl.semaphore_signal(barrier, inc=1, device_id=(iw, lax.rem(ino + j, nn)), device_id_type=MESH)
    for k in range(4, 8):
        @pl.when(there[k])
        def _():
            pl.semaphore_signal(barrier, inc=1, device_id=peer(k), device_id_type=MESH)

    beside_x = jnp.minimum(iw, 1) + jnp.minimum(nw - 1 - iw, 1)
    beside_y = jnp.minimum(ino, 1) + jnp.minimum(nn - 1 - ino, 1)
    pl.semaphore_wait(barrier, nb - 1 + nn // 2 + beside_x * beside_y)

    def remote(src, dst, ssem, rsem, dev):
        return pltpu.make_async_remote_copy(src_ref=src, dst_ref=dst, send_sem=ssem, recv_sem=rsem,
                                            device_id=dev, device_id_type=MESH)

    def to_side(side, pairs, rsem):
        land = OPPOSITE[side]
        if rsem is e0r and land > 3:
            land -= 2
        return [remote(src, dst, ss.at[side], rsem.at[land], peer(side)) for src, dst in pairs]

    def e0_sends(side):
        land = OPPOSITE[side]
        if side < 2:
            pairs = []
            at = 0
            for ref, width in ((m_hbm, 2), (s_hbm, 1), (c_hbm, 1)):
                lo = 0 if side == 0 else bx - width
                pairs.append((ref.at[lo : lo + width], rx.at[land, at : at + width]))
                at += width
            return to_side(side, pairs, e0r)
        return to_side(side, [(cp.at[side - 4], rcn.at[land - 4])], e0r)

    def y0_sends(side, lo, hi, sem):
        land = OPPOSITE[side] - 2
        return [remote(yp.at[side - 2, lo:hi], ry.at[land, lo:hi], ss.at[side], y0r.at[sem + land], peer(side))]

    def each(fn, sides=range(8)):
        for side in sides:
            @pl.when(there[side])
            def _():
                fn(side)

    def start(copies):
        for copy in copies:
            copy.start()

    each(lambda k: start(e0_sends(k)), (0, 1))
    view = tok.at[0 : 3 * bx * by * nz // 1024]
    pltpu.make_async_copy(view, view, ins.at[0]).wait()
    def yp_fill(side, at, ref, k):
        yp[side, at] = ref[:, by - 1 - k if side else k, :]

    for side in range(2):
        yp_fill(side, 0, m_ref, 0)
    each(lambda k: start(y0_sends(k, 0, 1, 0)), (2, 3))
    for side in range(2):
        for at, (ref, k) in enumerate(((m_ref, 1), (m_ref, 2), (s_ref, 0), (s_ref, 1), (c_ref, 0), (c_ref, 1))):
            yp_fill(side, 1 + at, ref, k)
    each(lambda k: start(y0_sends(k, 1, 7, 2)), (2, 3))
    for k in range(4, 8):
        dx, dy = SIDES[k]
        xa, xb = (0, 1) if dx < 0 else (bx - 1, bx - 2)
        ya, yb = (0, 1) if dy < 0 else (by - 1, by - 2)
        for i, (ref, x, y) in enumerate(((m_ref, xa, ya), (m_ref, xa, yb), (m_ref, xb, ya),
                                         (s_ref, xa, ya), (c_ref, xa, ya))):
            cp[k - 4, i] = ref[x, y : y + 1, :]

    each(lambda k: start(e0_sends(k)), (4, 5, 6, 7))

    near1 = ((1, 1), (1, 2), (1, 3), (2, 1), (2, 2), (3, 1))
    near_m1 = near1 + ((2, 3), (1, 4))

    def inside1(side, i, j):
        dx, dy = SIDES[side]
        return H1 + i - 1 if dx < 0 else H1 + b1x - i, b1y + j - 1 if dy < 0 else 2 * b1y - j

    def outside1(side, i, j):
        dx, dy = SIDES[side]
        return H1 - i if dx < 0 else H1 + b1x + i - 1, b1y - j if dy < 0 else 2 * b1y + j - 1

    def box1(side, sending, width):
        dx, dy = SIDES[side]
        w = width
        if sending:
            xlo, w = (H1, w) if dx < 0 else ((H1 + b1x - w, w) if dx > 0 else (H1, b1x))
            ylo = b1y
        else:
            xlo, w = (H1 - w, w) if dx < 0 else ((H1 + b1x, w) if dx > 0 else (H1, b1x))
            ylo = b1y * (1 + dy)
        return xlo, w, ylo

    def level1_sends(ref, rsem, side, width, kc):
        if side > 3:
            src, dst = (cs2, cr2) if kc else (cs1, cr1)
            return to_side(side, [(src.at[side - 4], dst.at[OPPOSITE[side] - 4])], rsem)
        sx, w, sy = box1(side, True, width)
        tx, _, ty = box1(OPPOSITE[side], False, width)
        return to_side(side, [(ref.at[:, sx : sx + w, sy : sy + b1y], ref.at[:, tx : tx + w, ty : ty + b1y])], rsem)

    def level1_landed(ref, rsem, width, kc):
        def fn(side):
            if side > 3:
                view = (cr2 if kc else cr1).at[side - 4]
            else:
                tx, w, ty = box1(side, False, width)
                view = ref.at[:, tx : tx + w, ty : ty + b1y]
            pltpu.make_async_copy(view, view, rsem.at[side]).wait()
        return fn

    def e0_landed(side):
        if side in (2, 3):
            view = ry.at[side - 2, 1:7]
            pltpu.make_async_copy(view, view, y0r.at[side]).wait()
        else:
            view = rx.at[side] if side < 2 else rcn.at[side - 4]
            pltpu.make_async_copy(view, view, e0r.at[side if side < 2 else side - 2]).wait()

    def near_landed(side):
        view = ry.at[side - 2, 0:1]
        pltpu.make_async_copy(view, view, y0r.at[side - 2]).wait()

    own_y = slice(b1y, 2 * b1y)
    for i in range(b1x):
        put_halves(t0, 0, slice(i * by, (i + 1) * by), m_ref[2 * i] + m_ref[2 * i + 1])
    for i in range(b1x):
        m1[0, H1 + i, own_y, :] = 0.125 * yz_pairs(t0, 0, i * by)
    for k in range(4, 8):
        for n, (i, j) in enumerate(near_m1):
            x, y = inside1(k, i, j)
            cs1[k - 4, n : n + 1, :] = m1[0, x, y : y + 1, :]
    for i in range(0, b2x, 2):
        quads = [y_pairs(m1[0, H1 + 2 * k, own_y, :] + m1[0, H1 + 2 * k + 1, own_y, :]) for k in (i, i + 1)]
        mob2 = 0.125 * z_pairs(top_bottom(quads[0], quads[1]))
        sm2[i * b2y : (i + 2) * b2y, :] = mob2
        gm[odd, me, i * b2y : (i + 2) * b2y, :] = mob2

    def to_fellows(src, dst, kind):
        over_fellows(lambda j: remote(src, dst, gs.at[2 if kind > 3 else kind % 2], gq.at[kind], fellow(j)).start())

    def to_twin(src, dst, kind):
        remote(src, dst, gs.at[2 if kind > 3 else kind % 2], gq.at[kind], (iw, twin)).start()

    def landed(view, kind):
        pltpu.make_async_copy(view, view, gq.at[kind]).wait()

    for ref, src, width in ((m0, m_ref, 2), (rs0, s_ref, 1), (rc0, c_ref, 1)):
        blank = jnp.zeros(m0.shape[1:], F32)
        for i in range(width):
            ref[H0 - 1 - i] = blank
            ref[H0 + bx + i] = blank

        def put(i):
            ref[H0 + i, H0 : H0 + by, :] = src[i]

        slabs(0, bx, bx, put)
    side_rows = (slice(0, b1y), slice(2 * b1y, 3 * b1y))
    for k in range(8):
        @pl.when(jnp.logical_not(there[k]))
        def _():
            if k > 3:
                clear(rcn, k - 4)
                clear(cr1, k - 4)
                clear(cr2, k - 4)
                return
            lands = ((rx, hx, hu, h1, hc) if k < 2 else (ry, hy))
            for ref in lands:
                clear(ref, k % 2)
            for ref, width in ((m1, 3), (r1, 2)):
                xlo, w, ylo = box1(k, False, width)
                clear(ref, (slice(None), slice(xlo, xlo + w), slice(ylo, ylo + b1y)))
    for a in (0, H1 + b1x + 3):
        clear(m1, (0, a))
    for a in (1, 2, 3, H1 + b1x, H1 + b1x + 1, H1 + b1x + 2):
        for rows in side_rows:
            clear(m1, (0, a, rows))
            for v in range(2):
                clear(r1, (v, a, rows))
    for ref in (us0, uc0):
        ref[H0 - 2] = jnp.zeros(m0.shape[1:], F32)
        ref[H0 + bx + 1] = jnp.zeros(m0.shape[1:], F32)
    for a in (0, 1, 2, 3, H1 + b1x, H1 + b1x + 1, H1 + b1x + 2, H1 + b1x + 3):
        for v in range(2):
            v1[v, a] = jnp.zeros(v1.shape[2:], F32)
    for ref in (u4, v4):
        zero = jnp.zeros(ref.shape[1:], F32)
        for a in (0, 1, ref.shape[0] - 2, ref.shape[0] - 1):
            ref[a] = zero
    for ref in (u2, v2, r2, cx2, cy2, cz2, rd2, u3, v3, r3, cx3, cy3, cz3, rd3):
        zero = jnp.zeros(ref.shape[1:], F32)
        for a in range(PAD2):
            ref[a] = zero
            ref[ref.shape[0] - 1 - a] = zero
    cx4[PAD - 1] = jnp.zeros(cx4.shape[1:], F32)

    ops0 = (cx0, cy0, cz0, rd0, d0)
    firsts0 = ((rs0, us0), (rc0, uc0))
    each(near_landed, (2, 3))
    m0[H0 : H0 + bx, H0 - 1, :] = ry[0, 0]
    m0[H0 : H0 + bx, H0 + by, :] = ry[1, 0]
    for side, a in enumerate((H0 + 1, H0 + bx - 2)):
        build(m0, cx0, cy0, cz0, rd0, d0, a, 1, BASE_TAU, nz, 1, firsts0)
        for v, ref in enumerate((us0, uc0)):
            xu[side, v] = ref[a, H0 : H0 + by, :]
    each(lambda k: start(to_side(k, [(xu.at[k], hu.at[OPPOSITE[k]])], u0r)), (0, 1))
    each(lambda k: start(level1_sends(m1, m1r, k, 3, 0)))
    each(e0_landed, (2, 3))
    for ref, at, lo, width in ((m0, 1, 1, 2), (rs0, 3, 0, 2), (rc0, 5, 0, 2)):
        for i in range(width):
            ref[H0 : H0 + bx, H0 - 1 - lo - i, :] = ry[0, at + i]
            ref[H0 : H0 + bx, H0 + by + lo + i, :] = ry[1, at + i]

    build(m0, cx0, cy0, cz0, rd0, d0, H0 + 1, bx - 2, BASE_TAU, nz, bx - 2, firsts0)
    sweep((us0, uc0), (vs0, vc0), (rs0, rc0), ops0, H0 + 2, bx - 4, bx - 4)

    def down0(i, carry):
        num, den = carry
        sums = []
        for k in range(2):
            a = H0 + 2 * i + k
            vs, es = residual(vs0, rs0, a, ops0)
            vc, ec = residual(vc0, rc0, a, ops0)
            both = es + rs0[a]
            num = num + fold_own(both * vc)
            den = den + fold_own(both * vs)
            sums.append((es, ec))
        at = slice(i * m0.shape[1], (i + 1) * m0.shape[1])
        put_halves(t0, 0, at, sums[0][0] + sums[1][0])
        put_halves(t0, 1, at, sums[0][1] + sums[1][1])
        return num, den

    zero8 = jnp.zeros(TILE, F32)
    part0 = loop(b1x - 4, b1x - 4, lambda i, c: down0(2 + i, c), (zero8, zero8))


    def coarse0(i):
        for v in range(2):
            r1[v, H1 + i, own_y, :] = 0.125 * yz_pairs(t0, v, i * m0.shape[1] + H0)

    slabs(2, b1x - 4, b1x - 4, coarse0)
    def u0_landed(side):
        pltpu.make_async_copy(hu.at[side], hu.at[side], u0r.at[side]).wait()

    each(e0_landed, (0, 1, 4, 5, 6, 7))
    for ref, at, width in ((m0, 0, 2), (rs0, 2, 1), (rc0, 3, 1)):
        for i in range(width):
            ref[H0 - width + i, H0 : H0 + by, :] = rx[0, at + i]
            ref[H0 + bx + i, H0 : H0 + by, :] = rx[1, at + i]
    for k in range(4):
        dx, dy = SIDES[4 + k]
        xa, xb = (H0 - 1, H0 - 2) if dx < 0 else (H0 + bx, H0 + bx + 1)
        ya, yb = (H0 - 1, H0 - 2) if dy < 0 else (H0 + by, H0 + by + 1)
        for i, (ref, x, y) in enumerate(((m0, xa, ya), (m0, xa, yb), (m0, xb, ya), (rs0, xa, ya), (rc0, xa, ya))):
            ref[x, y : y + 1, :] = rcn[k, i]
    beyond = m0[H0 - 2]
    own = m0[H0 - 1]
    cx0[H0 - 2] = jnp.where(jnp.minimum(own, beyond) > 0.0, rounded(0.5 * BASE_TAU * (own + beyond)), 0.0)
    for lo in (H0 - 1, H0 + bx - 1):
        build(m0, cx0, cy0, cz0, rd0, d0, lo, 2, BASE_TAU, nz, 2, firsts0)
    each(u0_landed, (0, 1))
    for v, ref in enumerate((us0, uc0)):
        ref[H0 - 2, H0 : H0 + by, :] = hu[0, v]
        ref[H0 + bx + 1, H0 : H0 + by, :] = hu[1, v]
    for v_lo in (H0 - 1, H0 + bx - 2):
        sweep((us0, uc0), (vs0, vc0), (rs0, rc0), ops0, v_lo, 3, 3)
    num0, den0 = loop(2, 2, lambda i, c: down0(b1x - 2 + i, down0(i, c)), part0)
    for i in (0, 1, b1x - 2, b1x - 1):
        coarse0(i)
    for k in range(4, 8):
        for n in range(6):
            x, y = inside1(k, 1, 1 + n // 2)
            cs2[k - 4, n] = r1[n % 2, x, y : y + 1, :]
    each(lambda k: start(level1_sends(r1, r1r, k, 2, 1)))
    to_fellows(sm2, gm.at[odd, me], 0)
    for side, (x_far, x_near) in enumerate(((H0 + 1, H0), (H0 + bx - 2, H0 + bx - 1))):
        for v, ref in enumerate((vs0, vc0)):
            xv[side, v, 0:by, :] = ref[x_far, H0 : H0 + by, :]
            xv[side, v, by : by + 1, :] = ref[x_near, H0 - 1 : H0, :]
            xv[side, v, by + 1 : by + 2, :] = ref[x_near, H0 + by : H0 + by + 1, :]
    for side, col in enumerate((H0 + 1, H0 + by - 2)):
        for v, ref in enumerate((vs0, vc0)):
            yv[side, v] = ref[H0 : H0 + bx, col, :]

    def v0_sends(side):
        land = OPPOSITE[side]
        src, dst = (xv.at[side], hx.at[land]) if side < 2 else (yv.at[side - 2], hy.at[land - 2])
        return to_side(side, [(src, dst)], v0r)

    each(level1_landed(m1, m1r, 3, 0))
    for k in range(4, 8):
        for n, (i, j) in enumerate(near_m1):
            x, y = outside1(k, i, j)
            m1[0, x, y : y + 1, :] = cr1[k - 4, n : n + 1, :]
    ops1 = (cx1, cy1, cz1, rd1, d1)
    build(m1.at[0], cx1, cy1, cz1, rd1, d1, H1 - 3, b1x + 6, BASE_TAU / 4, z1, b1x + 6)
    rr1 = (r1.at[0], r1.at[1])
    uu1 = (u1.at[0], u1.at[1])
    vv1 = (v1.at[0], v1.at[1])
    halves1 = {}

    def first1(a):
        for v in range(2):
            u1[v, a] = rd1[a] * r1[v, a]

    def down1(i, carry):
        num, den = carry
        pair = []
        for k in range(2):
            a = H1 + 2 * i + k
            vs, es = residual(vv1[0], rr1[0], a, ops1)
            vc, ec = residual(vv1[1], rr1[1], a, ops1)
            both = (es + r1[0, a])[own_y]
            num = num + both * vc[own_y]
            den = den + both * vs[own_y]
            pair.append((es[own_y], ec[own_y]))
        halves1[i] = [y_pairs(pair[0][v] + pair[1][v]) for v in range(2)]
        return num, den

    landed1 = level1_landed(r1, r1r, 2, 1)
    each(landed1, (2, 3))
    slabs(H1, b1x, b1x, first1)
    sweep(uu1, vv1, rr1, ops1, H1 + 1, b1x - 2, b1x - 2)
    sums1 = loop(b2x - 2, b2x - 2, lambda i, c: down1(1 + i, c), (zero8, zero8))
    each(landed1, (0, 1, 4, 5, 6, 7))
    for k in range(4, 8):
        for n in range(6):
            x, y = outside1(k, 1, 1 + n // 2)
            r1[n % 2, x, y : y + 1, :] = cr2[k - 4, n]
    for a in (H1 - 2, H1 + b1x):
        slabs(a, 2, 2, first1)
    for a in (H1 - 1, H1 + b1x - 1):
        sweep(uu1, vv1, rr1, ops1, a, 2, 2)
    num1, den1 = down1(b2x - 1, down1(0, sums1))
    for i in range(0, b2x, 2):
        packed = [z_pairs(top_bottom(halves1[i][v], halves1[i + 1][v])) for v in range(2)]
        own2 = 0.125 * jnp.where(iota(TILE, 1) < z2, packed[0], packed[1])
        sr2[i * b2y : (i + 2) * b2y, :] = own2
        gr[odd, me, i * b2y : (i + 2) * b2y, :] = own2
    to_fellows(sr2, gr.at[odd, me], 2)
    num_row = jnp.sum(num0 + 8.0 * num1, axis=0, keepdims=True)
    den_row = jnp.sum(den0 + 8.0 * den1, axis=0, keepdims=True)
    low1 = iota((1, 128), 1) < 64
    part = jnp.where(low1, num_row + shift(num_row, 64, 1), den_row + shift(den_row, 64, 1))
    sp2[...] = part
    gp[me] = part
    to_fellows(sp2, gp.at[me], 4)

    def v1_corners(side, ref_v, ref_r, tiles, outward):
        for d in range(2):
            corner = 4 + 2 * side + d
            for n, (i, j) in enumerate(near1 + ((1, 2), (2, 1))):
                x = (outside1 if outward else inside1)(corner, i, j)[0]
                y = outside1(corner, i, j)[1]
                ref = ref_v if n < 6 else ref_r
                for v in range(2):
                    if outward:
                        ref[v, x, y : y + 1, :] = tiles[side, v, d, n : n + 1, :]
                    else:
                        tiles[side, v, d, n : n + 1, :] = ref[v, x, y : y + 1, :]

    for side in range(2):
        v1_corners(side, v1, r1, cv1, False)
    landed(gm.at[0, 0 : nb - 1], 0)
    to_twin(gm.at[odd], gm.at[odd], 1)
    landed(gm.at[0], 1)
    def v1_sends(side):
        land = OPPOSITE[side]
        lo = H1 if side == 0 else H1 + b1x - 3
        return to_side(side, [(v1.at[:, lo : lo + 3, own_y], h1.at[land]), (cv1.at[side], hc.at[land])], v1r)

    each(lambda k: start(v1_sends(k)), range(2))
    each(lambda k: start(v0_sends(k)), range(4))

    def unpack(src, dst, u=None):
        def step(w, carry):
            for i in range(b2x):
                a = PAD2 + w * b2x + i
                for n in range(nn):
                    dst[a, n * b2y : (n + 1) * b2y, :] = src[n % 2, n // 2 * nw + w, i * b2y : (i + 1) * b2y, :]
                if u is not None:
                    u[a] = rd2[a] * dst[a]
            return carry

        loop(nw, 8, step, 0)

    unpack(gm, v2)
    kept2 = d2 if d2.shape == v2.shape else None
    build(v2, cx2, cy2, cz2, rd2, kept2, PAD2, x2, BASE_TAU / 16, z2, 16)

    def coarsen_y(x):
        if x.shape[0] == 16:
            return top_bottom(y_pairs(x[0:8]), y_pairs(x[8:16]))
        return top_bottom(y_pairs(x), 0.0)

    def coarsen_z(dst, lo, count):
        def body(a):
            dst[a] = 0.125 * z_pairs(dst[a])

        slabs(lo, count, min(count, 16), body)

    def coarsen_pairs(src, dst, xc, pad):
        def body(i, carry):
            a = PAD2 + 2 * i
            dst[pad + i] = coarsen_y(src[a] + src[a + 1])
            return carry

        loop(xc, 16, body, 0)
        coarsen_z(dst, pad, xc)

    coarsen_pairs(v2, v3, x3, PAD2)
    build(v3, cx3, cy3, cz3, rd3, d3, PAD2, x3, BASE_TAU / 64, z2 // 2, 16)
    coarsen_pairs(v3, v4, x4, PAD)
    build(v4, cx4, cy4, cz4, rd4, None, PAD, x4, BASE_TAU / 256, z2 // 4, 8)

    landed(gr.at[0, 0 : nb - 1], 2)
    to_twin(gr.at[odd], gr.at[odd], 3)


    def v0_landed(side):
        view = hx.at[side] if side < 2 else hy.at[side - 2]
        pltpu.make_async_copy(view, view, v0r.at[side]).wait()

    landed(gr.at[0], 3)
    landed(gp.at[0 : nb - 1], 4)
    total = gp[0]
    if nb <= 32:
        for w in range(1, nb):
            total = total + gp[w]
    else:
        total = lax.fori_loop(1, nb, lambda w, acc: acc + gp[w], total)
    pb[...] = total
    to_twin(pb, pbs, 5)
    unpack(gr, r2, u2)

    ops2 = (cx2, cy2, cz2, rd2, kept2)
    ops3 = (cx3, cy3, cz3, rd3, d3)
    ops4 = (cx4, cy4, cz4, rd4, None)

    def coarsen_residual(v, r, ops, dst, xc, pad, seg):
        low = iota(v.shape[1:], 1) < seg

        def step(i, carry):
            num, den = carry
            pair = []
            for j in range(2):
                a = PAD2 + 2 * i + j
                own, e = residual(v, r, a, ops)
                both = jnp.where(low, e + r[a], 0.0)
                num = num + fold(both * shift(own, -seg, 1))
                den = den + fold(both * own)
                pair.append(e)
            dst[pad + i] = coarsen_y(pair[0] + pair[1])
            return num, den

        sums = loop(xc, 16, step, (zero8, zero8))
        coarsen_z(dst, pad, xc)
        return sums

    sweep((u2,), (v2,), (r2,), ops2, PAD2, x2, 32)
    num2, den2 = coarsen_residual(v2, r2, ops2, r3, x3, PAD2, z2)
    def first3(a):
        u3[a] = rd3[a] * r3[a]

    slabs(PAD2, x3, 16, first3)
    sweep((u3,), (v3,), (r3,), ops3, PAD2, x3, 16)
    num3, den3 = coarsen_residual(v3, r3, ops3, r4, x4, PAD, z2 // 2)

    def first4(a):
        u4[a] = rd4[a] * r4[a]

    slabs(PAD, x4, 8, first4)
    sweep((u4,), (v4,), (r4,), ops4, PAD, x4, 8)
    low4 = iota(TILE, 1) < z2 // 4

    def dots(i, carry):
        num, den = carry
        for k in range(8):
            a = PAD + 8 * i + k
            both = jnp.where(low4, r4[a], 0.0)
            den = den + both * v4[a]
            num = num + both * shift(v4[a], -(z2 // 4), 1)
        return num, den

    num4, den4 = dots(0, (zero8, zero8)) if x4 == 8 else lax.fori_loop(0, x4 // 8, dots, (zero8, zero8))
    b3x = b2x // 2
    base3 = PAD2 + iw * b3x
    for i in range(b3x // 2 + 4):
        add = y_repeat(z_repeat(v4[PAD + iw * (b3x // 2) - 2 + i]))
        for j in range(2):
            a = base3 - 4 + 2 * i + j
            v3[a] = v3[a] + add
    sweep((v3,), (u3,), (r3,), ops3, base3 - 3, b3x + 6, b3x + 6)
    sweep((u3,), (v3,), (r3,), ops3, base3 - 2, b3x + 4, b3x + 4)
    landed(pbs, 5)
    whole = total + pbs[...]

    def total_of(mask, n2, n3, n4):
        x = jnp.sum(64.0 * n2 + 512.0 * n3 + 4096.0 * n4, axis=0, keepdims=True)
        return jnp.sum(x + jnp.where(mask, whole, 0.0), axis=1, keepdims=True)

    ratio = total_of(low1, num2, num3, num4) / (1.0 + total_of(jnp.logical_not(low1), den2, den3, den4))
    ratio = jnp.broadcast_to(ratio, (1, 128))
    base = PAD2 + iw * b2x
    for i in range(b2x // 2 + 4):
        wide_tile = z_repeat(v3[base3 - 2 + i])
        for j in range(2):
            a = base - 4 + 2 * i + j
            v2[a, 0:8, :] = v2[a, 0:8, :] + y_repeat(wide_tile)
            v2[a, 8:16, :] = v2[a, 8:16, :] + y_repeat(wide_tile, 4)
    sweep((v2,), (u2,), (r2,), ops2, base - 3, b2x + 6, b2x + 6)
    sweep((u2,), (v2,), (r2,), ops2, base - 2, b2x + 4, b2x + 4)

    def v1_landed(side):
        view = tok.at[0 : 10]
        pltpu.make_async_copy(view, view, v1r.at[side]).wait()

    each(v1_landed, range(2))
    for side, a in enumerate((H1 - 3, H1 + b1x)):
        v1[:, a : a + 3, own_y] = h1[side]
        v1_corners(side, v1, r1, hc, True)
    rows2 = v2.shape[1]
    full_y = 2 * rows2
    for i in range(b2x + 4):
        f1p[i, 0:b1y, :] = jnp.zeros((b1y, z1), F32)
        f1p[i, b1y + full_y : 2 * b1y + full_y, :] = jnp.zeros((b1y, z1), F32)
        for j in range(rows2 // 8):
            e = v2[base - 2 + i, 8 * j : 8 * j + 8, :]
            part = z_repeat(shift(e, z2, 1) - ratio * e)
            f1p[i, pl.ds(b1y + 16 * j, 8, stride=2), :] = part
            f1p[i, pl.ds(b1y + 16 * j + 1, 8, stride=2), :] = part
    window = pl.ds(pl.multiple_of(ino * b1y, 8), 3 * b1y)
    for x in range(-3, b1x + 3):
        a = H1 + x
        u1[0, a] = v1[1, a] - ratio * v1[0, a] + f1p[x // 2 + 2, window, :]
        if -2 <= x < b1x + 2:
            w1[a] = r1[1, a] - ratio * r1[0, a]
    sweep((u1.at[0],), (u1.at[1],), (w1,), ops1, H1 - 2, b1x + 4, b1x + 4)
    sweep((u1.at[1],), (u1.at[0],), (w1,), ops1, H1 - 1, b1x + 2, b1x + 2)

    each(v0_landed, range(4))
    for side, (x_far, x_near) in enumerate(((H0 - 2, H0 - 1), (H0 + bx + 1, H0 + bx))):
        for v, ref in enumerate((vs0, vc0)):
            ref[x_far, H0 : H0 + by, :] = hx[side, v, 0:by, :]
            ref[x_near, H0 - 1 : H0, :] = hx[side, v, by : by + 1, :]
            ref[x_near, H0 + by : H0 + by + 1, :] = hx[side, v, by + 1 : by + 2, :]
    for side, col in enumerate((H0 - 2, H0 + by + 1)):
        for v, ref in enumerate((vs0, vc0)):
            ref[H0 : H0 + bx, col, :] = hy[side, v]
    ratio0 = jnp.concatenate([ratio] * (nz // 128), axis=1)

    def up0(g):
        tiles = [[u1[0, H1 - 1 + 2 * g + k, 8 * j : 8 * j + 8, :] for j in range(3)] for k in range(2)]
        sub = iota(TILE, 0)
        ends = [top_bottom(jnp.where(sub < 2, shift(t[0], 2, 0), shift(t[2], 2, 0)), 0.0) for t in tiles]
        ends = top_bottom(ends[0], shift(ends[1], 4, 0))
        halves = [[z_repeat(t, start) for t in (ends, tiles[0][1], tiles[1][1])] for start in (0, 64)]
        for k in range(2):
            adds = []
            for end, mid in ((h[0], h[1 + k]) for h in halves):
                end = shift(end, -4 * k, 0) if k else end
                adds.append((top_bottom(y_repeat(end), y_repeat(mid, -2)), y_repeat(mid, 2),
                             top_bottom(y_repeat(mid, 6), y_repeat(end))))
            add = jnp.concatenate([jnp.concatenate([adds[0][j], adds[1][j]], axis=1) for j in range(3)], axis=0)
            for i in range(2):
                a = H0 - 2 + 4 * g + 2 * k + i
                us0[a] = vc0[a] - ratio0 * vs0[a] + add
                rc0[a] = rc0[a] - ratio0 * rs0[a]

    slabs(0, b1x // 2 + 1, b1x // 2 + 1, up0)
    sweep((us0,), (uc0,), (rc0,), ops0, H0 - 1, bx + 2, bx + 2)

    def last(a):
        own, t = neighbours(uc0, a, cx0, cy0, cz0)
        out_ref[a - H0] = (KEEP * own + rd0[a] * (rc0[a] + t))[H0 : H0 + by]

    slabs(H0, bx, bx, last)

    def sent(side):
        dx, dy = SIDES[side]
        if dy == 0:
            tiles = 6 * by * nz // 1024 + 3 + 4 + 2 * (by + 8) * nz // 1024 + 10
        elif dx == 0:
            tiles = 7 * bx * nz // 1024 + b1x + 2 * b1x + 2 * bx * nz // 1024
        else:
            tiles = 3
        view = tok.at[0:tiles]
        pltpu.make_async_copy(view, view, ss.at[side]).wait()

    each(sent)
    for i, view in enumerate((gr.at[:, 0 : nb - 1], gr, gp)):
        pltpu.make_async_copy(view, view, gs.at[i]).wait()


def solution(mesh):
    nw, nn = mesh.shape["wide"], mesh.shape["narrow"]

    def per_device(mobility, sav_vector, cotangent):
        bx, by, nz = mobility.shape
        b1x, b1y, z1 = bx // 2, by // 2, nz // 2
        x2, y2 = nw * bx // 4, nn * by // 4
        own = (bx, by, nz)
        l0 = (bx + 2 * H0, by + 2 * H0, nz)
        l1 = (b1x + 2 * H1, 3 * b1y, z1)
        l2 = (x2 + 2 * PAD2, y2, z1)
        l3 = (x2 // 2 + 2 * PAD2, y2 // 2, z1)
        l4 = (x2 // 4 + 2 * PAD, 8, z1)
        own2 = (bx // 4 * (by // 4), z1)
        buffers = (
            [own] * 3 + [l0] * 12
            + [(2, 4, by, nz), (2, 7, bx, nz), (2, 7, bx, nz), (4, 5, 1, nz), (4, 5, 1, nz)]
            + [(2, 2, by + 8, nz)] * 2 + [(2, 2, bx, nz)] * 2 + [(2, 2, by, nz)] * 2
            + [(1, *l1)] + [l1] * 5 + [(2, *l1)] * 3 + [l1] + [(2, 2, 3, b1y, z1), (2, 2, 2, b1y, z1), (2, 2, 2, b1y, z1), (4, *TILE), (4, *TILE), (4, 6, 1, z1), (4, 6, 1, z1)]
            + [l2] * 7 + [l2 if nw <= 16 else (1, *TILE)] + [l3] * 8 + [l4] * 7
            + [(2, 2, b1x * l0[1], nz // 2)]
            + [own2, own2, (1, 128), (2, nn // 2 * nw, *own2), (2, nn // 2 * nw, *own2), (nn // 2 * nw, 1, 128), (1, 128), (1, 128)]
            + [(bx // 4 + 4, 2 * y2 + 2 * b1y, z1), (3 * bx * by * nz // 1024, *TILE)]
        )
        size = sum(4 * functools.reduce(lambda p, q: p * q, shape) for shape in buffers)
        dma = lambda n: pltpu.SemaphoreType.DMA((n,))
        scratch = [pltpu.VMEM(shape, F32) for shape in buffers]
        scratch += [dma(n) for n in (1, 8, 3, 6, 6, 4, 8, 8, 4, 2, 2)]
        return pl.pallas_call(
            functools.partial(kernel, nw, nn, bx, by, nz),
            out_shape=jax.ShapeDtypeStruct((bx, by, nz), F32),
            in_specs=[pl.BlockSpec(memory_space=pltpu.HBM)] * 3,
            out_specs=pl.BlockSpec(memory_space=pltpu.VMEM),
            scratch_shapes=scratch,
            compiler_params=pltpu.CompilerParams(
                collective_id=0, has_side_effects=True, vmem_limit_bytes=GRANT if size < GRANT else 67043328
            ),
        )(mobility, sav_vector, cotangent)

    spec = P("wide", "narrow", None)
    return jax.shard_map(per_device, mesh=mesh, in_specs=(spec,) * 3, out_specs=spec, check_vma=False)
```

```python
import functools
import jax
import jax.numpy as jnp
from jax import lax
from jax.experimental import pallas as pl
from jax.experimental.pallas import tpu as pltpu
from jax.sharding import PartitionSpec as P

DAMPING = 0.8
KEEP = 1.0 - DAMPING
BASE_TAU = 16.0
H0 = 4
H1 = 4
PAD = 2
PAD2 = 4
GRANT = 56200000
MESH = pl.DeviceIdType.MESH
F32 = jnp.float32
SIDES = [(-1, 0), (1, 0), (0, -1), (0, 1), (-1, -1), (-1, 1), (1, -1), (1, 1)]
OPPOSITE = [1, 0, 3, 2, 7, 6, 5, 4]
TILE = (8, 128)


def iota(shape, dim):
    return lax.broadcasted_iota(jnp.int32, shape, dim)


def shift(value, amount, axis):
    return pltpu.roll(value, amount % value.shape[axis], axis)


def take(value, index, axis):
    return jnp.take_along_axis(value, index, axis=axis, mode="promise_in_bounds")


def z_pairs(tile):
    return take(tile + shift(tile, -1, 1), lax.rem(2 * iota(TILE, 1), 128), 1)


def put_halves(ref, v, at, value):
    for h in range(2):
        ref[v, h, at, :] = value[:, 128 * h : 128 * h + 128]


def yz_pairs(ref, v, at):
    halves = []
    for h in range(2):
        halves.append(z_pairs(ref[v, h, pl.ds(at, 8, stride=2), :] + ref[v, h, pl.ds(at + 1, 8, stride=2), :]))
    return jnp.where(iota(TILE, 1) < 64, halves[0], halves[1])


def z_repeat(tile, start=0):
    return take(tile, start + iota(TILE, 1) // 2, 1)


def y_pairs(tile):
    return take(tile + shift(tile, -1, 0), lax.rem(2 * iota(TILE, 0), 8), 0)


def y_repeat(tile, start=0):
    return take(tile, jnp.clip(start + iota(TILE, 0) // 2, 0, 7), 0)


def top_bottom(top, bottom):
    return jnp.where(iota(TILE, 0) < 4, top, bottom)


def rounded(x):
    return x.astype(jnp.bfloat16).astype(F32)


def loop(count, chunk, body, carry):
    if count <= chunk:
        for i in range(count):
            carry = body(i, carry)
        return carry

    def step(g, carry):
        for k in range(chunk):
            carry = body(g * chunk + k, carry)
        return carry

    return lax.fori_loop(0, count // chunk, step, carry)


def slabs(lo, count, chunk, body):
    if count <= chunk:
        for k in range(count):
            body(lo + k)
        return

    def step(i, _):
        for k in range(chunk):
            body(lo + i * chunk + k)
        return 0

    lax.fori_loop(0, count // chunk, step, 0)


def build(m, cx, cy, cz, rd, d, lo, count, tau, seg, chunk, firsts=()):
    shape = m.shape[1:]
    row = iota(shape, 0)
    lane = lax.rem(iota(shape, 1), seg)
    last_row, first_row = row == shape[0] - 1, row == 0
    last_lane, first_lane = lane == seg - 1, lane == 0
    half = 0.5 * tau

    def body(a):
        own = m[a]
        xp, xm = m[a + 1], m[a - 1]
        yp = jnp.where(last_row, 0.0, shift(own, -1, 0))
        ym = jnp.where(first_row, 0.0, shift(own, 1, 0))
        zp = jnp.where(last_lane, 0.0, shift(own, -1, 1))
        zm = jnp.where(first_lane, 0.0, shift(own, 1, 1))
        total = 1.0
        for other, ref in ((xp, cx), (xm, None), (yp, cy), (ym, None), (zp, cz), (zm, None)):
            face = rounded(half * (own + other))
            total = total + face
            if ref is not None:
                ref[a] = jnp.where(jnp.minimum(own, other) > 0.0, face, 0.0)
        inverse = DAMPING / total
        rd[a] = inverse
        if d is not None:
            d[a] = total
        for r, u in firsts:
            u[a] = inverse * r[a]

    slabs(lo, count, chunk, body)


def neighbours(v, a, cx, cy, cz):
    own = v[a]
    cya, cza = cy[a], cz[a]
    total = cx[a] * v[a + 1] + cx[a - 1] * v[a - 1]
    total = total + (cya * shift(own, -1, 0) + shift(cya * own, 1, 0))
    total = total + (cza * shift(own, -1, 1) + shift(cza * own, 1, 1))
    return own, total


def sweep(vin, vout, r, ops, lo, count, chunk):
    cx, cy, cz, rd, d = ops

    def body(a):
        for vi, vo, ri in zip(vin, vout, r):
            own, t = neighbours(vi, a, cx, cy, cz)
            vo[a] = KEEP * own + rd[a] * (ri[a] + t)

    slabs(lo, count, chunk, body)


def residual(vi, ri, a, ops):
    cx, cy, cz, rd, d = ops
    own, t = neighbours(vi, a, cx, cy, cz)
    diag = d[a] if d is not None else DAMPING / rd[a]
    return own, ri[a] + t - diag * own


def fold(x):
    total = None
    for i in range(x.shape[0] // 8):
        for j in range(x.shape[1] // 128):
            part = x[8 * i : 8 * i + 8, 128 * j : 128 * j + 128]
            total = part if total is None else total + part
    return total


def fold_own(x):
    total = None
    for j in range(x.shape[1] // 128):
        lanes = slice(128 * j, 128 * j + 128)
        part = x[8:16, lanes] + top_bottom(x[16:24, lanes], x[0:8, lanes])
        total = part if total is None else total + part
    return total


def kernel(nw, nn, bx, by, nz, m_hbm, s_hbm, c_hbm, out_ref,
           m_ref, s_ref, c_ref,
           m0, cx0, cy0, cz0, rd0, d0, rs0, rc0, us0, uc0, vs0, vc0,
           rx, yp, ry, cp, rcn, xv, hx, yv, hy, xu, hu,
           m1, cx1, cy1, cz1, rd1, d1, r1, u1, v1, w1, h1, hc, cv1, cs1, cr1, cs2, cr2, qs1, qr1,
           cx2, cy2, cz2, rd2, r2, u2, v2, d2,
           cx3, cy3, cz3, rd3, r3, u3, v3, d3,
           cx4, cy4, cz4, rd4, r4, u4, v4,
           t0, sm2, sr2, sp2, gm, gr, gp, pb, pbs, f1p, tok,
           ins, ss, gs, gq, e0r, y0r, m1r, r1r, v0r, v1r, u0r, mr):
    iw, ino = lax.axis_index("wide"), lax.axis_index("narrow")
    b1x, b1y, z1 = bx // 2, by // 2, nz // 2
    b2x, b2y, z2 = bx // 4, by // 4, nz // 4
    x2, x3, x4 = nw * b2x, nw * b2x // 2, nw * b2x // 4
    there = []
    for dx, dy in SIDES:
        ok = None
        for cond, on in ((iw > 0, dx < 0), (iw < nw - 1, dx > 0), (ino > 0, dy < 0), (ino < nn - 1, dy > 0)):
            if on:
                ok = cond if ok is None else jnp.logical_and(ok, cond)
        there.append(ok)

    def peer(side):
        return (iw + SIDES[side][0], ino + SIDES[side][1])

    inputs = [pltpu.make_async_copy(src, dst, ins.at[0])
              for src, dst in ((m_hbm, m_ref), (s_hbm, s_ref), (c_hbm, c_ref))]
    for copy in inputs:
        copy.start()

    def clear(ref, index):
        ref[index] = jnp.zeros(ref[index].shape, F32)

    barrier = pltpu.get_barrier_semaphore()

    nb = nn // 2 * nw
    me, odd = ino // 2 * nw + iw, lax.rem(ino, 2)
    twin = ino + 1 - 2 * odd

    def fellow(j):
        to = me + j
        to = jnp.where(to >= nb, to - nb, to)
        row = to // nw
        return to - row * nw, 2 * row + odd

    def over_fellows(fn):
        if nb <= 16:
            for j in range(1, nb):
                fn(j)
        else:
            def step(j, _):
                fn(j)
                return 0

            lax.fori_loop(1, nb, step, 0)

    rounds = []
    while 1 << len(rounds) < nb:
        rounds.append(1 << len(rounds))

    def partner(d):
        to = me + d - 2 * d * lax.rem(me // d, 2)
        row = to // nw
        return to - row * nw, 2 * row + odd

    for d in rounds[1:]:
        pl.semaphore_signal(barrier, inc=1, device_id=partner(d), device_id_type=MESH)
    for k in range(8):
        @pl.when(there[k])
        def _():
            pl.semaphore_signal(barrier, inc=1, device_id=peer(k), device_id_type=MESH)

    def meet(n):
        if n > 0:
            pl.semaphore_wait(mr.at[n - 1], 1)
        if n < len(rounds):
            pl.semaphore_signal(mr.at[n], inc=1, device_id=partner(rounds[n]), device_id_type=MESH)

    beside_x = jnp.minimum(iw, 1) + jnp.minimum(nw - 1 - iw, 1)
    beside_y = jnp.minimum(ino, 1) + jnp.minimum(nn - 1 - ino, 1)
    pl.semaphore_wait(barrier, len(rounds) - 1 + beside_x + beside_y + beside_x * beside_y)

    def remote(src, dst, ssem, rsem, dev):
        return pltpu.make_async_remote_copy(src_ref=src, dst_ref=dst, send_sem=ssem, recv_sem=rsem,
                                            device_id=dev, device_id_type=MESH)

    def to_side(side, pairs, rsem):
        land = OPPOSITE[side]
        if rsem is e0r and land > 3:
            land -= 2
        return [remote(src, dst, ss.at[side], rsem.at[land], peer(side)) for src, dst in pairs]

    def e0_sends(side):
        land = OPPOSITE[side]
        if side < 2:
            pairs = []
            at = 0
            for ref, width in ((m_hbm, 2), (s_hbm, 1), (c_hbm, 1)):
                lo = 0 if side == 0 else bx - width
                pairs.append((ref.at[lo : lo + width], rx.at[land, at : at + width]))
                at += width
            return to_side(side, pairs, e0r)
        return to_side(side, [(cp.at[side - 4], rcn.at[land - 4])], e0r)

    def y0_sends(side, lo, hi, sem):
        land = OPPOSITE[side] - 2
        return [remote(yp.at[side - 2, lo:hi], ry.at[land, lo:hi], ss.at[side], y0r.at[sem + land], peer(side))]

    def each(fn, sides=range(8)):
        for side in sides:
            @pl.when(there[side])
            def _():
                fn(side)

    def start(copies):
        for copy in copies:
            copy.start()

    each(lambda k: start(e0_sends(k)), (0, 1))
    meet(0)
    view = tok.at[0 : 3 * bx * by * nz // 1024]
    pltpu.make_async_copy(view, view, ins.at[0]).wait()
    def yp_fill(side, at, ref, k):
        yp[side, at] = ref[:, by - 1 - k if side else k, :]

    for side in range(2):
        yp_fill(side, 0, m_ref, 0)
    each(lambda k: start(y0_sends(k, 0, 1, 0)), (2, 3))
    for side in range(2):
        for at, (ref, k) in enumerate(((m_ref, 1), (m_ref, 2), (s_ref, 0), (s_ref, 1), (c_ref, 0), (c_ref, 1))):
            yp_fill(side, 1 + at, ref, k)
    each(lambda k: start(y0_sends(k, 1, 7, 2)), (2, 3))
    for k in range(4, 8):
        dx, dy = SIDES[k]
        xa, xb = (0, 1) if dx < 0 else (bx - 1, bx - 2)
        ya, yb = (0, 1) if dy < 0 else (by - 1, by - 2)
        for i, (ref, x, y) in enumerate(((m_ref, xa, ya), (m_ref, xa, yb), (m_ref, xb, ya),
                                         (s_ref, xa, ya), (c_ref, xa, ya))):
            cp[k - 4, i] = ref[x, y : y + 1, :]

    each(lambda k: start(e0_sends(k)), (4, 5, 6, 7))

    near1 = ((1, 1), (1, 2), (1, 3), (2, 1), (2, 2), (3, 1))
    near_m1 = near1 + ((2, 3), (1, 4))

    def inside1(side, i, j):
        dx, dy = SIDES[side]
        return H1 + i - 1 if dx < 0 else H1 + b1x - i, b1y + j - 1 if dy < 0 else 2 * b1y - j

    def outside1(side, i, j):
        dx, dy = SIDES[side]
        return H1 - i if dx < 0 else H1 + b1x + i - 1, b1y - j if dy < 0 else 2 * b1y + j - 1

    def box1(side, sending, width):
        dx, dy = SIDES[side]
        w = width
        if sending:
            xlo, w = (H1, w) if dx < 0 else ((H1 + b1x - w, w) if dx > 0 else (H1, b1x))
            ylo = b1y
        else:
            xlo, w = (H1 - w, w) if dx < 0 else ((H1 + b1x, w) if dx > 0 else (H1, b1x))
            ylo = b1y * (1 + dy)
        return xlo, w, ylo

    def level1_sends(ref, rsem, side, width, kc):
        if side > 3:
            src, dst = (cs2, cr2) if kc else (cs1, cr1)
            return to_side(side, [(src.at[side - 4], dst.at[OPPOSITE[side] - 4])], rsem)
        if kc and side > 1:
            return to_side(side, [(qs1.at[side - 2], qr1.at[OPPOSITE[side] - 2])], rsem)
        sx, w, sy = box1(side, True, width)
        tx, _, ty = box1(OPPOSITE[side], False, width)
        return to_side(side, [(ref.at[:, sx : sx + w, sy : sy + b1y], ref.at[:, tx : tx + w, ty : ty + b1y])], rsem)

    def r1_pack(side):
        for x in range(b1x):
            rs, rc = r1[0, H1 + x, own_y, :], r1[1, H1 + x, own_y, :]
            qs1[side - 2, x] = top_bottom(rs, shift(rc, 4, 0)) if side == 2 else top_bottom(shift(rs, 4, 0), rc)

    def r1_unpack(side):
        rows = side_rows[side - 2]
        for x in range(b1x):
            tile = qr1[side - 2, x]
            other = shift(tile, 4, 0)
            r1[0, H1 + x, rows, :] = other if side == 2 else tile
            r1[1, H1 + x, rows, :] = tile if side == 2 else other

    def level1_landed(ref, rsem, width, kc):
        def fn(side):
            if side > 3:
                view = (cr2 if kc else cr1).at[side - 4]
            elif kc and side > 1:
                view = qr1.at[side - 2]
            else:
                tx, w, ty = box1(side, False, width)
                view = ref.at[:, tx : tx + w, ty : ty + b1y]
            pltpu.make_async_copy(view, view, rsem.at[side]).wait()
        return fn

    def e0_landed(side):
        if side in (2, 3):
            view = ry.at[side - 2, 1:7]
            pltpu.make_async_copy(view, view, y0r.at[side]).wait()
        else:
            view = rx.at[side] if side < 2 else rcn.at[side - 4]
            pltpu.make_async_copy(view, view, e0r.at[side if side < 2 else side - 2]).wait()

    def near_landed(side):
        view = ry.at[side - 2, 0:1]
        pltpu.make_async_copy(view, view, y0r.at[side - 2]).wait()

    own_y = slice(b1y, 2 * b1y)
    for i in range(b1x):
        put_halves(t0, 0, slice(i * by, (i + 1) * by), m_ref[2 * i] + m_ref[2 * i + 1])
    for i in range(b1x):
        m1[0, H1 + i, own_y, :] = 0.125 * yz_pairs(t0, 0, i * by)
    for k in range(4, 8):
        for n, (i, j) in enumerate(near_m1):
            x, y = inside1(k, i, j)
            cs1[k - 4, n : n + 1, :] = m1[0, x, y : y + 1, :]
    low2 = iota(TILE, 1) < z2
    for i in range(0, b2x, 4):
        tiles = []
        for n in range(i, i + 4, 2):
            quads = [y_pairs(m1[0, H1 + 2 * k, own_y, :] + m1[0, H1 + 2 * k + 1, own_y, :]) for k in (n, n + 1)]
            tiles.append(0.125 * z_pairs(top_bottom(quads[0], quads[1])))
        mob2 = jnp.where(low2, tiles[0], tiles[1])
        sm2[2 * i : 2 * i + 8, :] = mob2
        gm[odd, me, 2 * i : 2 * i + 8, :] = mob2

    def to_fellows(src, dst, kind):
        over_fellows(lambda j: remote(src, dst, gs.at[kind if kind < 4 else 4], gq.at[kind], fellow(j)).start())

    def to_twin(src, dst, kind):
        remote(src, dst, gs.at[kind if kind < 4 else 4], gq.at[kind], (iw, twin)).start()

    def landed(view, kind):
        pltpu.make_async_copy(view, view, gq.at[kind]).wait()

    for ref, src, width in ((m0, m_ref, 2), (rs0, s_ref, 1), (rc0, c_ref, 1)):
        blank = jnp.zeros(m0.shape[1:], F32)
        for i in range(width):
            ref[H0 - 1 - i] = blank
            ref[H0 + bx + i] = blank

        def put(i):
            ref[H0 + i, H0 : H0 + by, :] = src[i]

        slabs(0, bx, bx, put)
    side_rows = (slice(0, b1y), slice(2 * b1y, 3 * b1y))
    for k in range(8):
        @pl.when(jnp.logical_not(there[k]))
        def _():
            if k > 3:
                clear(rcn, k - 4)
                clear(cr1, k - 4)
                clear(cr2, k - 4)
                return
            lands = ((rx, hx, hu, h1, hc) if k < 2 else (ry, hy, qr1))
            for ref in lands:
                clear(ref, k % 2)
            for ref, width in (((m1, 3), (r1, 2)) if k < 2 else ((m1, 3),)):
                xlo, w, ylo = box1(k, False, width)
                clear(ref, (slice(None), slice(xlo, xlo + w), slice(ylo, ylo + b1y)))
    for a in (0, H1 + b1x + 3):
        clear(m1, (0, a))
    for a in (1, 2, 3, H1 + b1x, H1 + b1x + 1, H1 + b1x + 2):
        for rows in side_rows:
            clear(m1, (0, a, rows))
            for v in range(2):
                clear(r1, (v, a, rows))
    for ref in (us0, uc0):
        ref[H0 - 2] = jnp.zeros(m0.shape[1:], F32)
        ref[H0 + bx + 1] = jnp.zeros(m0.shape[1:], F32)
    for a in (0, 1, 2, 3, H1 + b1x, H1 + b1x + 1, H1 + b1x + 2, H1 + b1x + 3):
        for v in range(2):
            v1[v, a] = jnp.zeros(v1.shape[2:], F32)
    for ref in (u4, v4):
        zero = jnp.zeros(ref.shape[1:], F32)
        for a in (0, 1, ref.shape[0] - 2, ref.shape[0] - 1):
            ref[a] = zero
    for ref in (u2, v2, r2, cx2, cy2, cz2, rd2, u3, v3, r3, cx3, cy3, cz3, rd3):
        zero = jnp.zeros(ref.shape[1:], F32)
        for a in range(PAD2):
            ref[a] = zero
            ref[ref.shape[0] - 1 - a] = zero
    cx4[PAD - 1] = jnp.zeros(cx4.shape[1:], F32)

    ops0 = (cx0, cy0, cz0, rd0, d0)
    firsts0 = ((rs0, us0), (rc0, uc0))
    meet(1)
    each(near_landed, (2, 3))
    m0[H0 : H0 + bx, H0 - 1, :] = ry[0, 0]
    m0[H0 : H0 + bx, H0 + by, :] = ry[1, 0]
    for side, a in enumerate((H0 + 1, H0 + bx - 2)):
        build(m0, cx0, cy0, cz0, rd0, d0, a, 1, BASE_TAU, nz, 1, firsts0)
        for v, ref in enumerate((us0, uc0)):
            xu[side, v] = ref[a, H0 : H0 + by, :]
    each(lambda k: start(to_side(k, [(xu.at[k], hu.at[OPPOSITE[k]])], u0r)), (0, 1))
    each(lambda k: start(level1_sends(m1, m1r, k, 3, 0)))
    each(e0_landed, (2, 3))
    for ref, at, lo, width in ((m0, 1, 1, 2), (rs0, 3, 0, 2), (rc0, 5, 0, 2)):
        for i in range(width):
            ref[H0 : H0 + bx, H0 - 1 - lo - i, :] = ry[0, at + i]
            ref[H0 : H0 + bx, H0 + by + lo + i, :] = ry[1, at + i]

    meet(2)
    build(m0, cx0, cy0, cz0, rd0, d0, H0 + 1, bx - 2, BASE_TAU, nz, bx - 2, firsts0)
    sweep((us0, uc0), (vs0, vc0), (rs0, rc0), ops0, H0 + 2, bx - 4, bx - 4)

    def down0(i, carry):
        num, den = carry
        sums = []
        for k in range(2):
            a = H0 + 2 * i + k
            vs, es = residual(vs0, rs0, a, ops0)
            vc, ec = residual(vc0, rc0, a, ops0)
            both = es + rs0[a]
            num = num + fold_own(both * vc)
            den = den + fold_own(both * vs)
            sums.append((es, ec))
        at = slice(i * m0.shape[1], (i + 1) * m0.shape[1])
        put_halves(t0, 0, at, sums[0][0] + sums[1][0])
        put_halves(t0, 1, at, sums[0][1] + sums[1][1])
        return num, den

    zero8 = jnp.zeros(TILE, F32)
    part0 = loop(b1x - 4, b1x - 4, lambda i, c: down0(2 + i, c), (zero8, zero8))


    def coarse0(i):
        for v in range(2):
            r1[v, H1 + i, own_y, :] = 0.125 * yz_pairs(t0, v, i * m0.shape[1] + H0)

    slabs(2, b1x - 4, b1x - 4, coarse0)
    meet(3)
    def u0_landed(side):
        pltpu.make_async_copy(hu.at[side], hu.at[side], u0r.at[side]).wait()

    each(e0_landed, (0, 1, 4, 5, 6, 7))
    for ref, at, width in ((m0, 0, 2), (rs0, 2, 1), (rc0, 3, 1)):
        for i in range(width):
            ref[H0 - width + i, H0 : H0 + by, :] = rx[0, at + i]
            ref[H0 + bx + i, H0 : H0 + by, :] = rx[1, at + i]
    for k in range(4):
        dx, dy = SIDES[4 + k]
        xa, xb = (H0 - 1, H0 - 2) if dx < 0 else (H0 + bx, H0 + bx + 1)
        ya, yb = (H0 - 1, H0 - 2) if dy < 0 else (H0 + by, H0 + by + 1)
        for i, (ref, x, y) in enumerate(((m0, xa, ya), (m0, xa, yb), (m0, xb, ya), (rs0, xa, ya), (rc0, xa, ya))):
            ref[x, y : y + 1, :] = rcn[k, i]
    beyond = m0[H0 - 2]
    own = m0[H0 - 1]
    cx0[H0 - 2] = jnp.where(jnp.minimum(own, beyond) > 0.0, rounded(0.5 * BASE_TAU * (own + beyond)), 0.0)
    for lo in (H0 - 1, H0 + bx - 1):
        build(m0, cx0, cy0, cz0, rd0, d0, lo, 2, BASE_TAU, nz, 2, firsts0)
    each(u0_landed, (0, 1))
    for v, ref in enumerate((us0, uc0)):
        ref[H0 - 2, H0 : H0 + by, :] = hu[0, v]
        ref[H0 + bx + 1, H0 : H0 + by, :] = hu[1, v]
    for v_lo in (H0 - 1, H0 + bx - 2):
        sweep((us0, uc0), (vs0, vc0), (rs0, rc0), ops0, v_lo, 3, 3)
    num0, den0 = loop(2, 2, lambda i, c: down0(b1x - 2 + i, down0(i, c)), part0)
    for i in (0, 1, b1x - 2, b1x - 1):
        coarse0(i)
    for k in range(4, 8):
        for n in range(6):
            x, y = inside1(k, 1, 1 + n // 2)
            cs2[k - 4, n] = r1[n % 2, x, y : y + 1, :]
    for k in (2, 3):
        r1_pack(k)
    each(lambda k: start(level1_sends(r1, r1r, k, 2, 1)))
    for side, (x_far, x_near) in enumerate(((H0 + 1, H0), (H0 + bx - 2, H0 + bx - 1))):
        for v, ref in enumerate((vs0, vc0)):
            xv[side, v, 0:by, :] = ref[x_far, H0 : H0 + by, :]
            xv[side, v, by : by + 1, :] = ref[x_near, H0 - 1 : H0, :]
            xv[side, v, by + 1 : by + 2, :] = ref[x_near, H0 + by : H0 + by + 1, :]
    for side, col in enumerate((H0 + 1, H0 + by - 2)):
        for v, ref in enumerate((vs0, vc0)):
            yv[side, v] = ref[H0 : H0 + bx, col, :]

    def v0_sends(side):
        land = OPPOSITE[side]
        src, dst = (xv.at[side], hx.at[land]) if side < 2 else (yv.at[side - 2], hy.at[land - 2])
        return to_side(side, [(src, dst)], v0r)

    each(level1_landed(m1, m1r, 3, 0))
    for k in range(4, 8):
        for n, (i, j) in enumerate(near_m1):
            x, y = outside1(k, i, j)
            m1[0, x, y : y + 1, :] = cr1[k - 4, n : n + 1, :]
    ops1 = (cx1, cy1, cz1, rd1, d1)
    build(m1.at[0], cx1, cy1, cz1, rd1, d1, H1 - 3, b1x + 6, BASE_TAU / 4, z1, b1x + 6)
    for n in range(4, len(rounds) + 1):
        meet(n)
    to_fellows(sm2, gm.at[odd, me], 0)
    rr1 = (r1.at[0], r1.at[1])
    uu1 = (u1.at[0], u1.at[1])
    vv1 = (v1.at[0], v1.at[1])
    halves1 = {}

    def first1(a):
        for v in range(2):
            u1[v, a] = rd1[a] * r1[v, a]

    def down1(i, carry):
        num, den = carry
        pair = []
        for k in range(2):
            a = H1 + 2 * i + k
            vs, es = residual(vv1[0], rr1[0], a, ops1)
            vc, ec = residual(vv1[1], rr1[1], a, ops1)
            both = (es + r1[0, a])[own_y]
            num = num + both * vc[own_y]
            den = den + both * vs[own_y]
            pair.append((es[own_y], ec[own_y]))
        halves1[i] = [y_pairs(pair[0][v] + pair[1][v]) for v in range(2)]
        return num, den

    landed1 = level1_landed(r1, r1r, 2, 1)
    each(landed1, (2, 3))
    for k in (2, 3):
        r1_unpack(k)
    slabs(H1, b1x, b1x, first1)
    sweep(uu1, vv1, rr1, ops1, H1 + 1, b1x - 2, b1x - 2)
    sums1 = loop(b2x - 2, b2x - 2, lambda i, c: down1(1 + i, c), (zero8, zero8))
    each(landed1, (0, 1, 4, 5, 6, 7))
    for k in range(4, 8):
        for n in range(6):
            x, y = outside1(k, 1, 1 + n // 2)
            r1[n % 2, x, y : y + 1, :] = cr2[k - 4, n]
    for a in (H1 - 2, H1 + b1x):
        slabs(a, 2, 2, first1)
    for a in (H1 - 1, H1 + b1x - 1):
        sweep(uu1, vv1, rr1, ops1, a, 2, 2)
    num1, den1 = down1(b2x - 1, down1(0, sums1))
    for i in range(0, b2x, 2):
        packed = [z_pairs(top_bottom(halves1[i][v], halves1[i + 1][v])) for v in range(2)]
        own2 = 0.125 * jnp.where(low2, packed[0], packed[1])
        sr2[i * b2y : (i + 2) * b2y, :] = own2
        gr[odd, me, i * b2y : (i + 2) * b2y, :] = own2
    to_fellows(sr2, gr.at[odd, me], 2)
    num_row = jnp.sum(num0 + 8.0 * num1, axis=0, keepdims=True)
    den_row = jnp.sum(den0 + 8.0 * den1, axis=0, keepdims=True)
    low1 = iota((1, 128), 1) < 64
    part = jnp.where(low1, num_row + shift(num_row, 64, 1), den_row + shift(den_row, 64, 1))
    sp2[...] = part
    gp[me] = part
    to_fellows(sp2, gp.at[me], 4)

    def v1_corners(side, ref_v, ref_r, tiles, outward):
        for d in range(2):
            corner = 4 + 2 * side + d
            for n, (i, j) in enumerate(near1 + ((1, 2), (2, 1))):
                x = (outside1 if outward else inside1)(corner, i, j)[0]
                y = outside1(corner, i, j)[1]
                ref = ref_v if n < 6 else ref_r
                for v in range(2):
                    if outward:
                        ref[v, x, y : y + 1, :] = tiles[side, v, d, n : n + 1, :]
                    else:
                        tiles[side, v, d, n : n + 1, :] = ref[v, x, y : y + 1, :]

    for side in range(2):
        v1_corners(side, v1, r1, cv1, False)
    landed(gm.at[0, 0 : nb - 1], 0)
    to_twin(gm.at[odd], gm.at[odd], 1)
    landed(gm.at[0], 1)
    def v1_sends(side):
        land = OPPOSITE[side]
        lo = H1 if side == 0 else H1 + b1x - 3
        return to_side(side, [(v1.at[:, lo : lo + 3, own_y], h1.at[land]), (cv1.at[side], hc.at[land])], v1r)


    def unpack(src, dst, u=None):
        def step(w, carry):
            for i in range(b2x):
                a = PAD2 + w * b2x + i
                for n in range(nn):
                    dst[a, n * b2y : (n + 1) * b2y, :] = src[n % 2, n // 2 * nw + w, i * b2y : (i + 1) * b2y, :]
                if u is not None:
                    u[a] = rd2[a] * dst[a]
            return carry

        loop(nw, 8, step, 0)

    def unpack_m(w, carry):
        for n in range(nn):
            for i in range(0, b2x, 4):
                tile = gm[n % 2, n // 2 * nw + w, 2 * i : 2 * i + 8, :]
                other = shift(tile, z2, 1)
                for k, part in enumerate((jnp.where(low2, tile, other), jnp.where(low2, other, tile))):
                    for h in range(2):
                        a = PAD2 + w * b2x + i + 2 * k + h
                        v2[a, n * b2y : (n + 1) * b2y, :] = part[h * b2y : (h + 1) * b2y, :]
        return carry

    loop(nw, 8, unpack_m, 0)
    kept2 = d2 if d2.shape == v2.shape else None
    build(v2, cx2, cy2, cz2, rd2, kept2, PAD2, x2, BASE_TAU / 16, z2, 16)

    def coarsen_y(x):
        if x.shape[0] == 16:
            return top_bottom(y_pairs(x[0:8]), y_pairs(x[8:16]))
        return top_bottom(y_pairs(x), 0.0)

    def coarsen_z(dst, lo, count):
        def body(a):
            dst[a] = 0.125 * z_pairs(dst[a])

        slabs(lo, count, min(count, 16), body)

    def coarsen_pairs(src, dst, xc, pad):
        def body(i, carry):
            a = PAD2 + 2 * i
            dst[pad + i] = coarsen_y(src[a] + src[a + 1])
            return carry

        loop(xc, 16, body, 0)
        coarsen_z(dst, pad, xc)

    coarsen_pairs(v2, v3, x3, PAD2)
    build(v3, cx3, cy3, cz3, rd3, d3, PAD2, x3, BASE_TAU / 64, z2 // 2, 16)
    coarsen_pairs(v3, v4, x4, PAD)
    build(v4, cx4, cy4, cz4, rd4, None, PAD, x4, BASE_TAU / 256, z2 // 4, 8)

    each(lambda k: start(v1_sends(k)), range(2))
    each(lambda k: start(v0_sends(k)), range(4))
    landed(gr.at[0, 0 : nb - 1], 2)
    to_twin(gr.at[odd], gr.at[odd], 3)


    def v0_landed(side):
        view = hx.at[side] if side < 2 else hy.at[side - 2]
        pltpu.make_async_copy(view, view, v0r.at[side]).wait()

    landed(gr.at[0], 3)
    landed(gp.at[0 : nb - 1], 4)
    total = gp[0]
    if nb <= 32:
        for w in range(1, nb):
            total = total + gp[w]
    else:
        total = lax.fori_loop(1, nb, lambda w, acc: acc + gp[w], total)
    pb[...] = total
    to_twin(pb, pbs, 5)
    unpack(gr, r2, u2)

    ops2 = (cx2, cy2, cz2, rd2, kept2)
    ops3 = (cx3, cy3, cz3, rd3, d3)
    ops4 = (cx4, cy4, cz4, rd4, None)

    def coarsen_residual(v, r, ops, dst, xc, pad, seg):
        low = iota(v.shape[1:], 1) < seg

        def step(i, carry):
            num, den = carry
            pair = []
            for j in range(2):
                a = PAD2 + 2 * i + j
                own, e = residual(v, r, a, ops)
                both = jnp.where(low, e + r[a], 0.0)
                num = num + fold(both * shift(own, -seg, 1))
                den = den + fold(both * own)
                pair.append(e)
            dst[pad + i] = coarsen_y(pair[0] + pair[1])
            return num, den

        sums = loop(xc, 16, step, (zero8, zero8))
        coarsen_z(dst, pad, xc)
        return sums

    sweep((u2,), (v2,), (r2,), ops2, PAD2, x2, 32)
    num2, den2 = coarsen_residual(v2, r2, ops2, r3, x3, PAD2, z2)
    def first3(a):
        u3[a] = rd3[a] * r3[a]

    slabs(PAD2, x3, 16, first3)
    sweep((u3,), (v3,), (r3,), ops3, PAD2, x3, 16)
    num3, den3 = coarsen_residual(v3, r3, ops3, r4, x4, PAD, z2 // 2)

    def first4(a):
        u4[a] = rd4[a] * r4[a]

    slabs(PAD, x4, 8, first4)
    sweep((u4,), (v4,), (r4,), ops4, PAD, x4, 8)
    low4 = iota(TILE, 1) < z2 // 4

    def dots(i, carry):
        num, den = carry
        for k in range(8):
            a = PAD + 8 * i + k
            both = jnp.where(low4, r4[a], 0.0)
            den = den + both * v4[a]
            num = num + both * shift(v4[a], -(z2 // 4), 1)
        return num, den

    num4, den4 = dots(0, (zero8, zero8)) if x4 == 8 else lax.fori_loop(0, x4 // 8, dots, (zero8, zero8))
    b3x = b2x // 2
    base3 = PAD2 + iw * b3x
    for i in range(b3x // 2 + 4):
        add = y_repeat(z_repeat(v4[PAD + iw * (b3x // 2) - 2 + i]))
        for j in range(2):
            a = base3 - 4 + 2 * i + j
            v3[a] = v3[a] + add
    sweep((v3,), (u3,), (r3,), ops3, base3 - 3, b3x + 6, b3x + 6)
    sweep((u3,), (v3,), (r3,), ops3, base3 - 2, b3x + 4, b3x + 4)
    landed(pbs, 5)
    whole = total + pbs[...]

    def total_of(mask, n2, n3, n4):
        x = jnp.sum(64.0 * n2 + 512.0 * n3 + 4096.0 * n4, axis=0, keepdims=True)
        return jnp.sum(x + jnp.where(mask, whole, 0.0), axis=1, keepdims=True)

    ratio = total_of(low1, num2, num3, num4) / (1.0 + total_of(jnp.logical_not(low1), den2, den3, den4))
    ratio = jnp.broadcast_to(ratio, (1, 128))
    base = PAD2 + iw * b2x
    for i in range(b2x // 2 + 4):
        wide_tile = z_repeat(v3[base3 - 2 + i])
        for j in range(2):
            a = base - 4 + 2 * i + j
            v2[a, 0:8, :] = v2[a, 0:8, :] + y_repeat(wide_tile)
            v2[a, 8:16, :] = v2[a, 8:16, :] + y_repeat(wide_tile, 4)
    sweep((v2,), (u2,), (r2,), ops2, base - 3, b2x + 6, b2x + 6)
    sweep((u2,), (v2,), (r2,), ops2, base - 2, b2x + 4, b2x + 4)

    def v1_landed(side):
        view = tok.at[0 : 10]
        pltpu.make_async_copy(view, view, v1r.at[side]).wait()

    each(v1_landed, range(2))
    for side, a in enumerate((H1 - 3, H1 + b1x)):
        v1[:, a : a + 3, own_y] = h1[side]
        v1_corners(side, v1, r1, hc, True)
    rows2 = v2.shape[1]
    full_y = 2 * rows2
    for i in range(b2x + 4):
        f1p[i, 0:b1y, :] = jnp.zeros((b1y, z1), F32)
        f1p[i, b1y + full_y : 2 * b1y + full_y, :] = jnp.zeros((b1y, z1), F32)
        for j in range(rows2 // 8):
            e = v2[base - 2 + i, 8 * j : 8 * j + 8, :]
            part = z_repeat(shift(e, z2, 1) - ratio * e)
            f1p[i, pl.ds(b1y + 16 * j, 8, stride=2), :] = part
            f1p[i, pl.ds(b1y + 16 * j + 1, 8, stride=2), :] = part
    window = pl.ds(pl.multiple_of(ino * b1y, 8), 3 * b1y)
    for x in range(-3, b1x + 3):
        a = H1 + x
        u1[0, a] = v1[1, a] - ratio * v1[0, a] + f1p[x // 2 + 2, window, :]
        if -2 <= x < b1x + 2:
            w1[a] = r1[1, a] - ratio * r1[0, a]
    sweep((u1.at[0],), (u1.at[1],), (w1,), ops1, H1 - 2, b1x + 4, b1x + 4)
    sweep((u1.at[1],), (u1.at[0],), (w1,), ops1, H1 - 1, b1x + 2, b1x + 2)

    each(v0_landed, range(4))
    for side, (x_far, x_near) in enumerate(((H0 - 2, H0 - 1), (H0 + bx + 1, H0 + bx))):
        for v, ref in enumerate((vs0, vc0)):
            ref[x_far, H0 : H0 + by, :] = hx[side, v, 0:by, :]
            ref[x_near, H0 - 1 : H0, :] = hx[side, v, by : by + 1, :]
            ref[x_near, H0 + by : H0 + by + 1, :] = hx[side, v, by + 1 : by + 2, :]
    for side, col in enumerate((H0 - 2, H0 + by + 1)):
        for v, ref in enumerate((vs0, vc0)):
            ref[H0 : H0 + bx, col, :] = hy[side, v]
    ratio0 = jnp.concatenate([ratio] * (nz // 128), axis=1)

    def up0(g):
        tiles = [[u1[0, H1 - 1 + 2 * g + k, 8 * j : 8 * j + 8, :] for j in range(3)] for k in range(2)]
        sub = iota(TILE, 0)
        ends = [top_bottom(jnp.where(sub < 2, shift(t[0], 2, 0), shift(t[2], 2, 0)), 0.0) for t in tiles]
        ends = top_bottom(ends[0], shift(ends[1], 4, 0))
        halves = [[z_repeat(t, start) for t in (ends, tiles[0][1], tiles[1][1])] for start in (0, 64)]
        for k in range(2):
            adds = []
            for end, mid in ((h[0], h[1 + k]) for h in halves):
                end = shift(end, -4 * k, 0) if k else end
                adds.append((top_bottom(y_repeat(end), y_repeat(mid, -2)), y_repeat(mid, 2),
                             top_bottom(y_repeat(mid, 6), y_repeat(end))))
            add = jnp.concatenate([jnp.concatenate([adds[0][j], adds[1][j]], axis=1) for j in range(3)], axis=0)
            for i in range(2):
                a = H0 - 2 + 4 * g + 2 * k + i
                us0[a] = vc0[a] - ratio0 * vs0[a] + add
                rc0[a] = rc0[a] - ratio0 * rs0[a]

    slabs(0, b1x // 2 + 1, b1x // 2 + 1, up0)
    sweep((us0,), (uc0,), (rc0,), ops0, H0 - 1, bx + 2, bx + 2)

    def last(a):
        own, t = neighbours(uc0, a, cx0, cy0, cz0)
        out_ref[a - H0] = (KEEP * own + rd0[a] * (rc0[a] + t))[H0 : H0 + by]

    slabs(H0, bx, bx, last)

    def sent(side):
        dx, dy = SIDES[side]
        if dy == 0:
            tiles = 6 * by * nz // 1024 + 3 + 4 + 2 * (by + 8) * nz // 1024 + 10
        elif dx == 0:
            tiles = 7 * bx * nz // 1024 + b1x + b1x + 2 * bx * nz // 1024
        else:
            tiles = 3
        view = tok.at[0:tiles]
        pltpu.make_async_copy(view, view, ss.at[side]).wait()

    each(sent)
    for i, view in enumerate((gm.at[0, 0 : nb - 1], gm.at[0], gr.at[0, 0 : nb - 1], gr.at[0], gp)):
        pltpu.make_async_copy(view, view, gs.at[i]).wait()


def solution(mesh):
    nw, nn = mesh.shape["wide"], mesh.shape["narrow"]

    def per_device(mobility, sav_vector, cotangent):
        bx, by, nz = mobility.shape
        b1x, b1y, z1 = bx // 2, by // 2, nz // 2
        x2, y2 = nw * bx // 4, nn * by // 4
        own = (bx, by, nz)
        l0 = (bx + 2 * H0, by + 2 * H0, nz)
        l1 = (b1x + 2 * H1, 3 * b1y, z1)
        l2 = (x2 + 2 * PAD2, y2, z1)
        l3 = (x2 // 2 + 2 * PAD2, y2 // 2, z1)
        l4 = (x2 // 4 + 2 * PAD, 8, z1)
        own2 = (bx // 4 * (by // 4), z1)
        half2 = (bx // 4 * (by // 4) // 2, z1)
        buffers = (
            [own] * 3 + [l0] * 12
            + [(2, 4, by, nz), (2, 7, bx, nz), (2, 7, bx, nz), (4, 5, 1, nz), (4, 5, 1, nz)]
            + [(2, 2, by + 8, nz)] * 2 + [(2, 2, bx, nz)] * 2 + [(2, 2, by, nz)] * 2
            + [(1, *l1)] + [l1] * 5 + [(2, *l1)] * 3 + [l1] + [(2, 2, 3, b1y, z1), (2, 2, 2, b1y, z1), (2, 2, 2, b1y, z1), (4, *TILE), (4, *TILE), (4, 6, 1, z1), (4, 6, 1, z1), (2, b1x, *TILE), (2, b1x, *TILE)]
            + [l2] * 7 + [l2 if nw <= 16 else (1, *TILE)] + [l3] * 8 + [l4] * 7
            + [(2, 2, b1x * l0[1], nz // 2)]
            + [half2, own2, (1, 128), (2, nn // 2 * nw, *half2), (2, nn // 2 * nw, *own2), (nn // 2 * nw, 1, 128), (1, 128), (1, 128)]
            + [(bx // 4 + 4, 2 * y2 + 2 * b1y, z1), (3 * bx * by * nz // 1024, *TILE)]
        )
        size = sum(4 * functools.reduce(lambda p, q: p * q, shape) for shape in buffers)
        dma = lambda n: pltpu.SemaphoreType.DMA((n,))
        scratch = [pltpu.VMEM(shape, F32) for shape in buffers]
        scratch += [dma(n) for n in (1, 8, 5, 6, 6, 4, 8, 8, 4, 2, 2)]
        steps = (nn // 2 * nw - 1).bit_length()
        scratch.append(pltpu.SemaphoreType.REGULAR((steps,)))
        return pl.pallas_call(
            functools.partial(kernel, nw, nn, bx, by, nz),
            out_shape=jax.ShapeDtypeStruct((bx, by, nz), F32),
            in_specs=[pl.BlockSpec(memory_space=pltpu.HBM)] * 3,
            out_specs=pl.BlockSpec(memory_space=pltpu.VMEM),
            scratch_shapes=scratch,
            compiler_params=pltpu.CompilerParams(
                collective_id=0, has_side_effects=True, vmem_limit_bytes=GRANT if size < GRANT else 67043328
            ),
        )(mobility, sav_vector, cotangent)

    spec = P("wide", "narrow", None)
    return jax.shard_map(per_device, mesh=mesh, in_specs=(spec,) * 3, out_specs=spec, check_vma=False)
```

```python
import functools
import jax
import jax.numpy as jnp
from jax import lax
from jax.experimental import pallas as pl
from jax.experimental.pallas import tpu as pltpu
from jax.sharding import PartitionSpec as P

DAMPING = 0.8
KEEP = 1.0 - DAMPING
BASE_TAU = 16.0
H0 = 4
H1 = 4
PAD = 2
PAD2 = 4
GRANT = 56200000
MESH = pl.DeviceIdType.MESH
F32 = jnp.float32
SIDES = [(-1, 0), (1, 0), (0, -1), (0, 1), (-1, -1), (-1, 1), (1, -1), (1, 1)]
OPPOSITE = [1, 0, 3, 2, 7, 6, 5, 4]
TILE = (8, 128)


def iota(shape, dim):
    return lax.broadcasted_iota(jnp.int32, shape, dim)


def shift(value, amount, axis):
    return pltpu.roll(value, amount % value.shape[axis], axis)


def take(value, index, axis):
    return jnp.take_along_axis(value, index, axis=axis, mode="promise_in_bounds")


def z_pairs(tile):
    return take(tile + shift(tile, -1, 1), lax.rem(2 * iota(TILE, 1), 128), 1)


def put_halves(ref, v, at, value):
    for h in range(2):
        ref[v, h, at, :] = value[:, 128 * h : 128 * h + 128]


def yz_pairs(ref, v, at):
    halves = []
    for h in range(2):
        halves.append(z_pairs(ref[v, h, pl.ds(at, 8, stride=2), :] + ref[v, h, pl.ds(at + 1, 8, stride=2), :]))
    return jnp.where(iota(TILE, 1) < 64, halves[0], halves[1])


def z_repeat(tile, start=0):
    return take(tile, start + iota(TILE, 1) // 2, 1)


def y_pairs(tile):
    return take(tile + shift(tile, -1, 0), lax.rem(2 * iota(TILE, 0), 8), 0)


def y_repeat(tile, start=0):
    return take(tile, jnp.clip(start + iota(TILE, 0) // 2, 0, 7), 0)


def top_bottom(top, bottom):
    return jnp.where(iota(TILE, 0) < 4, top, bottom)


def rounded(x):
    return x.astype(jnp.bfloat16).astype(F32)


def loop(count, chunk, body, carry):
    if count <= chunk:
        for i in range(count):
            carry = body(i, carry)
        return carry

    def step(g, carry):
        for k in range(chunk):
            carry = body(g * chunk + k, carry)
        return carry

    return lax.fori_loop(0, count // chunk, step, carry)


def slabs(lo, count, chunk, body):
    if count <= chunk:
        for k in range(count):
            body(lo + k)
        return

    def step(i, _):
        for k in range(chunk):
            body(lo + i * chunk + k)
        return 0

    lax.fori_loop(0, count // chunk, step, 0)


def build(m, cx, cy, cz, rd, d, lo, count, tau, seg, chunk, firsts=()):
    shape = m.shape[1:]
    row = iota(shape, 0)
    lane = lax.rem(iota(shape, 1), seg)
    last_row, first_row = row == shape[0] - 1, row == 0
    last_lane, first_lane = lane == seg - 1, lane == 0
    half = 0.5 * tau

    def body(a):
        own = m[a]
        xp, xm = m[a + 1], m[a - 1]
        yp = jnp.where(last_row, 0.0, shift(own, -1, 0))
        ym = jnp.where(first_row, 0.0, shift(own, 1, 0))
        zp = jnp.where(last_lane, 0.0, shift(own, -1, 1))
        zm = jnp.where(first_lane, 0.0, shift(own, 1, 1))
        total = 1.0
        for other, ref in ((xp, cx), (xm, None), (yp, cy), (ym, None), (zp, cz), (zm, None)):
            face = rounded(half * (own + other))
            total = total + face
            if ref is not None:
                ref[a] = jnp.where(jnp.minimum(own, other) > 0.0, face, 0.0)
        inverse = DAMPING / total
        rd[a] = inverse
        if d is not None:
            d[a] = total
        for r, u in firsts:
            u[a] = inverse * r[a]

    slabs(lo, count, chunk, body)


def neighbours(v, a, cx, cy, cz):
    own = v[a]
    cya, cza = cy[a], cz[a]
    total = cx[a] * v[a + 1] + cx[a - 1] * v[a - 1]
    total = total + (cya * shift(own, -1, 0) + shift(cya * own, 1, 0))
    total = total + (cza * shift(own, -1, 1) + shift(cza * own, 1, 1))
    return own, total


def sweep(vin, vout, r, ops, lo, count, chunk):
    cx, cy, cz, rd, d = ops

    def body(a):
        for vi, vo, ri in zip(vin, vout, r):
            own, t = neighbours(vi, a, cx, cy, cz)
            vo[a] = KEEP * own + rd[a] * (ri[a] + t)

    slabs(lo, count, chunk, body)


def residual(vi, ri, a, ops):
    cx, cy, cz, rd, d = ops
    own, t = neighbours(vi, a, cx, cy, cz)
    diag = d[a] if d is not None else DAMPING / rd[a]
    return own, ri[a] + t - diag * own


def fold(x):
    total = None
    for i in range(x.shape[0] // 8):
        for j in range(x.shape[1] // 128):
            part = x[8 * i : 8 * i + 8, 128 * j : 128 * j + 128]
            total = part if total is None else total + part
    return total


def fold_own(x):
    total = None
    for j in range(x.shape[1] // 128):
        lanes = slice(128 * j, 128 * j + 128)
        part = x[8:16, lanes] + top_bottom(x[16:24, lanes], x[0:8, lanes])
        total = part if total is None else total + part
    return total


def kernel(nw, nn, bx, by, nz, m_hbm, s_hbm, c_hbm, out_ref,
           m_ref, s_ref, c_ref,
           m0, cx0, cy0, cz0, rd0, d0, rs0, rc0, us0, uc0, vs0, vc0,
           rx, yp, ry, cp, rcn, xv, hx, yv, hy, xu, hu,
           m1, cx1, cy1, cz1, rd1, d1, r1, u1, v1, w1, h1, hc, cv1, cs1, cr1, cs2, cr2, qs1, qr1,
           cx2, cy2, cz2, rd2, r2, u2, v2, d2,
           cx3, cy3, cz3, rd3, r3, u3, v3, d3,
           cx4, cy4, cz4, rd4, r4, u4, v4,
           t0, sm2, sr2, sp2, gm, gr, gp, f1p, tok,
           ins, ss, gs, gq, e0r, y0r, m1r, r1r, u0r, mr):
    iw, ino = lax.axis_index("wide"), lax.axis_index("narrow")
    b1x, b1y, z1 = bx // 2, by // 2, nz // 2
    b2x, b2y, z2 = bx // 4, by // 4, nz // 4
    x2, x3, x4 = nw * b2x, nw * b2x // 2, nw * b2x // 4
    there = []
    for dx, dy in SIDES:
        ok = None
        for cond, on in ((iw > 0, dx < 0), (iw < nw - 1, dx > 0), (ino > 0, dy < 0), (ino < nn - 1, dy > 0)):
            if on:
                ok = cond if ok is None else jnp.logical_and(ok, cond)
        there.append(ok)

    def peer(side):
        return (iw + SIDES[side][0], ino + SIDES[side][1])

    inputs = [pltpu.make_async_copy(src, dst, ins.at[0])
              for src, dst in ((m_hbm, m_ref), (s_hbm, s_ref), (c_hbm, c_ref))]
    for copy in inputs:
        copy.start()

    def clear(ref, index):
        ref[index] = jnp.zeros(ref[index].shape, F32)

    barrier = pltpu.get_barrier_semaphore()

    nb = nn // 2 * nw
    me, odd = ino // 2 * nw + iw, lax.rem(ino, 2)
    twin = ino + 1 - 2 * odd

    def fellow(j):
        to = me + j
        to = jnp.where(to >= nb, to - nb, to)
        row = to // nw
        return to - row * nw, 2 * row + odd

    def over_fellows(fn):
        if nb <= 16:
            for j in range(1, nb):
                fn(j)
        else:
            def step(j, _):
                fn(j)
                return 0

            lax.fori_loop(1, nb, step, 0)

    rounds = []
    while 1 << len(rounds) < nb:
        rounds.append(1 << len(rounds))

    def partner(d):
        to = me + d - 2 * d * lax.rem(me // d, 2)
        row = to // nw
        return to - row * nw, 2 * row + odd

    for d in rounds[1:]:
        pl.semaphore_signal(barrier, inc=1, device_id=partner(d), device_id_type=MESH)
    for k in range(8):
        @pl.when(there[k])
        def _():
            pl.semaphore_signal(barrier, inc=1, device_id=peer(k), device_id_type=MESH)

    def meet(n):
        if n > 0:
            pl.semaphore_wait(mr.at[n - 1], 1)
        if n <= len(rounds):
            to = partner(rounds[n]) if n < len(rounds) else (iw, twin)
            pl.semaphore_signal(mr.at[n], inc=1, device_id=to, device_id_type=MESH)

    beside_x = jnp.minimum(iw, 1) + jnp.minimum(nw - 1 - iw, 1)
    beside_y = jnp.minimum(ino, 1) + jnp.minimum(nn - 1 - ino, 1)
    pl.semaphore_wait(barrier, len(rounds) - 1 + beside_x + beside_y + beside_x * beside_y)

    def remote(src, dst, ssem, rsem, dev):
        return pltpu.make_async_remote_copy(src_ref=src, dst_ref=dst, send_sem=ssem, recv_sem=rsem,
                                            device_id=dev, device_id_type=MESH)

    def to_side(side, pairs, rsem):
        land = OPPOSITE[side]
        if rsem is e0r and land > 3:
            land -= 2
        return [remote(src, dst, ss.at[side], rsem.at[land], peer(side)) for src, dst in pairs]

    def e0_sends(side):
        land = OPPOSITE[side]
        if side < 2:
            pairs = []
            at = 0
            for ref, width in ((m_hbm, 2), (s_hbm, 1), (c_hbm, 1)):
                lo = 0 if side == 0 else bx - width
                pairs.append((ref.at[lo : lo + width], rx.at[land, at : at + width]))
                at += width
            return to_side(side, pairs, e0r)
        return to_side(side, [(cp.at[side - 4], rcn.at[land - 4])], e0r)

    def y0_sends(side, lo, hi, sem):
        land = OPPOSITE[side] - 2
        return [remote(yp.at[side - 2, lo:hi], ry.at[land, lo:hi], ss.at[side], y0r.at[sem + land], peer(side))]

    def each(fn, sides=range(8)):
        for side in sides:
            @pl.when(there[side])
            def _():
                fn(side)

    def start(copies):
        for copy in copies:
            copy.start()

    each(lambda k: start(e0_sends(k)), (0, 1))
    meet(0)
    view = tok.at[0 : 3 * bx * by * nz // 1024]
    pltpu.make_async_copy(view, view, ins.at[0]).wait()
    def yp_fill(side, at, ref, k):
        yp[side, at] = ref[:, by - 1 - k if side else k, :]

    for side in range(2):
        yp_fill(side, 0, m_ref, 0)
    each(lambda k: start(y0_sends(k, 0, 1, 0)), (2, 3))
    for side in range(2):
        for at, (ref, k) in enumerate(((m_ref, 1), (m_ref, 2), (s_ref, 0), (s_ref, 1), (c_ref, 0), (c_ref, 1))):
            yp_fill(side, 1 + at, ref, k)
    each(lambda k: start(y0_sends(k, 1, 7, 2)), (2, 3))
    for k in range(4, 8):
        dx, dy = SIDES[k]
        xa, xb = (0, 1) if dx < 0 else (bx - 1, bx - 2)
        ya, yb = (0, 1) if dy < 0 else (by - 1, by - 2)
        for i, (ref, x, y) in enumerate(((m_ref, xa, ya), (m_ref, xa, yb), (m_ref, xb, ya),
                                         (s_ref, xa, ya), (c_ref, xa, ya))):
            cp[k - 4, i] = ref[x, y : y + 1, :]

    each(lambda k: start(e0_sends(k)), (4, 5, 6, 7))

    near1 = ((1, 1), (1, 2), (1, 3), (2, 1), (2, 2), (3, 1))
    near_m1 = near1 + ((2, 3), (1, 4))

    def inside1(side, i, j):
        dx, dy = SIDES[side]
        return H1 + i - 1 if dx < 0 else H1 + b1x - i, b1y + j - 1 if dy < 0 else 2 * b1y - j

    def outside1(side, i, j):
        dx, dy = SIDES[side]
        return H1 - i if dx < 0 else H1 + b1x + i - 1, b1y - j if dy < 0 else 2 * b1y + j - 1

    def box1(side, sending, width):
        dx, dy = SIDES[side]
        w = width
        if sending:
            xlo, w = (H1, w) if dx < 0 else ((H1 + b1x - w, w) if dx > 0 else (H1, b1x))
            ylo = b1y
        else:
            xlo, w = (H1 - w, w) if dx < 0 else ((H1 + b1x, w) if dx > 0 else (H1, b1x))
            ylo = b1y * (1 + dy)
        return xlo, w, ylo

    def level1_sends(ref, rsem, side, width, kc):
        if side > 3:
            src, dst = (cs2, cr2) if kc else (cs1, cr1)
            return to_side(side, [(src.at[side - 4], dst.at[OPPOSITE[side] - 4])], rsem)
        if kc and side > 1:
            return to_side(side, [(qs1.at[side - 2], qr1.at[OPPOSITE[side] - 2])], rsem)
        sx, w, sy = box1(side, True, width)
        tx, _, ty = box1(OPPOSITE[side], False, width)
        return to_side(side, [(ref.at[:, sx : sx + w, sy : sy + b1y], ref.at[:, tx : tx + w, ty : ty + b1y])], rsem)

    def r1_pack(side):
        for x in range(b1x):
            rs, rc = r1[0, H1 + x, own_y, :], r1[1, H1 + x, own_y, :]
            qs1[side - 2, x] = top_bottom(rs, shift(rc, 4, 0)) if side == 2 else top_bottom(shift(rs, 4, 0), rc)

    def r1_unpack(side):
        rows = side_rows[side - 2]
        for x in range(b1x):
            tile = qr1[side - 2, x]
            other = shift(tile, 4, 0)
            r1[0, H1 + x, rows, :] = other if side == 2 else tile
            r1[1, H1 + x, rows, :] = tile if side == 2 else other

    def level1_landed(ref, rsem, width, kc):
        def fn(side):
            if side > 3:
                view = (cr2 if kc else cr1).at[side - 4]
            elif kc and side > 1:
                view = qr1.at[side - 2]
            else:
                tx, w, ty = box1(side, False, width)
                view = ref.at[:, tx : tx + w, ty : ty + b1y]
            pltpu.make_async_copy(view, view, rsem.at[side]).wait()
        return fn

    def e0_landed(side):
        if side in (2, 3):
            view = ry.at[side - 2, 1:7]
            pltpu.make_async_copy(view, view, y0r.at[side]).wait()
        else:
            view = rx.at[side] if side < 2 else rcn.at[side - 4]
            pltpu.make_async_copy(view, view, e0r.at[side if side < 2 else side - 2]).wait()

    def near_landed(side):
        view = ry.at[side - 2, 0:1]
        pltpu.make_async_copy(view, view, y0r.at[side - 2]).wait()

    own_y = slice(b1y, 2 * b1y)
    for i in range(b1x):
        put_halves(t0, 0, slice(i * by, (i + 1) * by), m_ref[2 * i] + m_ref[2 * i + 1])
    for i in range(b1x):
        m1[0, H1 + i, own_y, :] = 0.125 * yz_pairs(t0, 0, i * by)
    for k in range(4, 8):
        for n, (i, j) in enumerate(near_m1):
            x, y = inside1(k, i, j)
            cs1[k - 4, n : n + 1, :] = m1[0, x, y : y + 1, :]
    low2 = iota(TILE, 1) < z2
    for i in range(0, b2x, 4):
        tiles = []
        for n in range(i, i + 4, 2):
            quads = [y_pairs(m1[0, H1 + 2 * k, own_y, :] + m1[0, H1 + 2 * k + 1, own_y, :]) for k in (n, n + 1)]
            tiles.append(0.125 * z_pairs(top_bottom(quads[0], quads[1])))
        mob2 = jnp.where(low2, tiles[0], tiles[1])
        sm2[2 * i : 2 * i + 8, :] = mob2
        gm[odd, me, 2 * i : 2 * i + 8, :] = mob2

    def send_sem(kind):
        return gs.at[gs.shape[0] - 1 if kind > 3 else min(kind, gs.shape[0] - 2)]

    def to_fellows(src, dst, kind):
        over_fellows(lambda j: remote(src, dst, send_sem(kind), gq.at[kind], fellow(j)).start())

    def to_twin(src, dst, kind):
        remote(src, dst, send_sem(kind), gq.at[kind], (iw, twin)).start()

    def to_others(src, dst, kind):
        def to_one(j):
            to = me + j
            to = jnp.where(to >= nb, to - nb, to)
            row = to // nw
            remote(src, dst, send_sem(kind), gq.at[kind], (to - row * nw, 2 * row + 1 - odd)).start()

        if nb <= 16:
            for j in range(nb):
                to_one(j)
        else:
            def step(j, _):
                to_one(j)
                return 0

            lax.fori_loop(0, nb, step, 0)

    def landed(view, kind):
        pltpu.make_async_copy(view, view, gq.at[kind]).wait()

    for ref, src, width in ((m0, m_ref, 2), (rs0, s_ref, 1), (rc0, c_ref, 1)):
        blank = jnp.zeros(m0.shape[1:], F32)
        for i in range(width):
            ref[H0 - 1 - i] = blank
            ref[H0 + bx + i] = blank

        def put(i):
            ref[H0 + i, H0 : H0 + by, :] = src[i]

        slabs(0, bx, bx, put)
    side_rows = (slice(0, b1y), slice(2 * b1y, 3 * b1y))
    for k in range(8):
        @pl.when(jnp.logical_not(there[k]))
        def _():
            if k > 3:
                clear(rcn, k - 4)
                clear(cr1, k - 4)
                clear(cr2, k - 4)
                return
            lands = ((rx, hx, hu, h1, hc) if k < 2 else (ry, hy, qr1))
            for ref in lands:
                clear(ref, k % 2)
            for ref, width in (((m1, 3), (r1, 2)) if k < 2 else ((m1, 3),)):
                xlo, w, ylo = box1(k, False, width)
                clear(ref, (slice(None), slice(xlo, xlo + w), slice(ylo, ylo + b1y)))
    for a in (0, H1 + b1x + 3):
        clear(m1, (0, a))
    for a in (1, 2, 3, H1 + b1x, H1 + b1x + 1, H1 + b1x + 2):
        for rows in side_rows:
            clear(m1, (0, a, rows))
            for v in range(2):
                clear(r1, (v, a, rows))
    for ref in (us0, uc0):
        ref[H0 - 2] = jnp.zeros(m0.shape[1:], F32)
        ref[H0 + bx + 1] = jnp.zeros(m0.shape[1:], F32)
    for a in (0, 1, 2, 3, H1 + b1x, H1 + b1x + 1, H1 + b1x + 2, H1 + b1x + 3):
        for v in range(2):
            v1[v, a] = jnp.zeros(v1.shape[2:], F32)
    for ref in (u4, v4):
        zero = jnp.zeros(ref.shape[1:], F32)
        for a in (0, 1, ref.shape[0] - 2, ref.shape[0] - 1):
            ref[a] = zero
    for ref in (u2, v2, r2, cx2, cy2, cz2, rd2, u3, v3, r3, cx3, cy3, cz3, rd3):
        zero = jnp.zeros(ref.shape[1:], F32)
        for a in range(PAD2):
            ref[a] = zero
            ref[ref.shape[0] - 1 - a] = zero
    cx4[PAD - 1] = jnp.zeros(cx4.shape[1:], F32)

    ops0 = (cx0, cy0, cz0, rd0, d0)
    firsts0 = ((rs0, us0), (rc0, uc0))
    meet(1)
    each(near_landed, (2, 3))
    m0[H0 : H0 + bx, H0 - 1, :] = ry[0, 0]
    m0[H0 : H0 + bx, H0 + by, :] = ry[1, 0]
    for side, a in enumerate((H0 + 1, H0 + bx - 2)):
        build(m0, cx0, cy0, cz0, rd0, d0, a, 1, BASE_TAU, nz, 1, firsts0)
        for v, ref in enumerate((us0, uc0)):
            xu[side, v] = ref[a, H0 : H0 + by, :]
    each(lambda k: start(to_side(k, [(xu.at[k], hu.at[OPPOSITE[k]])], u0r)), (0, 1))
    each(lambda k: start(level1_sends(m1, m1r, k, 3, 0)))
    each(e0_landed, (2, 3))
    for ref, at, lo, width in ((m0, 1, 1, 2), (rs0, 3, 0, 2), (rc0, 5, 0, 2)):
        for i in range(width):
            ref[H0 : H0 + bx, H0 - 1 - lo - i, :] = ry[0, at + i]
            ref[H0 : H0 + bx, H0 + by + lo + i, :] = ry[1, at + i]

    meet(2)
    build(m0, cx0, cy0, cz0, rd0, d0, H0 + 1, bx - 2, BASE_TAU, nz, bx - 2, firsts0)
    sweep((us0, uc0), (vs0, vc0), (rs0, rc0), ops0, H0 + 2, bx - 4, bx - 4)

    def down0(i, carry):
        num, den = carry
        sums = []
        for k in range(2):
            a = H0 + 2 * i + k
            vs, es = residual(vs0, rs0, a, ops0)
            vc, ec = residual(vc0, rc0, a, ops0)
            both = es + rs0[a]
            num = num + fold_own(both * vc)
            den = den + fold_own(both * vs)
            sums.append((es, ec))
        at = slice(i * m0.shape[1], (i + 1) * m0.shape[1])
        put_halves(t0, 0, at, sums[0][0] + sums[1][0])
        put_halves(t0, 1, at, sums[0][1] + sums[1][1])
        return num, den

    zero8 = jnp.zeros(TILE, F32)
    part0 = loop(b1x - 4, b1x - 4, lambda i, c: down0(2 + i, c), (zero8, zero8))


    def coarse0(i):
        for v in range(2):
            r1[v, H1 + i, own_y, :] = 0.125 * yz_pairs(t0, v, i * m0.shape[1] + H0)

    slabs(2, b1x - 4, b1x - 4, coarse0)
    meet(3)
    def u0_landed(side):
        pltpu.make_async_copy(hu.at[side], hu.at[side], u0r.at[side]).wait()

    each(e0_landed, (0, 1, 4, 5, 6, 7))
    for n in range(4, len(rounds) + 1):
        meet(n)
    to_fellows(sm2, gm.at[odd, me], 0)
    for ref, at, width in ((m0, 0, 2), (rs0, 2, 1), (rc0, 3, 1)):
        for i in range(width):
            ref[H0 - width + i, H0 : H0 + by, :] = rx[0, at + i]
            ref[H0 + bx + i, H0 : H0 + by, :] = rx[1, at + i]
    for k in range(4):
        dx, dy = SIDES[4 + k]
        xa, xb = (H0 - 1, H0 - 2) if dx < 0 else (H0 + bx, H0 + bx + 1)
        ya, yb = (H0 - 1, H0 - 2) if dy < 0 else (H0 + by, H0 + by + 1)
        for i, (ref, x, y) in enumerate(((m0, xa, ya), (m0, xa, yb), (m0, xb, ya), (rs0, xa, ya), (rc0, xa, ya))):
            ref[x, y : y + 1, :] = rcn[k, i]
    beyond = m0[H0 - 2]
    own = m0[H0 - 1]
    cx0[H0 - 2] = jnp.where(jnp.minimum(own, beyond) > 0.0, rounded(0.5 * BASE_TAU * (own + beyond)), 0.0)
    for lo in (H0 - 1, H0 + bx - 1):
        build(m0, cx0, cy0, cz0, rd0, d0, lo, 2, BASE_TAU, nz, 2, firsts0)
    each(u0_landed, (0, 1))
    for v, ref in enumerate((us0, uc0)):
        ref[H0 - 2, H0 : H0 + by, :] = hu[0, v]
        ref[H0 + bx + 1, H0 : H0 + by, :] = hu[1, v]
    for v_lo in (H0 - 1, H0 + bx - 2):
        sweep((us0, uc0), (vs0, vc0), (rs0, rc0), ops0, v_lo, 3, 3)
    num0, den0 = loop(2, 2, lambda i, c: down0(b1x - 2 + i, down0(i, c)), part0)
    for i in (0, 1, b1x - 2, b1x - 1):
        coarse0(i)
    for k in range(4, 8):
        for n in range(6):
            x, y = inside1(k, 1, 1 + n // 2)
            cs2[k - 4, n] = r1[n % 2, x, y : y + 1, :]
    for k in (2, 3):
        r1_pack(k)
    each(lambda k: start(level1_sends(r1, r1r, k, 2, 1)), (4, 5, 6, 7, 0, 1, 2, 3))
    for side, (x_far, x_near) in enumerate(((H0 + 1, H0), (H0 + bx - 2, H0 + bx - 1))):
        for v, ref in enumerate((vs0, vc0)):
            xv[side, v, 0:by, :] = ref[x_far, H0 : H0 + by, :]
            xv[side, v, by : by + 1, :] = ref[x_near, H0 - 1 : H0, :]
            xv[side, v, by + 1 : by + 2, :] = ref[x_near, H0 + by : H0 + by + 1, :]
    for side, col in enumerate((H0 + 1, H0 + by - 2)):
        for v, ref in enumerate((vs0, vc0)):
            yv[side, v] = ref[H0 : H0 + bx, col, :]

    def v0_sends(side):
        land = OPPOSITE[side]
        src, dst = (xv.at[side], hx.at[land]) if side < 2 else (yv.at[side - 2], hy.at[land - 2])
        if side < 2:
            return to_side(side, [(src, dst)], e0r)
        return [remote(src, dst, ss.at[side], y0r.at[land], peer(side))]

    each(level1_landed(m1, m1r, 3, 0))
    for k in range(4, 8):
        for n, (i, j) in enumerate(near_m1):
            x, y = outside1(k, i, j)
            m1[0, x, y : y + 1, :] = cr1[k - 4, n : n + 1, :]
    ops1 = (cx1, cy1, cz1, rd1, d1)
    build(m1.at[0], cx1, cy1, cz1, rd1, d1, H1 - 3, b1x + 6, BASE_TAU / 4, z1, b1x + 6)
    rr1 = (r1.at[0], r1.at[1])
    uu1 = (u1.at[0], u1.at[1])
    vv1 = (v1.at[0], v1.at[1])
    halves1 = {}

    def first1(a):
        for v in range(2):
            u1[v, a] = rd1[a] * r1[v, a]

    def down1(i, carry):
        num, den = carry
        pair = []
        for k in range(2):
            a = H1 + 2 * i + k
            vs, es = residual(vv1[0], rr1[0], a, ops1)
            vc, ec = residual(vv1[1], rr1[1], a, ops1)
            both = (es + r1[0, a])[own_y]
            num = num + both * vc[own_y]
            den = den + both * vs[own_y]
            pair.append((es[own_y], ec[own_y]))
        halves1[i] = [y_pairs(pair[0][v] + pair[1][v]) for v in range(2)]
        return num, den

    landed1 = level1_landed(r1, r1r, 2, 1)
    each(landed1, (2, 3))
    for k in (2, 3):
        r1_unpack(k)
    slabs(H1, b1x, b1x, first1)
    sweep(uu1, vv1, rr1, ops1, H1 + 1, b1x - 2, b1x - 2)
    sums1 = loop(b2x - 2, b2x - 2, lambda i, c: down1(1 + i, c), (zero8, zero8))
    each(landed1, (0, 1, 4, 5, 6, 7))
    for k in range(4, 8):
        for n in range(6):
            x, y = outside1(k, 1, 1 + n // 2)
            r1[n % 2, x, y : y + 1, :] = cr2[k - 4, n]
    for a in (H1 - 2, H1 + b1x):
        slabs(a, 2, 2, first1)
    for a in (H1 - 1, H1 + b1x - 1):
        sweep(uu1, vv1, rr1, ops1, a, 2, 2)
    num1, den1 = down1(b2x - 1, down1(0, sums1))
    for i in range(0, b2x, 2):
        packed = [z_pairs(top_bottom(halves1[i][v], halves1[i + 1][v])) for v in range(2)]
        own2 = 0.125 * jnp.where(low2, packed[0], packed[1])
        sr2[i * b2y : (i + 2) * b2y, :] = own2
        gr[odd, me, i * b2y : (i + 2) * b2y, :] = own2
    meet(len(rounds) + 1)
    to_fellows(sr2, gr.at[odd, me], 2)
    num_row = jnp.sum(num0 + 8.0 * num1, axis=0, keepdims=True)
    den_row = jnp.sum(den0 + 8.0 * den1, axis=0, keepdims=True)
    low1 = iota((1, 128), 1) < 64
    part = jnp.where(low1, num_row + shift(num_row, 64, 1), den_row + shift(den_row, 64, 1))
    sp2[...] = part
    mine = odd * nb + me
    gp[mine] = part
    to_fellows(sp2, gp.at[mine], 4)
    to_others(sp2, gp.at[mine], 4)

    def v1_corners(side, ref_v, ref_r, tiles, outward):
        for d in range(2):
            corner = 4 + 2 * side + d
            for n, (i, j) in enumerate(near1 + ((1, 2), (2, 1))):
                x = (outside1 if outward else inside1)(corner, i, j)[0]
                y = outside1(corner, i, j)[1]
                ref = ref_v if n < 6 else ref_r
                for v in range(2):
                    if outward:
                        ref[v, x, y : y + 1, :] = tiles[side, v, d, n : n + 1, :]
                    else:
                        tiles[side, v, d, n : n + 1, :] = ref[v, x, y : y + 1, :]

    for side in range(2):
        v1_corners(side, v1, r1, cv1, False)
    landed(gm.at[0, 0 : nb - 1], 0)
    to_twin(gm.at[odd], gm.at[odd], 1)
    landed(gm.at[0], 1)
    def v1_sends(side):
        land = OPPOSITE[side]
        lo = H1 if side == 0 else H1 + b1x - 3
        return to_side(side, [(v1.at[:, lo : lo + 3, own_y], h1.at[land]), (cv1.at[side], hc.at[land])], u0r)


    def unpack(src, dst, u=None):
        def step(w, carry):
            for i in range(b2x):
                a = PAD2 + w * b2x + i
                for n in range(nn):
                    dst[a, n * b2y : (n + 1) * b2y, :] = src[n % 2, n // 2 * nw + w, i * b2y : (i + 1) * b2y, :]
                if u is not None:
                    u[a] = rd2[a] * dst[a]
            return carry

        loop(nw, 8, step, 0)

    def unpack_m(w, carry):
        for n in range(nn):
            for i in range(0, b2x, 4):
                tile = gm[n % 2, n // 2 * nw + w, 2 * i : 2 * i + 8, :]
                other = shift(tile, z2, 1)
                for k, part in enumerate((jnp.where(low2, tile, other), jnp.where(low2, other, tile))):
                    for h in range(2):
                        a = PAD2 + w * b2x + i + 2 * k + h
                        v2[a, n * b2y : (n + 1) * b2y, :] = part[h * b2y : (h + 1) * b2y, :]
        return carry

    loop(nw, 8, unpack_m, 0)
    kept2 = d2 if d2.shape == v2.shape else None
    build(v2, cx2, cy2, cz2, rd2, kept2, PAD2, x2, BASE_TAU / 16, z2, 16)

    def coarsen_y(x):
        if x.shape[0] == 16:
            return top_bottom(y_pairs(x[0:8]), y_pairs(x[8:16]))
        return top_bottom(y_pairs(x), 0.0)

    def coarsen_z(dst, lo, count):
        def body(a):
            dst[a] = 0.125 * z_pairs(dst[a])

        slabs(lo, count, min(count, 16), body)

    def coarsen_pairs(src, dst, xc, pad):
        def body(i, carry):
            a = PAD2 + 2 * i
            dst[pad + i] = coarsen_y(src[a] + src[a + 1])
            return carry

        loop(xc, 16, body, 0)
        coarsen_z(dst, pad, xc)

    coarsen_pairs(v2, v3, x3, PAD2)
    build(v3, cx3, cy3, cz3, rd3, d3, PAD2, x3, BASE_TAU / 64, z2 // 2, 16)
    coarsen_pairs(v3, v4, x4, PAD)
    build(v4, cx4, cy4, cz4, rd4, None, PAD, x4, BASE_TAU / 256, z2 // 4, 8)

    each(lambda k: start(v1_sends(k)), range(2))
    each(lambda k: start(v0_sends(k)), range(4))
    landed(gr.at[0, 0 : nb - 1], 2)
    to_twin(gr.at[odd], gr.at[odd], 3)


    def v0_landed(side):
        view = hx.at[side] if side < 2 else hy.at[side - 2]
        pltpu.make_async_copy(view, view, e0r.at[side] if side < 2 else y0r.at[side]).wait()

    landed(gr.at[0], 3)
    unpack(gr, r2, u2)

    ops2 = (cx2, cy2, cz2, rd2, kept2)
    ops3 = (cx3, cy3, cz3, rd3, d3)
    ops4 = (cx4, cy4, cz4, rd4, None)

    def coarsen_residual(v, r, ops, dst, xc, pad, seg):
        low = iota(v.shape[1:], 1) < seg

        def step(i, carry):
            num, den = carry
            pair = []
            for j in range(2):
                a = PAD2 + 2 * i + j
                own, e = residual(v, r, a, ops)
                both = jnp.where(low, e + r[a], 0.0)
                num = num + fold(both * shift(own, -seg, 1))
                den = den + fold(both * own)
                pair.append(e)
            dst[pad + i] = coarsen_y(pair[0] + pair[1])
            return num, den

        sums = loop(xc, 16, step, (zero8, zero8))
        coarsen_z(dst, pad, xc)
        return sums

    sweep((u2,), (v2,), (r2,), ops2, PAD2, x2, 32)
    landed(gp.at[0 : 2 * nb - 1], 4)
    whole = loop(2 * nb, 32, lambda i, acc: acc + gp[i], jnp.zeros((1, 128), F32))
    num2, den2 = coarsen_residual(v2, r2, ops2, r3, x3, PAD2, z2)
    def first3(a):
        u3[a] = rd3[a] * r3[a]

    slabs(PAD2, x3, 16, first3)
    sweep((u3,), (v3,), (r3,), ops3, PAD2, x3, 16)
    num3, den3 = coarsen_residual(v3, r3, ops3, r4, x4, PAD, z2 // 2)

    def first4(a):
        u4[a] = rd4[a] * r4[a]

    slabs(PAD, x4, 8, first4)
    sweep((u4,), (v4,), (r4,), ops4, PAD, x4, 8)
    low4 = iota(TILE, 1) < z2 // 4

    def dots(i, carry):
        num, den = carry
        for k in range(8):
            a = PAD + 8 * i + k
            both = jnp.where(low4, r4[a], 0.0)
            den = den + both * v4[a]
            num = num + both * shift(v4[a], -(z2 // 4), 1)
        return num, den

    num4, den4 = dots(0, (zero8, zero8)) if x4 == 8 else lax.fori_loop(0, x4 // 8, dots, (zero8, zero8))
    b3x = b2x // 2
    base3 = PAD2 + iw * b3x
    for i in range(b3x // 2 + 4):
        add = y_repeat(z_repeat(v4[PAD + iw * (b3x // 2) - 2 + i]))
        for j in range(2):
            a = base3 - 4 + 2 * i + j
            v3[a] = v3[a] + add
    sweep((v3,), (u3,), (r3,), ops3, base3 - 3, b3x + 6, b3x + 6)
    sweep((u3,), (v3,), (r3,), ops3, base3 - 2, b3x + 4, b3x + 4)

    def total_of(mask, n2, n3, n4):
        x = jnp.sum(64.0 * n2 + 512.0 * n3 + 4096.0 * n4, axis=0, keepdims=True)
        return jnp.sum(x + jnp.where(mask, whole, 0.0), axis=1, keepdims=True)

    ratio = total_of(low1, num2, num3, num4) / (1.0 + total_of(jnp.logical_not(low1), den2, den3, den4))
    ratio = jnp.broadcast_to(ratio, (1, 128))
    base = PAD2 + iw * b2x
    for i in range(b2x // 2 + 4):
        wide_tile = z_repeat(v3[base3 - 2 + i])
        for j in range(2):
            a = base - 4 + 2 * i + j
            v2[a, 0:8, :] = v2[a, 0:8, :] + y_repeat(wide_tile)
            v2[a, 8:16, :] = v2[a, 8:16, :] + y_repeat(wide_tile, 4)
    sweep((v2,), (u2,), (r2,), ops2, base - 3, b2x + 6, b2x + 6)
    sweep((u2,), (v2,), (r2,), ops2, base - 2, b2x + 4, b2x + 4)

    def v1_landed(side):
        view = tok.at[0 : 10]
        pltpu.make_async_copy(view, view, u0r.at[side]).wait()

    each(v1_landed, range(2))
    for side, a in enumerate((H1 - 3, H1 + b1x)):
        v1[:, a : a + 3, own_y] = h1[side]
        v1_corners(side, v1, r1, hc, True)
    rows2 = v2.shape[1]
    full_y = 2 * rows2
    for i in range(b2x + 4):
        f1p[i, 0:b1y, :] = jnp.zeros((b1y, z1), F32)
        f1p[i, b1y + full_y : 2 * b1y + full_y, :] = jnp.zeros((b1y, z1), F32)
        for j in range(rows2 // 8):
            e = v2[base - 2 + i, 8 * j : 8 * j + 8, :]
            part = z_repeat(shift(e, z2, 1) - ratio * e)
            f1p[i, pl.ds(b1y + 16 * j, 8, stride=2), :] = part
            f1p[i, pl.ds(b1y + 16 * j + 1, 8, stride=2), :] = part
    window = pl.ds(pl.multiple_of(ino * b1y, 8), 3 * b1y)
    for x in range(-3, b1x + 3):
        a = H1 + x
        u1[0, a] = v1[1, a] - ratio * v1[0, a] + f1p[x // 2 + 2, window, :]
        if -2 <= x < b1x + 2:
            w1[a] = r1[1, a] - ratio * r1[0, a]
    sweep((u1.at[0],), (u1.at[1],), (w1,), ops1, H1 - 2, b1x + 4, b1x + 4)
    sweep((u1.at[1],), (u1.at[0],), (w1,), ops1, H1 - 1, b1x + 2, b1x + 2)

    each(v0_landed, range(4))
    for side, (x_far, x_near) in enumerate(((H0 - 2, H0 - 1), (H0 + bx + 1, H0 + bx))):
        for v, ref in enumerate((vs0, vc0)):
            ref[x_far, H0 : H0 + by, :] = hx[side, v, 0:by, :]
            ref[x_near, H0 - 1 : H0, :] = hx[side, v, by : by + 1, :]
            ref[x_near, H0 + by : H0 + by + 1, :] = hx[side, v, by + 1 : by + 2, :]
    for side, col in enumerate((H0 - 2, H0 + by + 1)):
        for v, ref in enumerate((vs0, vc0)):
            ref[H0 : H0 + bx, col, :] = hy[side, v]
    ratio0 = jnp.concatenate([ratio] * (nz // 128), axis=1)

    def up0(g):
        tiles = [[u1[0, H1 - 1 + 2 * g + k, 8 * j : 8 * j + 8, :] for j in range(3)] for k in range(2)]
        sub = iota(TILE, 0)
        ends = [top_bottom(jnp.where(sub < 2, shift(t[0], 2, 0), shift(t[2], 2, 0)), 0.0) for t in tiles]
        ends = top_bottom(ends[0], shift(ends[1], 4, 0))
        halves = [[z_repeat(t, start) for t in (ends, tiles[0][1], tiles[1][1])] for start in (0, 64)]
        for k in range(2):
            adds = []
            for end, mid in ((h[0], h[1 + k]) for h in halves):
                end = shift(end, -4 * k, 0) if k else end
                adds.append((top_bottom(y_repeat(end), y_repeat(mid, -2)), y_repeat(mid, 2),
                             top_bottom(y_repeat(mid, 6), y_repeat(end))))
            add = jnp.concatenate([jnp.concatenate([adds[0][j], adds[1][j]], axis=1) for j in range(3)], axis=0)
            for i in range(2):
                a = H0 - 2 + 4 * g + 2 * k + i
                us0[a] = vc0[a] - ratio0 * vs0[a] + add
                rc0[a] = rc0[a] - ratio0 * rs0[a]

    slabs(0, b1x // 2 + 1, b1x // 2 + 1, up0)
    sweep((us0,), (uc0,), (rc0,), ops0, H0 - 1, bx + 2, bx + 2)

    def last(a):
        own, t = neighbours(uc0, a, cx0, cy0, cz0)
        out_ref[a - H0] = (KEEP * own + rd0[a] * (rc0[a] + t))[H0 : H0 + by]

    slabs(H0, bx, bx, last)

    def sent(side):
        dx, dy = SIDES[side]
        if dy == 0:
            tiles = 6 * by * nz // 1024 + 3 + 4 + 2 * (by + 8) * nz // 1024 + 10
        elif dx == 0:
            tiles = 7 * bx * nz // 1024 + b1x + b1x + 2 * bx * nz // 1024
        else:
            tiles = 3
        view = tok.at[0:tiles]
        pltpu.make_async_copy(view, view, ss.at[side]).wait()

    each(sent)
    if gs.shape[0] == 2:
        views = (tok.at[0 : 3 * (nb - 1) + 3 * nb],)
    else:
        views = (gm.at[0, 0 : nb - 1], gm.at[0], gr.at[0, 0 : nb - 1], gr.at[0])
    views += (gp.at[0 : 2 * nb - 1],)
    for i, view in enumerate(views):
        pltpu.make_async_copy(view, view, gs.at[i]).wait()


def solution(mesh):
    nw, nn = mesh.shape["wide"], mesh.shape["narrow"]

    def per_device(mobility, sav_vector, cotangent):
        bx, by, nz = mobility.shape
        b1x, b1y, z1 = bx // 2, by // 2, nz // 2
        x2, y2 = nw * bx // 4, nn * by // 4
        own = (bx, by, nz)
        l0 = (bx + 2 * H0, by + 2 * H0, nz)
        l1 = (b1x + 2 * H1, 3 * b1y, z1)
        l2 = (x2 + 2 * PAD2, y2, z1)
        l3 = (x2 // 2 + 2 * PAD2, y2 // 2, z1)
        l4 = (x2 // 4 + 2 * PAD, 8, z1)
        own2 = (bx // 4 * (by // 4), z1)
        half2 = (bx // 4 * (by // 4) // 2, z1)
        buffers = (
            [own] * 3 + [l0] * 12
            + [(2, 4, by, nz), (2, 7, bx, nz), (2, 7, bx, nz), (4, 5, 1, nz), (4, 5, 1, nz)]
            + [(2, 2, by + 8, nz)] * 2 + [(2, 2, bx, nz)] * 2 + [(2, 2, by, nz)] * 2
            + [(1, *l1)] + [l1] * 5 + [(2, *l1)] * 3 + [l1] + [(2, 2, 3, b1y, z1), (2, 2, 2, b1y, z1), (2, 2, 2, b1y, z1), (4, *TILE), (4, *TILE), (4, 6, 1, z1), (4, 6, 1, z1), (2, b1x, *TILE), (2, b1x, *TILE)]
            + [l2] * 7 + [l2 if nw <= 16 else (1, *TILE)] + [l3] * 8 + [l4] * 7
            + [(2, 2, b1x * l0[1], nz // 2)]
            + [half2, own2, (1, 128), (2, nn // 2 * nw, *half2), (2, nn // 2 * nw, *own2), (nn * nw, 1, 128)]
            + [(bx // 4 + 4, 2 * y2 + 2 * b1y, z1), (3 * bx * by * nz // 1024, *TILE)]
        )
        size = sum(4 * functools.reduce(lambda p, q: p * q, shape) for shape in buffers)
        dma = lambda n: pltpu.SemaphoreType.DMA((n,))
        scratch = [pltpu.VMEM(shape, F32) for shape in buffers]
        scratch += [dma(n) for n in (1, 8, 2 if nn // 2 * nw <= 16 else 5, 5, 6, 4, 8, 8, 2)]
        steps = (nn // 2 * nw - 1).bit_length() + 1
        scratch.append(pltpu.SemaphoreType.REGULAR((steps,)))
        return pl.pallas_call(
            functools.partial(kernel, nw, nn, bx, by, nz),
            out_shape=jax.ShapeDtypeStruct((bx, by, nz), F32),
            in_specs=[pl.BlockSpec(memory_space=pltpu.HBM)] * 3,
            out_specs=pl.BlockSpec(memory_space=pltpu.VMEM),
            scratch_shapes=scratch,
            compiler_params=pltpu.CompilerParams(
                collective_id=0, has_side_effects=True, vmem_limit_bytes=GRANT if size < GRANT else 67043328
            ),
        )(mobility, sav_vector, cotangent)

    spec = P("wide", "narrow", None)
    return jax.shard_map(per_device, mesh=mesh, in_specs=(spec,) * 3, out_specs=spec, check_vma=False)
```

```python
import functools
import jax
import jax.numpy as jnp
from jax import lax
from jax.experimental import pallas as pl
from jax.experimental.pallas import tpu as pltpu
from jax.sharding import PartitionSpec as P

DAMPING = 0.8
KEEP = 1.0 - DAMPING
BASE_TAU = 16.0
H0 = 4
H1 = 4
PAD = 2
PAD2 = 4
GRANT = 56200000
MESH = pl.DeviceIdType.MESH
F32 = jnp.float32
SIDES = [(-1, 0), (1, 0), (0, -1), (0, 1), (-1, -1), (-1, 1), (1, -1), (1, 1)]
OPPOSITE = [1, 0, 3, 2, 7, 6, 5, 4]
TILE = (8, 128)


def iota(shape, dim):
    return lax.broadcasted_iota(jnp.int32, shape, dim)


def shift(value, amount, axis):
    return pltpu.roll(value, amount % value.shape[axis], axis)


def take(value, index, axis):
    return jnp.take_along_axis(value, index, axis=axis, mode="promise_in_bounds")


def z_pairs(tile):
    return take(tile + shift(tile, -1, 1), lax.rem(2 * iota(TILE, 1), 128), 1)


def put_halves(ref, v, at, value):
    for h in range(2):
        ref[v, h, at, :] = value[:, 128 * h : 128 * h + 128]


def yz_pairs(ref, v, at):
    halves = []
    for h in range(2):
        halves.append(z_pairs(ref[v, h, pl.ds(at, 8, stride=2), :] + ref[v, h, pl.ds(at + 1, 8, stride=2), :]))
    return jnp.where(iota(TILE, 1) < 64, halves[0], halves[1])


def z_repeat(tile, start=0):
    return take(tile, start + iota(TILE, 1) // 2, 1)


def y_pairs(tile):
    return take(tile + shift(tile, -1, 0), lax.rem(2 * iota(TILE, 0), 8), 0)


def y_repeat(tile, start=0):
    return take(tile, jnp.clip(start + iota(TILE, 0) // 2, 0, 7), 0)


def top_bottom(top, bottom):
    return jnp.where(iota(TILE, 0) < 4, top, bottom)


def rounded(x):
    return x.astype(jnp.bfloat16).astype(F32)


def loop(count, chunk, body, carry):
    if count <= chunk:
        for i in range(count):
            carry = body(i, carry)
        return carry

    def step(g, carry):
        for k in range(chunk):
            carry = body(g * chunk + k, carry)
        return carry

    return lax.fori_loop(0, count // chunk, step, carry)


def slabs(lo, count, chunk, body):
    if count <= chunk:
        for k in range(count):
            body(lo + k)
        return

    def step(i, _):
        for k in range(chunk):
            body(lo + i * chunk + k)
        return 0

    lax.fori_loop(0, count // chunk, step, 0)


def build(m, cx, cy, cz, rd, d, lo, count, tau, seg, chunk, firsts=()):
    shape = m.shape[1:]
    row = iota(shape, 0)
    lane = lax.rem(iota(shape, 1), seg)
    last_row, first_row = row == shape[0] - 1, row == 0
    last_lane, first_lane = lane == seg - 1, lane == 0
    half = 0.5 * tau

    def body(a):
        own = m[a]
        xp, xm = m[a + 1], m[a - 1]
        yp = jnp.where(last_row, 0.0, shift(own, -1, 0))
        ym = jnp.where(first_row, 0.0, shift(own, 1, 0))
        zp = jnp.where(last_lane, 0.0, shift(own, -1, 1))
        zm = jnp.where(first_lane, 0.0, shift(own, 1, 1))
        total = 1.0
        for other, ref in ((xp, cx), (xm, None), (yp, cy), (ym, None), (zp, cz), (zm, None)):
            face = rounded(half * (own + other))
            total = total + face
            if ref is not None:
                ref[a] = jnp.where(jnp.minimum(own, other) > 0.0, face, 0.0)
        inverse = DAMPING / total
        rd[a] = inverse
        if d is not None:
            d[a] = total
        for r, u in firsts:
            u[a] = inverse * r[a]

    slabs(lo, count, chunk, body)


def neighbours(v, a, cx, cy, cz):
    own = v[a]
    cya, cza = cy[a], cz[a]
    total = cx[a] * v[a + 1] + cx[a - 1] * v[a - 1]
    total = total + (cya * shift(own, -1, 0) + shift(cya * own, 1, 0))
    total = total + (cza * shift(own, -1, 1) + shift(cza * own, 1, 1))
    return own, total


class Scaled:
    def __init__(self, rd, r, lo, hi):
        self.rd, self.r, self.lo, self.hi, self.seen = rd, r, lo, hi, {}

    def __getitem__(self, a):
        if a not in self.seen:
            inside = self.lo <= a < self.hi
            self.seen[a] = self.rd[a] * self.r[a] if inside else jnp.zeros(self.r.shape[1:], F32)
        return self.seen[a]


def sweep(vin, vout, r, ops, lo, count, chunk):
    cx, cy, cz, rd, d = ops

    def body(a):
        for vi, vo, ri in zip(vin, vout, r):
            own, t = neighbours(vi, a, cx, cy, cz)
            vo[a] = KEEP * own + rd[a] * (ri[a] + t)

    slabs(lo, count, chunk, body)


def residual(vi, ri, a, ops):
    cx, cy, cz, rd, d = ops
    own, t = neighbours(vi, a, cx, cy, cz)
    diag = d[a] if d is not None else DAMPING / rd[a]
    return own, ri[a] + t - diag * own


def fold(x):
    total = None
    for i in range(x.shape[0] // 8):
        for j in range(x.shape[1] // 128):
            part = x[8 * i : 8 * i + 8, 128 * j : 128 * j + 128]
            total = part if total is None else total + part
    return total


def fold_own(x):
    total = None
    for j in range(x.shape[1] // 128):
        lanes = slice(128 * j, 128 * j + 128)
        part = x[8:16, lanes] + top_bottom(x[16:24, lanes], x[0:8, lanes])
        total = part if total is None else total + part
    return total


def kernel(nw, nn, bx, by, nz, m_hbm, s_hbm, c_hbm, out_ref,
           m_ref, s_ref, c_ref,
           m0, cx0, cy0, cz0, rd0, d0, rs0, rc0, us0, uc0, vs0, vc0,
           rx, yp, ry, cp, rcn, xv, hx, xc, hxc, yv, hy, xu, hu,
           m1, cx1, cy1, cz1, rd1, d1, r1, u1, v1, w1, h1, hc, cv1, cs1, cr1, cs2, cr2, qs1, qr1,
           cx2, cy2, cz2, rd2, r2, u2, v2, d2,
           cx3, cy3, cz3, rd3, r3, u3, v3, d3,
           cx4, cy4, cz4, rd4, r4, u4, v4,
           t0, sm2, sr2, sp2, gm, gr, gp, f1p, tok,
           ins, ss, gs, gq, e0r, y0r, m1r, r1r, u0r, mr):
    iw, ino = lax.axis_index("wide"), lax.axis_index("narrow")
    b1x, b1y, z1 = bx // 2, by // 2, nz // 2
    b2x, b2y, z2 = bx // 4, by // 4, nz // 4
    x2, x3, x4 = nw * b2x, nw * b2x // 2, nw * b2x // 4
    there = []
    for dx, dy in SIDES:
        ok = None
        for cond, on in ((iw > 0, dx < 0), (iw < nw - 1, dx > 0), (ino > 0, dy < 0), (ino < nn - 1, dy > 0)):
            if on:
                ok = cond if ok is None else jnp.logical_and(ok, cond)
        there.append(ok)

    def peer(side):
        return (iw + SIDES[side][0], ino + SIDES[side][1])

    inputs = [pltpu.make_async_copy(src, dst, ins.at[0])
              for src, dst in ((m_hbm, m_ref), (s_hbm, s_ref), (c_hbm, c_ref))]
    for copy in inputs:
        copy.start()

    def clear(ref, index):
        ref[index] = jnp.zeros(ref[index].shape, F32)

    barrier = pltpu.get_barrier_semaphore()

    nb = nn // 2 * nw
    me, odd = ino // 2 * nw + iw, lax.rem(ino, 2)
    twin = ino + 1 - 2 * odd

    def fellow(j):
        to = me + j
        to = jnp.where(to >= nb, to - nb, to)
        row = to // nw
        return to - row * nw, 2 * row + odd

    def over_fellows(fn):
        if nb <= 16:
            for j in range(1, nb):
                fn(j)
        else:
            def step(j, _):
                fn(j)
                return 0

            lax.fori_loop(1, nb, step, 0)

    rounds = []
    while 1 << len(rounds) < nb:
        rounds.append(1 << len(rounds))

    def partner(d):
        to = me + d - 2 * d * lax.rem(me // d, 2)
        row = to // nw
        return to - row * nw, 2 * row + odd

    for d in rounds[1:]:
        pl.semaphore_signal(barrier, inc=1, device_id=partner(d), device_id_type=MESH)
    for k in range(8):
        @pl.when(there[k])
        def _():
            pl.semaphore_signal(barrier, inc=1, device_id=peer(k), device_id_type=MESH)

    def meet(n):
        if n > 0:
            pl.semaphore_wait(mr.at[n - 1], 1)
        if n <= len(rounds):
            to = partner(rounds[n]) if n < len(rounds) else (iw, twin)
            pl.semaphore_signal(mr.at[n], inc=1, device_id=to, device_id_type=MESH)

    beside_x = jnp.minimum(iw, 1) + jnp.minimum(nw - 1 - iw, 1)
    beside_y = jnp.minimum(ino, 1) + jnp.minimum(nn - 1 - ino, 1)
    pl.semaphore_wait(barrier, len(rounds) - 1 + beside_x + beside_y + beside_x * beside_y)

    def remote(src, dst, ssem, rsem, dev):
        return pltpu.make_async_remote_copy(src_ref=src, dst_ref=dst, send_sem=ssem, recv_sem=rsem,
                                            device_id=dev, device_id_type=MESH)

    def to_side(side, pairs, rsem):
        land = OPPOSITE[side]
        if rsem is e0r and land > 3:
            land -= 2
        return [remote(src, dst, ss.at[side], rsem.at[land], peer(side)) for src, dst in pairs]

    def e0_sends(side):
        land = OPPOSITE[side]
        if side < 2:
            pairs = []
            at = 0
            for ref, width in ((m_hbm, 2), (s_hbm, 1), (c_hbm, 1)):
                lo = 0 if side == 0 else bx - width
                pairs.append((ref.at[lo : lo + width], rx.at[land, at : at + width]))
                at += width
            return to_side(side, pairs, e0r)
        return to_side(side, [(cp.at[side - 4], rcn.at[land - 4])], e0r)

    def y0_sends(side, lo, hi, sem):
        land = OPPOSITE[side] - 2
        return [remote(yp.at[side - 2, lo:hi], ry.at[land, lo:hi], ss.at[side], y0r.at[sem + land], peer(side))]

    def each(fn, sides=range(8)):
        for side in sides:
            @pl.when(there[side])
            def _():
                fn(side)

    def start(copies):
        for copy in copies:
            copy.start()

    each(lambda k: start(e0_sends(k)), (0, 1))
    meet(0)
    view = tok.at[0 : 3 * bx * by * nz // 1024]
    pltpu.make_async_copy(view, view, ins.at[0]).wait()
    def yp_fill(side, at, ref, k):
        yp[side, at] = ref[:, by - 1 - k if side else k, :]

    for side in range(2):
        yp_fill(side, 0, m_ref, 0)
    each(lambda k: start(y0_sends(k, 0, 1, 0)), (2, 3))
    for side in range(2):
        for at, (ref, k) in enumerate(((m_ref, 1), (m_ref, 2), (s_ref, 0), (s_ref, 1), (c_ref, 0), (c_ref, 1))):
            yp_fill(side, 1 + at, ref, k)
    each(lambda k: start(y0_sends(k, 1, 7, 2)), (2, 3))
    for k in range(4, 8):
        dx, dy = SIDES[k]
        xa, xb = (0, 1) if dx < 0 else (bx - 1, bx - 2)
        ya, yb = (0, 1) if dy < 0 else (by - 1, by - 2)
        for i, (ref, x, y) in enumerate(((m_ref, xa, ya), (m_ref, xa, yb), (m_ref, xb, ya),
                                         (s_ref, xa, ya), (c_ref, xa, ya))):
            cp[k - 4, i] = ref[x, y : y + 1, :]

    each(lambda k: start(e0_sends(k)), (4, 5, 6, 7))

    near1 = ((1, 1), (1, 2), (1, 3), (2, 1), (2, 2), (3, 1))
    near_m1 = near1 + ((2, 3), (1, 4))

    def inside1(side, i, j):
        dx, dy = SIDES[side]
        return H1 + i - 1 if dx < 0 else H1 + b1x - i, b1y + j - 1 if dy < 0 else 2 * b1y - j

    def outside1(side, i, j):
        dx, dy = SIDES[side]
        return H1 - i if dx < 0 else H1 + b1x + i - 1, b1y - j if dy < 0 else 2 * b1y + j - 1

    def box1(side, sending, width):
        dx, dy = SIDES[side]
        w = width
        if sending:
            xlo, w = (H1, w) if dx < 0 else ((H1 + b1x - w, w) if dx > 0 else (H1, b1x))
            ylo = b1y
        else:
            xlo, w = (H1 - w, w) if dx < 0 else ((H1 + b1x, w) if dx > 0 else (H1, b1x))
            ylo = b1y * (1 + dy)
        return xlo, w, ylo

    def level1_sends(ref, rsem, side, width, kc):
        if side > 3:
            src, dst = (cs2, cr2) if kc else (cs1, cr1)
            return to_side(side, [(src.at[side - 4], dst.at[OPPOSITE[side] - 4])], rsem)
        if kc and side > 1:
            return to_side(side, [(qs1.at[side - 2], qr1.at[OPPOSITE[side] - 2])], rsem)
        sx, w, sy = box1(side, True, width)
        tx, _, ty = box1(OPPOSITE[side], False, width)
        return to_side(side, [(ref.at[:, sx : sx + w, sy : sy + b1y], ref.at[:, tx : tx + w, ty : ty + b1y])], rsem)

    def r1_pack(side):
        for x in range(b1x):
            rs, rc = r1[0, H1 + x, own_y, :], r1[1, H1 + x, own_y, :]
            qs1[side - 2, x] = top_bottom(rs, shift(rc, 4, 0)) if side == 2 else top_bottom(shift(rs, 4, 0), rc)

    def r1_unpack(side):
        rows = side_rows[side - 2]
        for x in range(b1x):
            tile = qr1[side - 2, x]
            other = shift(tile, 4, 0)
            r1[0, H1 + x, rows, :] = other if side == 2 else tile
            r1[1, H1 + x, rows, :] = tile if side == 2 else other

    def level1_landed(ref, rsem, width, kc):
        def fn(side):
            if side > 3:
                view = (cr2 if kc else cr1).at[side - 4]
            elif kc and side > 1:
                view = qr1.at[side - 2]
            else:
                tx, w, ty = box1(side, False, width)
                view = ref.at[:, tx : tx + w, ty : ty + b1y]
            pltpu.make_async_copy(view, view, rsem.at[side]).wait()
        return fn

    def e0_landed(side):
        if side in (2, 3):
            view = ry.at[side - 2, 1:7]
            pltpu.make_async_copy(view, view, y0r.at[side]).wait()
        else:
            view = rx.at[side] if side < 2 else rcn.at[side - 4]
            pltpu.make_async_copy(view, view, e0r.at[side if side < 2 else side - 2]).wait()

    def near_landed(side):
        view = ry.at[side - 2, 0:1]
        pltpu.make_async_copy(view, view, y0r.at[side - 2]).wait()

    own_y = slice(b1y, 2 * b1y)
    for i in range(b1x):
        put_halves(t0, 0, slice(i * by, (i + 1) * by), m_ref[2 * i] + m_ref[2 * i + 1])
    for i in range(b1x):
        m1[0, H1 + i, own_y, :] = 0.125 * yz_pairs(t0, 0, i * by)
    for k in range(4, 8):
        for n, (i, j) in enumerate(near_m1):
            x, y = inside1(k, i, j)
            cs1[k - 4, n : n + 1, :] = m1[0, x, y : y + 1, :]
    low2 = iota(TILE, 1) < z2
    for i in range(0, b2x, 4):
        tiles = []
        for n in range(i, i + 4, 2):
            quads = [y_pairs(m1[0, H1 + 2 * k, own_y, :] + m1[0, H1 + 2 * k + 1, own_y, :]) for k in (n, n + 1)]
            tiles.append(0.125 * z_pairs(top_bottom(quads[0], quads[1])))
        mob2 = jnp.where(low2, tiles[0], tiles[1])
        sm2[2 * i : 2 * i + 8, :] = mob2
        gm[odd, me, 2 * i : 2 * i + 8, :] = mob2

    def send_sem(kind):
        return gs.at[gs.shape[0] - 1 if kind > 3 else min(kind, gs.shape[0] - 2)]

    def to_fellows(src, dst, kind):
        over_fellows(lambda j: remote(src, dst, send_sem(kind), gq.at[kind], fellow(j)).start())

    def to_twin(src, dst, kind):
        remote(src, dst, send_sem(kind), gq.at[kind], (iw, twin)).start()

    def to_others(src, dst, kind):
        def to_one(j):
            to = me + j
            to = jnp.where(to >= nb, to - nb, to)
            row = to // nw
            remote(src, dst, send_sem(kind), gq.at[kind], (to - row * nw, 2 * row + 1 - odd)).start()

        if nb <= 16:
            for j in range(nb):
                to_one(j)
        else:
            def step(j, _):
                to_one(j)
                return 0

            lax.fori_loop(0, nb, step, 0)

    def landed(view, kind):
        pltpu.make_async_copy(view, view, gq.at[kind]).wait()

    for ref, src, width in ((m0, m_ref, 2), (rs0, s_ref, 1), (rc0, c_ref, 1)):
        blank = jnp.zeros(m0.shape[1:], F32)
        for i in range(width):
            ref[H0 - 1 - i] = blank
            ref[H0 + bx + i] = blank

        def put(i):
            ref[H0 + i, H0 : H0 + by, :] = src[i]

        slabs(0, bx, bx, put)
    side_rows = (slice(0, b1y), slice(2 * b1y, 3 * b1y))
    for k in range(8):
        @pl.when(jnp.logical_not(there[k]))
        def _():
            if k > 3:
                clear(rcn, k - 4)
                clear(cr1, k - 4)
                clear(cr2, k - 4)
                return
            lands = ((rx, hx, hxc, hu, h1, hc) if k < 2 else (ry, hy, qr1))
            for ref in lands:
                clear(ref, k % 2)
            for ref, width in (((m1, 3), (r1, 2)) if k < 2 else ((m1, 3),)):
                xlo, w, ylo = box1(k, False, width)
                clear(ref, (slice(None), slice(xlo, xlo + w), slice(ylo, ylo + b1y)))
    for a in (0, H1 + b1x + 3):
        clear(m1, (0, a))
    for a in (1, 2, 3, H1 + b1x, H1 + b1x + 1, H1 + b1x + 2):
        for rows in side_rows:
            clear(m1, (0, a, rows))
            for v in range(2):
                clear(r1, (v, a, rows))
    for ref in (us0, uc0):
        ref[H0 - 2] = jnp.zeros(m0.shape[1:], F32)
        ref[H0 + bx + 1] = jnp.zeros(m0.shape[1:], F32)
    for a in (0, 1, 2, 3, H1 + b1x, H1 + b1x + 1, H1 + b1x + 2, H1 + b1x + 3):
        for v in range(2):
            v1[v, a] = jnp.zeros(v1.shape[2:], F32)
    for ref in (u4, v4):
        zero = jnp.zeros(ref.shape[1:], F32)
        for a in (0, 1, ref.shape[0] - 2, ref.shape[0] - 1):
            ref[a] = zero
    for ref in (u2, v2, r2, cx2, cy2, cz2, rd2, u3, v3, r3, cx3, cy3, cz3, rd3):
        zero = jnp.zeros(ref.shape[1:], F32)
        for a in range(PAD2):
            ref[a] = zero
            ref[ref.shape[0] - 1 - a] = zero
    cx4[PAD - 1] = jnp.zeros(cx4.shape[1:], F32)

    ops0 = (cx0, cy0, cz0, rd0, d0)
    firsts0 = ((rs0, us0), (rc0, uc0))
    each(near_landed, (2, 3))
    m0[H0 : H0 + bx, H0 - 1, :] = ry[0, 0]
    m0[H0 : H0 + bx, H0 + by, :] = ry[1, 0]
    for side, a in enumerate((H0 + 1, H0 + bx - 2)):
        build(m0, cx0, cy0, cz0, rd0, d0, a, 1, BASE_TAU, nz, 1, firsts0)
        for v, ref in enumerate((us0, uc0)):
            xu[side, v] = ref[a, H0 : H0 + by, :]
    each(lambda k: start(to_side(k, [(xu.at[k], hu.at[OPPOSITE[k]])], u0r)), (0, 1))
    each(lambda k: start(level1_sends(m1, m1r, k, 3, 0)))
    meet(1)
    each(e0_landed, (2, 3))
    for ref, at, lo, width in ((m0, 1, 1, 2), (rs0, 3, 0, 2), (rc0, 5, 0, 2)):
        for i in range(width):
            ref[H0 : H0 + bx, H0 - 1 - lo - i, :] = ry[0, at + i]
            ref[H0 : H0 + bx, H0 + by + lo + i, :] = ry[1, at + i]

    meet(2)
    build(m0, cx0, cy0, cz0, rd0, d0, H0 + 1, bx - 2, BASE_TAU, nz, bx - 2, firsts0)
    sweep((us0, uc0), (vs0, vc0), (rs0, rc0), ops0, H0 + 2, bx - 4, bx - 4)

    def down0(i, carry):
        num, den = carry
        sums = []
        for k in range(2):
            a = H0 + 2 * i + k
            vs, es = residual(vs0, rs0, a, ops0)
            vc, ec = residual(vc0, rc0, a, ops0)
            both = es + rs0[a]
            num = num + fold_own(both * vc)
            den = den + fold_own(both * vs)
            sums.append((es, ec))
        at = slice(i * m0.shape[1], (i + 1) * m0.shape[1])
        put_halves(t0, 0, at, sums[0][0] + sums[1][0])
        put_halves(t0, 1, at, sums[0][1] + sums[1][1])
        return num, den

    zero8 = jnp.zeros(TILE, F32)
    part0 = loop(b1x - 4, b1x - 4, lambda i, c: down0(2 + i, c), (zero8, zero8))


    def coarse0(i):
        for v in range(2):
            r1[v, H1 + i, own_y, :] = 0.125 * yz_pairs(t0, v, i * m0.shape[1] + H0)

    slabs(2, b1x - 4, b1x - 4, coarse0)
    meet(3)
    def u0_landed(side):
        pltpu.make_async_copy(hu.at[side], hu.at[side], u0r.at[side]).wait()

    each(e0_landed, (0, 1, 4, 5, 6, 7))
    for n in range(4, len(rounds) + 1):
        meet(n)
    to_fellows(sm2, gm.at[odd, me], 0)
    for ref, at, width in ((m0, 0, 2), (rs0, 2, 1), (rc0, 3, 1)):
        for i in range(width):
            ref[H0 - width + i, H0 : H0 + by, :] = rx[0, at + i]
            ref[H0 + bx + i, H0 : H0 + by, :] = rx[1, at + i]
    for k in range(4):
        dx, dy = SIDES[4 + k]
        xa, xb = (H0 - 1, H0 - 2) if dx < 0 else (H0 + bx, H0 + bx + 1)
        ya, yb = (H0 - 1, H0 - 2) if dy < 0 else (H0 + by, H0 + by + 1)
        for i, (ref, x, y) in enumerate(((m0, xa, ya), (m0, xa, yb), (m0, xb, ya), (rs0, xa, ya), (rc0, xa, ya))):
            ref[x, y : y + 1, :] = rcn[k, i]
    beyond = m0[H0 - 2]
    own = m0[H0 - 1]
    cx0[H0 - 2] = jnp.where(jnp.minimum(own, beyond) > 0.0, rounded(0.5 * BASE_TAU * (own + beyond)), 0.0)
    for lo in (H0 - 1, H0 + bx - 1):
        build(m0, cx0, cy0, cz0, rd0, d0, lo, 2, BASE_TAU, nz, 2, firsts0)
    each(u0_landed, (0, 1))
    for v, ref in enumerate((us0, uc0)):
        ref[H0 - 2, H0 : H0 + by, :] = hu[0, v]
        ref[H0 + bx + 1, H0 : H0 + by, :] = hu[1, v]
    for v_lo in (H0 - 1, H0 + bx - 2):
        sweep((us0, uc0), (vs0, vc0), (rs0, rc0), ops0, v_lo, 3, 3)
    num0, den0 = loop(2, 2, lambda i, c: down0(b1x - 2 + i, down0(i, c)), part0)
    for i in (0, 1, b1x - 2, b1x - 1):
        coarse0(i)
    for k in range(4, 8):
        for n in range(6):
            x, y = inside1(k, 1, 1 + n // 2)
            cs2[k - 4, n] = r1[n % 2, x, y : y + 1, :]
    for k in (2, 3):
        r1_pack(k)
    each(lambda k: start(level1_sends(r1, r1r, k, 2, 1)), (4, 5, 6, 7, 0, 1, 2, 3))
    for side, (x_far, x_near) in enumerate(((H0 + 1, H0), (H0 + bx - 2, H0 + bx - 1))):
        for v, ref in enumerate((vs0, vc0)):
            xv[side, v] = ref[x_far, H0 : H0 + by, :]
            xc[side, 2 * v] = ref[x_near, H0 - 1 : H0, :]
            xc[side, 2 * v + 1] = ref[x_near, H0 + by : H0 + by + 1, :]
    for side, col in enumerate((H0 + 1, H0 + by - 2)):
        for v, ref in enumerate((vs0, vc0)):
            yv[side, v] = ref[H0 : H0 + bx, col, :]

    def v0_sends(side):
        land = OPPOSITE[side]
        if side < 2:
            return to_side(side, [(xv.at[side], hx.at[land]), (xc.at[side], hxc.at[land])], e0r)
        return [remote(yv.at[side - 2], hy.at[land - 2], ss.at[side], y0r.at[land], peer(side))]

    each(level1_landed(m1, m1r, 3, 0))
    for k in range(4, 8):
        for n, (i, j) in enumerate(near_m1):
            x, y = outside1(k, i, j)
            m1[0, x, y : y + 1, :] = cr1[k - 4, n : n + 1, :]
    ops1 = (cx1, cy1, cz1, rd1, d1)
    build(m1.at[0], cx1, cy1, cz1, rd1, d1, H1 - 3, b1x + 6, BASE_TAU / 4, z1, b1x + 6)
    rr1 = (r1.at[0], r1.at[1])
    uu1 = (u1.at[0], u1.at[1])
    vv1 = (v1.at[0], v1.at[1])
    halves1 = {}

    def first1(a):
        for v in range(2):
            u1[v, a] = rd1[a] * r1[v, a]

    def down1(i, carry):
        num, den = carry
        pair = []
        for k in range(2):
            a = H1 + 2 * i + k
            vs, es = residual(vv1[0], rr1[0], a, ops1)
            vc, ec = residual(vv1[1], rr1[1], a, ops1)
            both = (es + r1[0, a])[own_y]
            num = num + both * vc[own_y]
            den = den + both * vs[own_y]
            pair.append((es[own_y], ec[own_y]))
        halves1[i] = [y_pairs(pair[0][v] + pair[1][v]) for v in range(2)]
        return num, den

    landed1 = level1_landed(r1, r1r, 2, 1)
    each(landed1, (2, 3))
    for k in (2, 3):
        r1_unpack(k)
    slabs(H1, b1x, b1x, first1)
    sweep(uu1, vv1, rr1, ops1, H1 + 1, b1x - 2, b1x - 2)
    sums1 = loop(b2x - 2, b2x - 2, lambda i, c: down1(1 + i, c), (zero8, zero8))
    each(landed1, (0, 1, 4, 5, 6, 7))
    for k in range(4, 8):
        for n in range(6):
            x, y = outside1(k, 1, 1 + n // 2)
            r1[n % 2, x, y : y + 1, :] = cr2[k - 4, n]
    for a in (H1 - 2, H1 + b1x):
        slabs(a, 2, 2, first1)
    for a in (H1 - 1, H1 + b1x - 1):
        sweep(uu1, vv1, rr1, ops1, a, 2, 2)
    num1, den1 = down1(b2x - 1, down1(0, sums1))
    for i in range(0, b2x, 2):
        packed = [z_pairs(top_bottom(halves1[i][v], halves1[i + 1][v])) for v in range(2)]
        own2 = 0.125 * jnp.where(low2, packed[0], packed[1])
        sr2[i * b2y : (i + 2) * b2y, :] = own2
        gr[odd, me, i * b2y : (i + 2) * b2y, :] = own2
    meet(len(rounds) + 1)
    to_fellows(sr2, gr.at[odd, me], 2)
    num_row = jnp.sum(num0 + 8.0 * num1, axis=0, keepdims=True)
    den_row = jnp.sum(den0 + 8.0 * den1, axis=0, keepdims=True)
    low1 = iota((1, 128), 1) < 64
    part = jnp.where(low1, num_row + shift(num_row, 64, 1), den_row + shift(den_row, 64, 1))
    sp2[...] = part
    mine = odd * nb + me
    gp[mine] = part
    to_fellows(sp2, gp.at[mine], 4)
    to_others(sp2, gp.at[mine], 4)

    def v1_corners(side, ref_v, ref_r, tiles, outward):
        for d in range(2):
            corner = 4 + 2 * side + d
            for n, (i, j) in enumerate(near1 + ((1, 2), (2, 1))):
                x = (outside1 if outward else inside1)(corner, i, j)[0]
                y = outside1(corner, i, j)[1]
                ref = ref_v if n < 6 else ref_r
                for v in range(2):
                    if outward:
                        ref[v, x, y : y + 1, :] = tiles[side, v, d, n : n + 1, :]
                    else:
                        tiles[side, v, d, n : n + 1, :] = ref[v, x, y : y + 1, :]

    for side in range(2):
        v1_corners(side, v1, r1, cv1, False)
    landed(gm.at[0, 0 : nb - 1], 0)
    to_twin(gm.at[odd], gm.at[odd], 1)
    landed(gm.at[0], 1)
    def v1_sends(side):
        land = OPPOSITE[side]
        lo = H1 if side == 0 else H1 + b1x - 3
        return to_side(side, [(v1.at[:, lo : lo + 3, own_y], h1.at[land]), (cv1.at[side], hc.at[land])], u0r)


    def unpack(src, dst, u=None):
        def step(w, carry):
            for i in range(b2x):
                a = PAD2 + w * b2x + i
                for n in range(nn):
                    dst[a, n * b2y : (n + 1) * b2y, :] = src[n % 2, n // 2 * nw + w, i * b2y : (i + 1) * b2y, :]
                if u is not None:
                    u[a] = rd2[a] * dst[a]
            return carry

        loop(nw, 8, step, 0)

    def unpack_m(w, carry):
        for n in range(nn):
            for i in range(0, b2x, 4):
                tile = gm[n % 2, n // 2 * nw + w, 2 * i : 2 * i + 8, :]
                other = shift(tile, z2, 1)
                for k, part in enumerate((jnp.where(low2, tile, other), jnp.where(low2, other, tile))):
                    for h in range(2):
                        a = PAD2 + w * b2x + i + 2 * k + h
                        v2[a, n * b2y : (n + 1) * b2y, :] = part[h * b2y : (h + 1) * b2y, :]
        return carry

    loop(nw, 8, unpack_m, 0)
    kept2 = d2 if d2.shape == v2.shape else None
    build(v2, cx2, cy2, cz2, rd2, kept2, PAD2, x2, BASE_TAU / 16, z2, 16)

    def coarsen_y(x):
        if x.shape[0] == 16:
            return top_bottom(y_pairs(x[0:8]), y_pairs(x[8:16]))
        return top_bottom(y_pairs(x), 0.0)

    def coarsen_z(dst, lo, count):
        def body(a):
            dst[a] = 0.125 * z_pairs(dst[a])

        slabs(lo, count, min(count, 16), body)

    def coarsen_pairs(src, dst, xc, pad):
        def body(i, carry):
            a = PAD2 + 2 * i
            dst[pad + i] = coarsen_y(src[a] + src[a + 1])
            return carry

        loop(xc, 16, body, 0)
        coarsen_z(dst, pad, xc)

    coarsen_pairs(v2, v3, x3, PAD2)
    build(v3, cx3, cy3, cz3, rd3, d3, PAD2, x3, BASE_TAU / 64, z2 // 2, 16)
    coarsen_pairs(v3, v4, x4, PAD)
    build(v4, cx4, cy4, cz4, rd4, None, PAD, x4, BASE_TAU / 256, z2 // 4, 8)

    each(lambda k: start(v1_sends(k)), range(2))
    each(lambda k: start(v0_sends(k)), range(4))
    landed(gr.at[0, 0 : nb - 1], 2)
    to_twin(gr.at[odd], gr.at[odd], 3)


    def v0_landed(side):
        view = tok.at[0 : (2 * by + 4) * nz // 1024] if side < 2 else hy.at[side - 2]
        pltpu.make_async_copy(view, view, e0r.at[side] if side < 2 else y0r.at[side]).wait()

    landed(gr.at[0], 3)
    unpack(gr, r2, u2)

    ops2 = (cx2, cy2, cz2, rd2, kept2)
    ops3 = (cx3, cy3, cz3, rd3, d3)
    ops4 = (cx4, cy4, cz4, rd4, None)

    def coarsen_residual(v, r, ops, dst, xc, pad, seg):
        low = iota(v.shape[1:], 1) < seg

        def step(i, carry):
            num, den = carry
            pair = []
            for j in range(2):
                a = PAD2 + 2 * i + j
                own, e = residual(v, r, a, ops)
                both = jnp.where(low, e + r[a], 0.0)
                num = num + fold(both * shift(own, -seg, 1))
                den = den + fold(both * own)
                pair.append(e)
            dst[pad + i] = coarsen_y(pair[0] + pair[1])
            return num, den

        sums = loop(xc, 16, step, (zero8, zero8))
        coarsen_z(dst, pad, xc)
        return sums

    sweep((u2,), (v2,), (r2,), ops2, PAD2, x2, 32)
    landed(gp.at[0 : 2 * nb - 1], 4)
    whole = loop(2 * nb, 32, lambda i, acc: acc + gp[i], jnp.zeros((1, 128), F32))
    num2, den2 = coarsen_residual(v2, r2, ops2, r3, x3, PAD2, z2)
    def first3(a):
        u3[a] = rd3[a] * r3[a]

    if x3 <= 16:
        sweep((Scaled(rd3, r3, PAD2, PAD2 + x3),), (v3,), (r3,), ops3, PAD2, x3, 16)
    else:
        slabs(PAD2, x3, 16, first3)
        sweep((u3,), (v3,), (r3,), ops3, PAD2, x3, 16)
    num3, den3 = coarsen_residual(v3, r3, ops3, r4, x4, PAD, z2 // 2)

    def first4(a):
        u4[a] = rd4[a] * r4[a]

    if x4 <= 8:
        sweep((Scaled(rd4, r4, PAD, PAD + x4),), (v4,), (r4,), ops4, PAD, x4, 8)
    else:
        slabs(PAD, x4, 8, first4)
        sweep((u4,), (v4,), (r4,), ops4, PAD, x4, 8)
    low4 = iota(TILE, 1) < z2 // 4

    def dots(i, carry):
        num, den = carry
        for k in range(8):
            a = PAD + 8 * i + k
            both = jnp.where(low4, r4[a], 0.0)
            den = den + both * v4[a]
            num = num + both * shift(v4[a], -(z2 // 4), 1)
        return num, den

    num4, den4 = dots(0, (zero8, zero8)) if x4 == 8 else lax.fori_loop(0, x4 // 8, dots, (zero8, zero8))
    b3x = b2x // 2
    base3 = PAD2 + iw * b3x
    for i in range(b3x // 2 + 4):
        add = y_repeat(z_repeat(v4[PAD + iw * (b3x // 2) - 2 + i]))
        for j in range(2):
            a = base3 - 4 + 2 * i + j
            v3[a] = v3[a] + add
    sweep((v3,), (u3,), (r3,), ops3, base3 - 3, b3x + 6, b3x + 6)
    sweep((u3,), (v3,), (r3,), ops3, base3 - 2, b3x + 4, b3x + 4)

    def total_of(mask, n2, n3, n4):
        x = jnp.sum(64.0 * n2 + 512.0 * n3 + 4096.0 * n4, axis=0, keepdims=True)
        return jnp.sum(x + jnp.where(mask, whole, 0.0), axis=1, keepdims=True)

    ratio = total_of(low1, num2, num3, num4) / (1.0 + total_of(jnp.logical_not(low1), den2, den3, den4))
    ratio = jnp.broadcast_to(ratio, (1, 128))
    base = PAD2 + iw * b2x
    for i in range(b2x // 2 + 4):
        wide_tile = z_repeat(v3[base3 - 2 + i])
        for j in range(2):
            a = base - 4 + 2 * i + j
            v2[a, 0:8, :] = v2[a, 0:8, :] + y_repeat(wide_tile)
            v2[a, 8:16, :] = v2[a, 8:16, :] + y_repeat(wide_tile, 4)
    sweep((v2,), (u2,), (r2,), ops2, base - 3, b2x + 6, b2x + 6)
    sweep((u2,), (v2,), (r2,), ops2, base - 2, b2x + 4, b2x + 4)

    def v1_landed(side):
        view = tok.at[0 : 10]
        pltpu.make_async_copy(view, view, u0r.at[side]).wait()

    each(v1_landed, range(2))
    for side, a in enumerate((H1 - 3, H1 + b1x)):
        v1[:, a : a + 3, own_y] = h1[side]
        v1_corners(side, v1, r1, hc, True)
    rows2 = v2.shape[1]
    full_y = 2 * rows2
    for i in range(b2x + 4):
        f1p[i, 0:b1y, :] = jnp.zeros((b1y, z1), F32)
        f1p[i, b1y + full_y : 2 * b1y + full_y, :] = jnp.zeros((b1y, z1), F32)
        for j in range(rows2 // 8):
            e = v2[base - 2 + i, 8 * j : 8 * j + 8, :]
            part = z_repeat(shift(e, z2, 1) - ratio * e)
            f1p[i, pl.ds(b1y + 16 * j, 8, stride=2), :] = part
            f1p[i, pl.ds(b1y + 16 * j + 1, 8, stride=2), :] = part
    window = pl.ds(pl.multiple_of(ino * b1y, 8), 3 * b1y)
    for x in range(-3, b1x + 3):
        a = H1 + x
        u1[0, a] = v1[1, a] - ratio * v1[0, a] + f1p[x // 2 + 2, window, :]
        if -2 <= x < b1x + 2:
            w1[a] = r1[1, a] - ratio * r1[0, a]
    sweep((u1.at[0],), (u1.at[1],), (w1,), ops1, H1 - 2, b1x + 4, b1x + 4)
    sweep((u1.at[1],), (u1.at[0],), (w1,), ops1, H1 - 1, b1x + 2, b1x + 2)

    each(v0_landed, range(4))
    for side, (x_far, x_near) in enumerate(((H0 - 2, H0 - 1), (H0 + bx + 1, H0 + bx))):
        for v, ref in enumerate((vs0, vc0)):
            ref[x_far, H0 : H0 + by, :] = hx[side, v]
            ref[x_near, H0 - 1 : H0, :] = hxc[side, 2 * v]
            ref[x_near, H0 + by : H0 + by + 1, :] = hxc[side, 2 * v + 1]
    for side, col in enumerate((H0 - 2, H0 + by + 1)):
        for v, ref in enumerate((vs0, vc0)):
            ref[H0 : H0 + bx, col, :] = hy[side, v]
    ratio0 = jnp.concatenate([ratio] * (nz // 128), axis=1)

    def up0(g):
        tiles = [[u1[0, H1 - 1 + 2 * g + k, 8 * j : 8 * j + 8, :] for j in range(3)] for k in range(2)]
        sub = iota(TILE, 0)
        ends = [top_bottom(jnp.where(sub < 2, shift(t[0], 2, 0), shift(t[2], 2, 0)), 0.0) for t in tiles]
        ends = top_bottom(ends[0], shift(ends[1], 4, 0))
        halves = [[z_repeat(t, start) for t in (ends, tiles[0][1], tiles[1][1])] for start in (0, 64)]
        for k in range(2):
            adds = []
            for end, mid in ((h[0], h[1 + k]) for h in halves):
                end = shift(end, -4 * k, 0) if k else end
                adds.append((top_bottom(y_repeat(end), y_repeat(mid, -2)), y_repeat(mid, 2),
                             top_bottom(y_repeat(mid, 6), y_repeat(end))))
            add = jnp.concatenate([jnp.concatenate([adds[0][j], adds[1][j]], axis=1) for j in range(3)], axis=0)
            for i in range(2):
                a = H0 - 2 + 4 * g + 2 * k + i
                us0[a] = vc0[a] - ratio0 * vs0[a] + add
                rc0[a] = rc0[a] - ratio0 * rs0[a]

    slabs(0, b1x // 2 + 1, b1x // 2 + 1, up0)
    sweep((us0,), (uc0,), (rc0,), ops0, H0 - 1, bx + 2, bx + 2)

    def last(a):
        own, t = neighbours(uc0, a, cx0, cy0, cz0)
        out_ref[a - H0] = (KEEP * own + rd0[a] * (rc0[a] + t))[H0 : H0 + by]

    slabs(H0, bx, bx, last)

    def sent(side):
        dx, dy = SIDES[side]
        if dy == 0:
            tiles = 6 * by * nz // 1024 + 3 + 4 + (2 * by + 4) * nz // 1024 + 10
        elif dx == 0:
            tiles = 7 * bx * nz // 1024 + b1x + b1x + 2 * bx * nz // 1024
        else:
            tiles = 3
        view = tok.at[0:tiles]
        pltpu.make_async_copy(view, view, ss.at[side]).wait()

    each(sent)
    if gs.shape[0] == 2:
        views = (tok.at[0 : 3 * (nb - 1) + 3 * nb],)
    else:
        views = (gm.at[0, 0 : nb - 1], gm.at[0], gr.at[0, 0 : nb - 1], gr.at[0])
    views += (gp.at[0 : 2 * nb - 1],)
    for i, view in enumerate(views):
        pltpu.make_async_copy(view, view, gs.at[i]).wait()


def solution(mesh):
    nw, nn = mesh.shape["wide"], mesh.shape["narrow"]

    def per_device(mobility, sav_vector, cotangent):
        bx, by, nz = mobility.shape
        b1x, b1y, z1 = bx // 2, by // 2, nz // 2
        x2, y2 = nw * bx // 4, nn * by // 4
        own = (bx, by, nz)
        l0 = (bx + 2 * H0, by + 2 * H0, nz)
        l1 = (b1x + 2 * H1, 3 * b1y, z1)
        l2 = (x2 + 2 * PAD2, y2, z1)
        l3 = (x2 // 2 + 2 * PAD2, y2 // 2, z1)
        l4 = (x2 // 4 + 2 * PAD, 8, z1)
        own2 = (bx // 4 * (by // 4), z1)
        half2 = (bx // 4 * (by // 4) // 2, z1)
        buffers = (
            [own] * 3 + [l0] * 12
            + [(2, 4, by, nz), (2, 7, bx, nz), (2, 7, bx, nz), (4, 5, 1, nz), (4, 5, 1, nz)]
            + [(2, 2, by, nz)] * 2 + [(2, 4, 1, nz)] * 2 + [(2, 2, bx, nz)] * 2 + [(2, 2, by, nz)] * 2
            + [(1, *l1)] + [l1] * 5 + [(2, *l1)] * 3 + [l1] + [(2, 2, 3, b1y, z1), (2, 2, 2, b1y, z1), (2, 2, 2, b1y, z1), (4, *TILE), (4, *TILE), (4, 6, 1, z1), (4, 6, 1, z1), (2, b1x, *TILE), (2, b1x, *TILE)]
            + [l2] * 7 + [l2 if nw <= 16 else (1, *TILE)] + [l3] * 8 + [l4] * 7
            + [(2, 2, b1x * l0[1], nz // 2)]
            + [half2, own2, (1, 128), (2, nn // 2 * nw, *half2), (2, nn // 2 * nw, *own2), (nn * nw, 1, 128)]
            + [(bx // 4 + 4, 2 * y2 + 2 * b1y, z1), (3 * bx * by * nz // 1024, *TILE)]
        )
        size = sum(4 * functools.reduce(lambda p, q: p * q, shape) for shape in buffers)
        dma = lambda n: pltpu.SemaphoreType.DMA((n,))
        scratch = [pltpu.VMEM(shape, F32) for shape in buffers]
        scratch += [dma(n) for n in (1, 8, 2 if nn // 2 * nw <= 16 else 5, 5, 6, 4, 8, 8, 2)]
        steps = (nn // 2 * nw - 1).bit_length() + 1
        scratch.append(pltpu.SemaphoreType.REGULAR((steps,)))
        return pl.pallas_call(
            functools.partial(kernel, nw, nn, bx, by, nz),
            out_shape=jax.ShapeDtypeStruct((bx, by, nz), F32),
            in_specs=[pl.BlockSpec(memory_space=pltpu.HBM)] * 3,
            out_specs=pl.BlockSpec(memory_space=pltpu.VMEM),
            scratch_shapes=scratch,
            compiler_params=pltpu.CompilerParams(
                collective_id=0, has_side_effects=True, vmem_limit_bytes=GRANT if size < GRANT else 67043328
            ),
        )(mobility, sav_vector, cotangent)

    spec = P("wide", "narrow", None)
    return jax.shard_map(per_device, mesh=mesh, in_specs=(spec,) * 3, out_specs=spec, check_vma=False)
```

```python
import functools
import jax
import jax.numpy as jnp
from jax import lax
from jax.experimental import pallas as pl
from jax.experimental.pallas import tpu as pltpu
from jax.sharding import PartitionSpec as P

DAMPING = 0.8
KEEP = 1.0 - DAMPING
BASE_TAU = 16.0
H0 = 4
H1 = 4
PAD = 2
PAD2 = 4
GRANT = 56200000
MESH = pl.DeviceIdType.MESH
F32 = jnp.float32
SIDES = [(-1, 0), (1, 0), (0, -1), (0, 1), (-1, -1), (-1, 1), (1, -1), (1, 1)]
OPPOSITE = [1, 0, 3, 2, 7, 6, 5, 4]
TILE = (8, 128)


def iota(shape, dim):
    return lax.broadcasted_iota(jnp.int32, shape, dim)


def shift(value, amount, axis):
    return pltpu.roll(value, amount % value.shape[axis], axis)


def take(value, index, axis):
    return jnp.take_along_axis(value, index, axis=axis, mode="promise_in_bounds")


def z_pairs(tile):
    return take(tile + shift(tile, -1, 1), lax.rem(2 * iota(TILE, 1), 128), 1)


def put_halves(ref, v, at, value):
    for h in range(2):
        ref[v, h, at, :] = value[:, 128 * h : 128 * h + 128]


def yz_pairs(ref, v, at):
    halves = []
    for h in range(2):
        halves.append(z_pairs(ref[v, h, pl.ds(at, 8, stride=2), :] + ref[v, h, pl.ds(at + 1, 8, stride=2), :]))
    return jnp.where(iota(TILE, 1) < 64, halves[0], halves[1])


def z_repeat(tile, start=0):
    return take(tile, start + iota(TILE, 1) // 2, 1)


def y_pairs(tile):
    return take(tile + shift(tile, -1, 0), lax.rem(2 * iota(TILE, 0), 8), 0)


def y_repeat(tile, start=0):
    return take(tile, jnp.clip(start + iota(TILE, 0) // 2, 0, 7), 0)


def top_bottom(top, bottom):
    return jnp.where(iota(TILE, 0) < 4, top, bottom)


def rounded(x):
    return x.astype(jnp.bfloat16).astype(F32)


def loop(count, chunk, body, carry):
    if count <= chunk:
        for i in range(count):
            carry = body(i, carry)
        return carry

    def step(g, carry):
        for k in range(chunk):
            carry = body(g * chunk + k, carry)
        return carry

    return lax.fori_loop(0, count // chunk, step, carry)


def slabs(lo, count, chunk, body):
    if count <= chunk:
        for k in range(count):
            body(lo + k)
        return

    def step(i, _):
        for k in range(chunk):
            body(lo + i * chunk + k)
        return 0

    lax.fori_loop(0, count // chunk, step, 0)


def build(m, cx, cy, cz, rd, d, lo, count, tau, seg, chunk, firsts=()):
    shape = m.shape[1:]
    row = iota(shape, 0)
    lane = lax.rem(iota(shape, 1), seg)
    last_row, first_row = row == shape[0] - 1, row == 0
    last_lane, first_lane = lane == seg - 1, lane == 0
    half = 0.5 * tau

    def body(a):
        own = m[a]
        xp, xm = m[a + 1], m[a - 1]
        yp = jnp.where(last_row, 0.0, shift(own, -1, 0))
        ym = jnp.where(first_row, 0.0, shift(own, 1, 0))
        zp = jnp.where(last_lane, 0.0, shift(own, -1, 1))
        zm = jnp.where(first_lane, 0.0, shift(own, 1, 1))
        total = 1.0
        for other, ref in ((xp, cx), (xm, None), (yp, cy), (ym, None), (zp, cz), (zm, None)):
            face = rounded(half * (own + other))
            total = total + face
            if ref is not None:
                ref[a] = jnp.where(jnp.minimum(own, other) > 0.0, face, 0.0)
        inverse = DAMPING / total
        rd[a] = inverse
        if d is not None:
            d[a] = total
        for r, u in firsts:
            u[a] = inverse * r[a]

    slabs(lo, count, chunk, body)


def neighbours(v, a, cx, cy, cz):
    own = v[a]
    cya, cza = cy[a], cz[a]
    total = cx[a] * v[a + 1] + cx[a - 1] * v[a - 1]
    total = total + (cya * shift(own, -1, 0) + shift(cya * own, 1, 0))
    total = total + (cza * shift(own, -1, 1) + shift(cza * own, 1, 1))
    return own, total


class Scaled:
    def __init__(self, rd, r, lo, hi):
        self.rd, self.r, self.lo, self.hi, self.seen = rd, r, lo, hi, {}

    def __getitem__(self, a):
        if a not in self.seen:
            inside = self.lo <= a < self.hi
            self.seen[a] = self.rd[a] * self.r[a] if inside else jnp.zeros(self.r.shape[1:], F32)
        return self.seen[a]


def sweep(vin, vout, r, ops, lo, count, chunk):
    cx, cy, cz, rd, d = ops

    def body(a):
        for vi, vo, ri in zip(vin, vout, r):
            own, t = neighbours(vi, a, cx, cy, cz)
            vo[a] = KEEP * own + rd[a] * (ri[a] + t)

    slabs(lo, count, chunk, body)


def residual(vi, ri, a, ops):
    cx, cy, cz, rd, d = ops
    own, t = neighbours(vi, a, cx, cy, cz)
    diag = d[a] if d is not None else DAMPING / rd[a]
    return own, ri[a] + t - diag * own


def fold(x):
    total = None
    for i in range(x.shape[0] // 8):
        for j in range(x.shape[1] // 128):
            part = x[8 * i : 8 * i + 8, 128 * j : 128 * j + 128]
            total = part if total is None else total + part
    return total


def fold_own(x):
    total = None
    for j in range(x.shape[1] // 128):
        lanes = slice(128 * j, 128 * j + 128)
        part = x[8:16, lanes] + top_bottom(x[16:24, lanes], x[0:8, lanes])
        total = part if total is None else total + part
    return total


def kernel(nw, nn, bx, by, nz, m_hbm, s_hbm, c_hbm, out_ref,
           m_ref, s_ref, c_ref,
           m0, cx0, cy0, cz0, rd0, d0, rs0, rc0, us0, uc0, vs0, vc0,
           rx, yp, ry, cp, rcn, xv, hx, xc, hxc, yv, hy, xu, hu,
           m1, cx1, cy1, cz1, rd1, d1, r1, u1, v1, w1, h1, hc, cv1, cs1, cr1, cs2, cr2, qs1, qr1,
           cx2, cy2, cz2, rd2, r2, u2, v2, d2,
           cx3, cy3, cz3, rd3, r3, u3, v3, d3,
           cx4, cy4, cz4, rd4, r4, u4, v4,
           t0, sm2, sr2, sp2, gm, gr, gp, f1p, tok,
           ins, ss, gs, gq, e0r, y0r, m1r, r1r, u0r, mr):
    iw, ino = lax.axis_index("wide"), lax.axis_index("narrow")
    b1x, b1y, z1 = bx // 2, by // 2, nz // 2
    b2x, b2y, z2 = bx // 4, by // 4, nz // 4
    x2, x3, x4 = nw * b2x, nw * b2x // 2, nw * b2x // 4
    there = []
    for dx, dy in SIDES:
        ok = None
        for cond, on in ((iw > 0, dx < 0), (iw < nw - 1, dx > 0), (ino > 0, dy < 0), (ino < nn - 1, dy > 0)):
            if on:
                ok = cond if ok is None else jnp.logical_and(ok, cond)
        there.append(ok)

    def peer(side):
        return (iw + SIDES[side][0], ino + SIDES[side][1])

    inputs = [pltpu.make_async_copy(src, dst, ins.at[0])
              for src, dst in ((m_hbm, m_ref), (s_hbm, s_ref), (c_hbm, c_ref))]
    for copy in inputs:
        copy.start()

    def clear(ref, index):
        ref[index] = jnp.zeros(ref[index].shape, F32)

    barrier = pltpu.get_barrier_semaphore()

    nb = nn // 2 * nw
    me, odd = ino // 2 * nw + iw, lax.rem(ino, 2)
    twin = ino + 1 - 2 * odd

    def fellow(j):
        to = me + j
        to = jnp.where(to >= nb, to - nb, to)
        row = to // nw
        return to - row * nw, 2 * row + odd

    def over_fellows(fn):
        if nb <= 16:
            for j in range(1, nb):
                fn(j)
        else:
            def step(j, _):
                fn(j)
                return 0

            lax.fori_loop(1, nb, step, 0)

    rounds = []
    while 1 << len(rounds) < nb:
        rounds.append(1 << len(rounds))

    def partner(d):
        to = me + d - 2 * d * lax.rem(me // d, 2)
        row = to // nw
        return to - row * nw, 2 * row + odd

    for d in rounds[1:]:
        pl.semaphore_signal(barrier, inc=1, device_id=partner(d), device_id_type=MESH)
    for k in range(8):
        @pl.when(there[k])
        def _():
            pl.semaphore_signal(barrier, inc=1, device_id=peer(k), device_id_type=MESH)

    def meet(n):
        if n > 0:
            pl.semaphore_wait(mr.at[n - 1], 1)
        if n <= len(rounds):
            to = partner(rounds[n]) if n < len(rounds) else (iw, twin)
            pl.semaphore_signal(mr.at[n], inc=1, device_id=to, device_id_type=MESH)

    beside_x = jnp.minimum(iw, 1) + jnp.minimum(nw - 1 - iw, 1)
    beside_y = jnp.minimum(ino, 1) + jnp.minimum(nn - 1 - ino, 1)
    pl.semaphore_wait(barrier, len(rounds) - 1 + beside_x + beside_y + beside_x * beside_y)

    def remote(src, dst, ssem, rsem, dev):
        return pltpu.make_async_remote_copy(src_ref=src, dst_ref=dst, send_sem=ssem, recv_sem=rsem,
                                            device_id=dev, device_id_type=MESH)

    def to_side(side, pairs, rsem):
        land = OPPOSITE[side]
        if rsem is e0r and land > 3:
            land -= 2
        return [remote(src, dst, ss.at[side], rsem.at[land], peer(side)) for src, dst in pairs]

    def e0_sends(side):
        land = OPPOSITE[side]
        if side < 2:
            pairs = []
            at = 0
            for ref, width in ((m_hbm, 2), (s_hbm, 1), (c_hbm, 1)):
                lo = 0 if side == 0 else bx - width
                pairs.append((ref.at[lo : lo + width], rx.at[land, at : at + width]))
                at += width
            return to_side(side, pairs, e0r)
        return to_side(side, [(cp.at[side - 4], rcn.at[land - 4])], e0r)

    def y0_sends(side, lo, hi, sem):
        land = OPPOSITE[side] - 2
        return [remote(yp.at[side - 2, lo:hi], ry.at[land, lo:hi], ss.at[side], y0r.at[sem + land], peer(side))]

    def each(fn, sides=range(8)):
        for side in sides:
            @pl.when(there[side])
            def _():
                fn(side)

    def start(copies):
        for copy in copies:
            copy.start()

    each(lambda k: start(e0_sends(k)), (0, 1))
    meet(0)
    view = tok.at[0 : 3 * bx * by * nz // 1024]
    pltpu.make_async_copy(view, view, ins.at[0]).wait()
    def yp_fill(side, at, ref, k):
        yp[side, at] = ref[:, by - 1 - k if side else k, :]

    for side in range(2):
        yp_fill(side, 0, m_ref, 0)
    each(lambda k: start(y0_sends(k, 0, 1, 0)), (2, 3))
    for side in range(2):
        for at, (ref, k) in enumerate(((m_ref, 1), (m_ref, 2), (s_ref, 0), (s_ref, 1), (c_ref, 0), (c_ref, 1))):
            yp_fill(side, 1 + at, ref, k)
    each(lambda k: start(y0_sends(k, 1, 7, 2)), (2, 3))
    for k in range(4, 8):
        dx, dy = SIDES[k]
        xa, xb = (0, 1) if dx < 0 else (bx - 1, bx - 2)
        ya, yb = (0, 1) if dy < 0 else (by - 1, by - 2)
        for i, (ref, x, y) in enumerate(((m_ref, xa, ya), (m_ref, xa, yb), (m_ref, xb, ya),
                                         (s_ref, xa, ya), (c_ref, xa, ya))):
            cp[k - 4, i] = ref[x, y : y + 1, :]

    each(lambda k: start(e0_sends(k)), (4, 5, 6, 7))

    near1 = ((1, 1), (1, 2), (1, 3), (2, 1), (2, 2), (3, 1))
    near_m1 = near1 + ((2, 3), (1, 4))

    def inside1(side, i, j):
        dx, dy = SIDES[side]
        return H1 + i - 1 if dx < 0 else H1 + b1x - i, b1y + j - 1 if dy < 0 else 2 * b1y - j

    def outside1(side, i, j):
        dx, dy = SIDES[side]
        return H1 - i if dx < 0 else H1 + b1x + i - 1, b1y - j if dy < 0 else 2 * b1y + j - 1

    def box1(side, sending, width):
        dx, dy = SIDES[side]
        w = width
        if sending:
            xlo, w = (H1, w) if dx < 0 else ((H1 + b1x - w, w) if dx > 0 else (H1, b1x))
            ylo = b1y
        else:
            xlo, w = (H1 - w, w) if dx < 0 else ((H1 + b1x, w) if dx > 0 else (H1, b1x))
            ylo = b1y * (1 + dy)
        return xlo, w, ylo

    def level1_sends(ref, rsem, side, width, kc):
        if side > 3:
            src, dst = (cs2, cr2) if kc else (cs1, cr1)
            return to_side(side, [(src.at[side - 4], dst.at[OPPOSITE[side] - 4])], rsem)
        if kc and side > 1:
            return to_side(side, [(qs1.at[side - 2], qr1.at[OPPOSITE[side] - 2])], rsem)
        sx, w, sy = box1(side, True, width)
        tx, _, ty = box1(OPPOSITE[side], False, width)
        return to_side(side, [(ref.at[:, sx : sx + w, sy : sy + b1y], ref.at[:, tx : tx + w, ty : ty + b1y])], rsem)

    def r1_pack(side):
        for x in range(b1x):
            rs, rc = r1[0, H1 + x, own_y, :], r1[1, H1 + x, own_y, :]
            qs1[side - 2, x] = top_bottom(rs, shift(rc, 4, 0)) if side == 2 else top_bottom(shift(rs, 4, 0), rc)

    def r1_unpack(side):
        rows = side_rows[side - 2]
        for x in range(b1x):
            tile = qr1[side - 2, x]
            other = shift(tile, 4, 0)
            r1[0, H1 + x, rows, :] = other if side == 2 else tile
            r1[1, H1 + x, rows, :] = tile if side == 2 else other

    def level1_landed(ref, rsem, width, kc):
        def fn(side):
            if side > 3:
                view = (cr2 if kc else cr1).at[side - 4]
            elif kc and side > 1:
                view = qr1.at[side - 2]
            else:
                tx, w, ty = box1(side, False, width)
                view = ref.at[:, tx : tx + w, ty : ty + b1y]
            pltpu.make_async_copy(view, view, rsem.at[side]).wait()
        return fn

    def e0_landed(side):
        if side in (2, 3):
            view = ry.at[side - 2, 1:7]
            pltpu.make_async_copy(view, view, y0r.at[side]).wait()
        else:
            view = rx.at[side] if side < 2 else rcn.at[side - 4]
            pltpu.make_async_copy(view, view, e0r.at[side if side < 2 else side - 2]).wait()

    def near_landed(side):
        view = ry.at[side - 2, 0:1]
        pltpu.make_async_copy(view, view, y0r.at[side - 2]).wait()

    own_y = slice(b1y, 2 * b1y)
    for i in range(b1x):
        put_halves(t0, 0, slice(i * by, (i + 1) * by), m_ref[2 * i] + m_ref[2 * i + 1])
    for i in range(b1x):
        m1[0, H1 + i, own_y, :] = 0.125 * yz_pairs(t0, 0, i * by)
    for k in range(4, 8):
        for n, (i, j) in enumerate(near_m1):
            x, y = inside1(k, i, j)
            cs1[k - 4, n : n + 1, :] = m1[0, x, y : y + 1, :]
    low2 = iota(TILE, 1) < z2
    for i in range(0, b2x, 4):
        tiles = []
        for n in range(i, i + 4, 2):
            quads = [y_pairs(m1[0, H1 + 2 * k, own_y, :] + m1[0, H1 + 2 * k + 1, own_y, :]) for k in (n, n + 1)]
            tiles.append(0.125 * z_pairs(top_bottom(quads[0], quads[1])))
        mob2 = jnp.where(low2, tiles[0], tiles[1])
        sm2[2 * i : 2 * i + 8, :] = mob2
        gm[odd, me, 2 * i : 2 * i + 8, :] = mob2

    def send_sem(kind):
        return gs.at[gs.shape[0] - 1 if kind > 3 else min(kind, gs.shape[0] - 2)]

    def to_fellows(src, dst, kind):
        over_fellows(lambda j: remote(src, dst, send_sem(kind), gq.at[kind], fellow(j)).start())

    def to_twin(src, dst, kind):
        remote(src, dst, send_sem(kind), gq.at[kind], (iw, twin)).start()

    def to_others(src, dst, kind):
        def to_one(j):
            to = me + j
            to = jnp.where(to >= nb, to - nb, to)
            row = to // nw
            remote(src, dst, send_sem(kind), gq.at[kind], (to - row * nw, 2 * row + 1 - odd)).start()

        if nb <= 16:
            for j in range(nb):
                to_one(j)
        else:
            def step(j, _):
                to_one(j)
                return 0

            lax.fori_loop(0, nb, step, 0)

    def landed(view, kind):
        pltpu.make_async_copy(view, view, gq.at[kind]).wait()

    for ref, src, width in ((m0, m_ref, 2), (rs0, s_ref, 1), (rc0, c_ref, 1)):
        blank = jnp.zeros(m0.shape[1:], F32)
        for i in range(width):
            ref[H0 - 1 - i] = blank
            ref[H0 + bx + i] = blank

        def put(i):
            ref[H0 + i, H0 : H0 + by, :] = src[i]

        slabs(0, bx, bx, put)
    side_rows = (slice(0, b1y), slice(2 * b1y, 3 * b1y))
    for k in range(8):
        @pl.when(jnp.logical_not(there[k]))
        def _():
            if k > 3:
                clear(rcn, k - 4)
                clear(cr1, k - 4)
                clear(cr2, k - 4)
                return
            lands = ((rx, hx, hxc, hu, h1, hc) if k < 2 else (ry, hy, qr1))
            for ref in lands:
                clear(ref, k % 2)
            for ref, width in (((m1, 3), (r1, 2)) if k < 2 else ((m1, 3),)):
                xlo, w, ylo = box1(k, False, width)
                clear(ref, (slice(None), slice(xlo, xlo + w), slice(ylo, ylo + b1y)))
    for a in (0, H1 + b1x + 3):
        clear(m1, (0, a))
    for a in (1, 2, 3, H1 + b1x, H1 + b1x + 1, H1 + b1x + 2):
        for rows in side_rows:
            clear(m1, (0, a, rows))
            for v in range(2):
                clear(r1, (v, a, rows))
    for ref in (us0, uc0):
        ref[H0 - 2] = jnp.zeros(m0.shape[1:], F32)
        ref[H0 + bx + 1] = jnp.zeros(m0.shape[1:], F32)
    for a in (0, 1, 2, 3, H1 + b1x, H1 + b1x + 1, H1 + b1x + 2, H1 + b1x + 3):
        for v in range(2):
            v1[v, a] = jnp.zeros(v1.shape[2:], F32)
    for ref in (u4, v4):
        zero = jnp.zeros(ref.shape[1:], F32)
        for a in (0, 1, ref.shape[0] - 2, ref.shape[0] - 1):
            ref[a] = zero
    for ref in (u2, v2, r2, cx2, cy2, cz2, rd2, u3, v3, r3, cx3, cy3, cz3, rd3):
        zero = jnp.zeros(ref.shape[1:], F32)
        for a in range(PAD2):
            ref[a] = zero
            ref[ref.shape[0] - 1 - a] = zero
    cx4[PAD - 1] = jnp.zeros(cx4.shape[1:], F32)

    ops0 = (cx0, cy0, cz0, rd0, d0)
    firsts0 = ((rs0, us0), (rc0, uc0))
    meet(1)
    each(near_landed, (2, 3))
    m0[H0 : H0 + bx, H0 - 1, :] = ry[0, 0]
    m0[H0 : H0 + bx, H0 + by, :] = ry[1, 0]
    for side, a in enumerate((H0 + 1, H0 + bx - 2)):
        build(m0, cx0, cy0, cz0, rd0, d0, a, 1, BASE_TAU, nz, 1, firsts0)
        for v, ref in enumerate((us0, uc0)):
            xu[side, v] = ref[a, H0 : H0 + by, :]
    each(lambda k: start(to_side(k, [(xu.at[k], hu.at[OPPOSITE[k]])], u0r)), (0, 1))
    each(lambda k: start(level1_sends(m1, m1r, k, 3, 0)))
    each(e0_landed, (2, 3))
    for ref, at, lo, width in ((m0, 1, 1, 2), (rs0, 3, 0, 2), (rc0, 5, 0, 2)):
        for i in range(width):
            ref[H0 : H0 + bx, H0 - 1 - lo - i, :] = ry[0, at + i]
            ref[H0 : H0 + bx, H0 + by + lo + i, :] = ry[1, at + i]

    meet(2)
    build(m0, cx0, cy0, cz0, rd0, d0, H0 + 1, bx - 2, BASE_TAU, nz, bx - 2, firsts0)
    sweep((us0, uc0), (vs0, vc0), (rs0, rc0), ops0, H0 + 2, bx - 4, bx - 4)

    def down0(i, carry):
        num, den = carry
        sums = []
        for k in range(2):
            a = H0 + 2 * i + k
            vs, es = residual(vs0, rs0, a, ops0)
            vc, ec = residual(vc0, rc0, a, ops0)
            both = es + rs0[a]
            num = num + fold_own(both * vc)
            den = den + fold_own(both * vs)
            sums.append((es, ec))
        at = slice(i * m0.shape[1], (i + 1) * m0.shape[1])
        put_halves(t0, 0, at, sums[0][0] + sums[1][0])
        put_halves(t0, 1, at, sums[0][1] + sums[1][1])
        return num, den

    zero8 = jnp.zeros(TILE, F32)
    part0 = loop(b1x - 4, b1x - 4, lambda i, c: down0(2 + i, c), (zero8, zero8))


    def coarse0(i):
        for v in range(2):
            r1[v, H1 + i, own_y, :] = 0.125 * yz_pairs(t0, v, i * m0.shape[1] + H0)

    slabs(2, b1x - 4, b1x - 4, coarse0)
    meet(3)
    def u0_landed(side):
        pltpu.make_async_copy(hu.at[side], hu.at[side], u0r.at[side]).wait()

    each(e0_landed, (0, 1, 4, 5, 6, 7))
    for n in range(4, len(rounds) + 1):
        meet(n)
    to_fellows(sm2, gm.at[odd, me], 0)
    for ref, at, width in ((m0, 0, 2), (rs0, 2, 1), (rc0, 3, 1)):
        for i in range(width):
            ref[H0 - width + i, H0 : H0 + by, :] = rx[0, at + i]
            ref[H0 + bx + i, H0 : H0 + by, :] = rx[1, at + i]
    for k in range(4):
        dx, dy = SIDES[4 + k]
        xa, xb = (H0 - 1, H0 - 2) if dx < 0 else (H0 + bx, H0 + bx + 1)
        ya, yb = (H0 - 1, H0 - 2) if dy < 0 else (H0 + by, H0 + by + 1)
        for i, (ref, x, y) in enumerate(((m0, xa, ya), (m0, xa, yb), (m0, xb, ya), (rs0, xa, ya), (rc0, xa, ya))):
            ref[x, y : y + 1, :] = rcn[k, i]
    beyond = m0[H0 - 2]
    own = m0[H0 - 1]
    cx0[H0 - 2] = jnp.where(jnp.minimum(own, beyond) > 0.0, rounded(0.5 * BASE_TAU * (own + beyond)), 0.0)
    for lo in (H0 - 1, H0 + bx - 1):
        build(m0, cx0, cy0, cz0, rd0, d0, lo, 2, BASE_TAU, nz, 2, firsts0)
    each(u0_landed, (0, 1))
    for v, ref in enumerate((us0, uc0)):
        ref[H0 - 2, H0 : H0 + by, :] = hu[0, v]
        ref[H0 + bx + 1, H0 : H0 + by, :] = hu[1, v]
    for v_lo in (H0 - 1, H0 + bx - 2):
        sweep((us0, uc0), (vs0, vc0), (rs0, rc0), ops0, v_lo, 3, 3)
    num0, den0 = loop(2, 2, lambda i, c: down0(b1x - 2 + i, down0(i, c)), part0)
    for i in (0, 1, b1x - 2, b1x - 1):
        coarse0(i)
    for k in range(4, 8):
        for n in range(6):
            x, y = inside1(k, 1, 1 + n // 2)
            cs2[k - 4, n] = r1[n % 2, x, y : y + 1, :]
    for k in (2, 3):
        r1_pack(k)
    each(lambda k: start(level1_sends(r1, r1r, k, 2, 1)), (4, 5, 6, 7, 0, 1, 2, 3))
    for side, (x_far, x_near) in enumerate(((H0 + 1, H0), (H0 + bx - 2, H0 + bx - 1))):
        for v, ref in enumerate((vs0, vc0)):
            xv[side, v] = ref[x_far, H0 : H0 + by, :]
            xc[side, 2 * v] = ref[x_near, H0 - 1 : H0, :]
            xc[side, 2 * v + 1] = ref[x_near, H0 + by : H0 + by + 1, :]
    for side, col in enumerate((H0 + 1, H0 + by - 2)):
        for v, ref in enumerate((vs0, vc0)):
            yv[side, v] = ref[H0 : H0 + bx, col, :]

    def v0_sends(side):
        land = OPPOSITE[side]
        if side < 2:
            return to_side(side, [(xv.at[side], hx.at[land]), (xc.at[side], hxc.at[land])], e0r)
        return [remote(yv.at[side - 2], hy.at[land - 2], ss.at[side], y0r.at[land], peer(side))]

    each(level1_landed(m1, m1r, 3, 0))
    for k in range(4, 8):
        for n, (i, j) in enumerate(near_m1):
            x, y = outside1(k, i, j)
            m1[0, x, y : y + 1, :] = cr1[k - 4, n : n + 1, :]
    ops1 = (cx1, cy1, cz1, rd1, d1)
    build(m1.at[0], cx1, cy1, cz1, rd1, d1, H1 - 3, b1x + 6, BASE_TAU / 4, z1, b1x + 6)
    rr1 = (r1.at[0], r1.at[1])
    uu1 = (u1.at[0], u1.at[1])
    vv1 = (v1.at[0], v1.at[1])
    halves1 = {}

    def first1(a):
        for v in range(2):
            u1[v, a] = rd1[a] * r1[v, a]

    def down1(i, carry):
        num, den = carry
        pair = []
        for k in range(2):
            a = H1 + 2 * i + k
            vs, es = residual(vv1[0], rr1[0], a, ops1)
            vc, ec = residual(vv1[1], rr1[1], a, ops1)
            both = (es + r1[0, a])[own_y]
            num = num + both * vc[own_y]
            den = den + both * vs[own_y]
            pair.append((es[own_y], ec[own_y]))
        halves1[i] = [y_pairs(pair[0][v] + pair[1][v]) for v in range(2)]
        return num, den

    landed1 = level1_landed(r1, r1r, 2, 1)
    each(landed1, (2, 3))
    for k in (2, 3):
        r1_unpack(k)
    slabs(H1, b1x, b1x, first1)
    sweep(uu1, vv1, rr1, ops1, H1 + 1, b1x - 2, b1x - 2)
    sums1 = loop(b2x - 2, b2x - 2, lambda i, c: down1(1 + i, c), (zero8, zero8))
    each(landed1, (0, 1, 4, 5, 6, 7))
    for k in range(4, 8):
        for n in range(6):
            x, y = outside1(k, 1, 1 + n // 2)
            r1[n % 2, x, y : y + 1, :] = cr2[k - 4, n]
    for a in (H1 - 2, H1 + b1x):
        slabs(a, 2, 2, first1)
    for a in (H1 - 1, H1 + b1x - 1):
        sweep(uu1, vv1, rr1, ops1, a, 2, 2)
    num1, den1 = down1(b2x - 1, down1(0, sums1))
    for i in range(0, b2x, 2):
        packed = [z_pairs(top_bottom(halves1[i][v], halves1[i + 1][v])) for v in range(2)]
        own2 = 0.125 * jnp.where(low2, packed[0], packed[1])
        sr2[i * b2y : (i + 2) * b2y, :] = own2
        gr[odd, me, i * b2y : (i + 2) * b2y, :] = own2
    meet(len(rounds) + 1)
    to_fellows(sr2, gr.at[odd, me], 2)
    num_row = jnp.sum(num0 + 8.0 * num1, axis=0, keepdims=True)
    den_row = jnp.sum(den0 + 8.0 * den1, axis=0, keepdims=True)
    low1 = iota((1, 128), 1) < 64
    part = jnp.where(low1, num_row + shift(num_row, 64, 1), den_row + shift(den_row, 64, 1))
    sp2[...] = part
    mine = odd * nb + me
    gp[mine] = part
    to_fellows(sp2, gp.at[mine], 4)
    to_others(sp2, gp.at[mine], 4)

    def v1_corners(side, ref_v, ref_r, tiles, outward):
        for d in range(2):
            corner = 4 + 2 * side + d
            for n, (i, j) in enumerate(near1 + ((1, 2), (2, 1))):
                x = (outside1 if outward else inside1)(corner, i, j)[0]
                y = outside1(corner, i, j)[1]
                ref = ref_v if n < 6 else ref_r
                for v in range(2):
                    if outward:
                        ref[v, x, y : y + 1, :] = tiles[side, v, d, n : n + 1, :]
                    else:
                        tiles[side, v, d, n : n + 1, :] = ref[v, x, y : y + 1, :]

    for side in range(2):
        v1_corners(side, v1, r1, cv1, False)
    landed(gm.at[0, 0 : nb - 1], 0)
    to_twin(gm.at[odd], gm.at[odd], 1)
    landed(gm.at[0], 1)
    def v1_sends(side):
        land = OPPOSITE[side]
        lo = H1 if side == 0 else H1 + b1x - 3
        return to_side(side, [(v1.at[:, lo : lo + 3, own_y], h1.at[land]), (cv1.at[side], hc.at[land])], u0r)


    def unpack(src, dst, u=None):
        def step(w, carry):
            for i in range(b2x):
                a = PAD2 + w * b2x + i
                for n in range(nn):
                    dst[a, n * b2y : (n + 1) * b2y, :] = src[n % 2, n // 2 * nw + w, i * b2y : (i + 1) * b2y, :]
                if u is not None:
                    u[a] = rd2[a] * dst[a]
            return carry

        loop(nw, 8, step, 0)

    def unpack_m(w, carry):
        for n in range(nn):
            for i in range(0, b2x, 4):
                tile = gm[n % 2, n // 2 * nw + w, 2 * i : 2 * i + 8, :]
                other = shift(tile, z2, 1)
                for k, part in enumerate((jnp.where(low2, tile, other), jnp.where(low2, other, tile))):
                    for h in range(2):
                        a = PAD2 + w * b2x + i + 2 * k + h
                        v2[a, n * b2y : (n + 1) * b2y, :] = part[h * b2y : (h + 1) * b2y, :]
        return carry

    loop(nw, 8, unpack_m, 0)
    kept2 = d2 if d2.shape == v2.shape else None
    build(v2, cx2, cy2, cz2, rd2, kept2, PAD2, x2, BASE_TAU / 16, z2, 16)

    def coarsen_y(x):
        if x.shape[0] == 16:
            return top_bottom(y_pairs(x[0:8]), y_pairs(x[8:16]))
        return top_bottom(y_pairs(x), 0.0)

    def coarsen_z(dst, lo, count):
        def body(a):
            dst[a] = 0.125 * z_pairs(dst[a])

        slabs(lo, count, min(count, 16), body)

    def coarsen_pairs(src, dst, xc, pad):
        def body(i, carry):
            a = PAD2 + 2 * i
            dst[pad + i] = coarsen_y(src[a] + src[a + 1])
            return carry

        loop(xc, 16, body, 0)
        coarsen_z(dst, pad, xc)

    coarsen_pairs(v2, v3, x3, PAD2)
    build(v3, cx3, cy3, cz3, rd3, d3, PAD2, x3, BASE_TAU / 64, z2 // 2, 16)
    coarsen_pairs(v3, v4, x4, PAD)
    build(v4, cx4, cy4, cz4, rd4, None, PAD, x4, BASE_TAU / 256, z2 // 4, 8)

    each(lambda k: start(v1_sends(k)), range(2))
    each(lambda k: start(v0_sends(k)), range(4))
    landed(gr.at[0, 0 : nb - 1], 2)
    to_twin(gr.at[odd], gr.at[odd], 3)


    def v0_landed(side):
        view = tok.at[0 : (2 * by + 4) * nz // 1024] if side < 2 else hy.at[side - 2]
        pltpu.make_async_copy(view, view, e0r.at[side] if side < 2 else y0r.at[side]).wait()

    landed(gr.at[0], 3)
    unpack(gr, r2, u2)

    ops2 = (cx2, cy2, cz2, rd2, kept2)
    ops3 = (cx3, cy3, cz3, rd3, d3)
    ops4 = (cx4, cy4, cz4, rd4, None)

    def coarsen_residual(v, r, ops, dst, xc, pad, seg):
        low = iota(v.shape[1:], 1) < seg

        def step(i, carry):
            num, den = carry
            pair = []
            for j in range(2):
                a = PAD2 + 2 * i + j
                own, e = residual(v, r, a, ops)
                both = jnp.where(low, e + r[a], 0.0)
                num = num + fold(both * shift(own, -seg, 1))
                den = den + fold(both * own)
                pair.append(e)
            dst[pad + i] = coarsen_y(pair[0] + pair[1])
            return num, den

        sums = loop(xc, 16, step, (zero8, zero8))
        coarsen_z(dst, pad, xc)
        return sums

    sweep((u2,), (v2,), (r2,), ops2, PAD2, x2, 32)
    landed(gp.at[0 : 2 * nb - 1], 4)
    whole = loop(2 * nb, 32, lambda i, acc: acc + gp[i], jnp.zeros((1, 128), F32))
    num2, den2 = coarsen_residual(v2, r2, ops2, r3, x3, PAD2, z2)
    def first3(a):
        u3[a] = rd3[a] * r3[a]

    if x3 <= 16:
        sweep((Scaled(rd3, r3, PAD2, PAD2 + x3),), (v3,), (r3,), ops3, PAD2, x3, 16)
    else:
        slabs(PAD2, x3, 16, first3)
        sweep((u3,), (v3,), (r3,), ops3, PAD2, x3, 16)
    num3, den3 = coarsen_residual(v3, r3, ops3, r4, x4, PAD, z2 // 2)

    def first4(a):
        u4[a] = rd4[a] * r4[a]

    if x4 <= 8:
        sweep((Scaled(rd4, r4, PAD, PAD + x4),), (v4,), (r4,), ops4, PAD, x4, 8)
    else:
        slabs(PAD, x4, 8, first4)
        sweep((u4,), (v4,), (r4,), ops4, PAD, x4, 8)
    low4 = iota(TILE, 1) < z2 // 4

    def dots(i, carry):
        num, den = carry
        for k in range(8):
            a = PAD + 8 * i + k
            both = jnp.where(low4, r4[a], 0.0)
            den = den + both * v4[a]
            num = num + both * shift(v4[a], -(z2 // 4), 1)
        return num, den

    num4, den4 = dots(0, (zero8, zero8)) if x4 == 8 else lax.fori_loop(0, x4 // 8, dots, (zero8, zero8))
    b3x = b2x // 2
    base3 = PAD2 + iw * b3x
    for i in range(b3x // 2 + 4):
        add = y_repeat(z_repeat(v4[PAD + iw * (b3x // 2) - 2 + i]))
        for j in range(2):
            a = base3 - 4 + 2 * i + j
            v3[a] = v3[a] + add
    sweep((v3,), (u3,), (r3,), ops3, base3 - 3, b3x + 6, b3x + 6)
    sweep((u3,), (v3,), (r3,), ops3, base3 - 2, b3x + 4, b3x + 4)

    def total_of(mask, n2, n3, n4):
        x = jnp.sum(64.0 * n2 + 512.0 * n3 + 4096.0 * n4, axis=0, keepdims=True)
        return jnp.sum(x + jnp.where(mask, whole, 0.0), axis=1, keepdims=True)

    ratio = total_of(low1, num2, num3, num4) / (1.0 + total_of(jnp.logical_not(low1), den2, den3, den4))
    ratio = jnp.broadcast_to(ratio, (1, 128))
    base = PAD2 + iw * b2x
    for i in range(b2x // 2 + 4):
        wide_tile = z_repeat(v3[base3 - 2 + i])
        for j in range(2):
            a = base - 4 + 2 * i + j
            v2[a, 0:8, :] = v2[a, 0:8, :] + y_repeat(wide_tile)
            v2[a, 8:16, :] = v2[a, 8:16, :] + y_repeat(wide_tile, 4)
    sweep((v2,), (u2,), (r2,), ops2, base - 3, b2x + 6, b2x + 6)
    sweep((u2,), (v2,), (r2,), ops2, base - 2, b2x + 4, b2x + 4)

    def v1_landed(side):
        view = tok.at[0 : 10]
        pltpu.make_async_copy(view, view, u0r.at[side]).wait()

    each(v1_landed, range(2))
    for side, a in enumerate((H1 - 3, H1 + b1x)):
        v1[:, a : a + 3, own_y] = h1[side]
        v1_corners(side, v1, r1, hc, True)
    rows2 = v2.shape[1]
    full_y = 2 * rows2
    for i in range(b2x + 4):
        f1p[i, 0:b1y, :] = jnp.zeros((b1y, z1), F32)
        f1p[i, b1y + full_y : 2 * b1y + full_y, :] = jnp.zeros((b1y, z1), F32)
        for j in range(rows2 // 8):
            e = v2[base - 2 + i, 8 * j : 8 * j + 8, :]
            part = z_repeat(shift(e, z2, 1) - ratio * e)
            f1p[i, pl.ds(b1y + 16 * j, 8, stride=2), :] = part
            f1p[i, pl.ds(b1y + 16 * j + 1, 8, stride=2), :] = part
    window = pl.ds(pl.multiple_of(ino * b1y, 8), 3 * b1y)
    for x in range(-3, b1x + 3):
        a = H1 + x
        u1[0, a] = v1[1, a] - ratio * v1[0, a] + f1p[x // 2 + 2, window, :]
        if -2 <= x < b1x + 2:
            w1[a] = r1[1, a] - ratio * r1[0, a]
    sweep((u1.at[0],), (u1.at[1],), (w1,), ops1, H1 - 2, b1x + 4, b1x + 4)
    sweep((u1.at[1],), (u1.at[0],), (w1,), ops1, H1 - 1, b1x + 2, b1x + 2)

    each(v0_landed, range(4))
    for side, (x_far, x_near) in enumerate(((H0 - 2, H0 - 1), (H0 + bx + 1, H0 + bx))):
        for v, ref in enumerate((vs0, vc0)):
            ref[x_far, H0 : H0 + by, :] = hx[side, v]
            ref[x_near, H0 - 1 : H0, :] = hxc[side, 2 * v]
            ref[x_near, H0 + by : H0 + by + 1, :] = hxc[side, 2 * v + 1]
    for side, col in enumerate((H0 - 2, H0 + by + 1)):
        for v, ref in enumerate((vs0, vc0)):
            ref[H0 : H0 + bx, col, :] = hy[side, v]
    ratio0 = jnp.concatenate([ratio] * (nz // 128), axis=1)

    def up0(g):
        tiles = [[u1[0, H1 - 1 + 2 * g + k, 8 * j : 8 * j + 8, :] for j in range(3)] for k in range(2)]
        sub = iota(TILE, 0)
        ends = [top_bottom(jnp.where(sub < 2, shift(t[0], 2, 0), shift(t[2], 2, 0)), 0.0) for t in tiles]
        ends = top_bottom(ends[0], shift(ends[1], 4, 0))
        halves = [[z_repeat(t, start) for t in (ends, tiles[0][1], tiles[1][1])] for start in (0, 64)]
        for k in range(2):
            adds = []
            for end, mid in ((h[0], h[1 + k]) for h in halves):
                end = shift(end, -4 * k, 0) if k else end
                adds.append((top_bottom(y_repeat(end), y_repeat(mid, -2)), y_repeat(mid, 2),
                             top_bottom(y_repeat(mid, 6), y_repeat(end))))
            add = jnp.concatenate([jnp.concatenate([adds[0][j], adds[1][j]], axis=1) for j in range(3)], axis=0)
            for i in range(2):
                a = H0 - 2 + 4 * g + 2 * k + i
                us0[a] = vc0[a] - ratio0 * vs0[a] + add
                rc0[a] = rc0[a] - ratio0 * rs0[a]

    slabs(0, b1x // 2 + 1, b1x // 2 + 1, up0)
    sweep((us0,), (uc0,), (rc0,), ops0, H0 - 1, bx + 2, bx + 2)

    def last(a):
        own, t = neighbours(uc0, a, cx0, cy0, cz0)
        out_ref[a - H0] = (KEEP * own + rd0[a] * (rc0[a] + t))[H0 : H0 + by]

    slabs(H0, bx, bx, last)

    def sent(side):
        dx, dy = SIDES[side]
        if dy == 0:
            tiles = 6 * by * nz // 1024 + 3 + 4 + (2 * by + 4) * nz // 1024 + 10
        elif dx == 0:
            tiles = 7 * bx * nz // 1024 + b1x + b1x + 2 * bx * nz // 1024
        else:
            tiles = 3
        view = tok.at[0:tiles]
        pltpu.make_async_copy(view, view, ss.at[side]).wait()

    each(sent)
    if gs.shape[0] == 2:
        views = (tok.at[0 : 3 * (nb - 1) + 3 * nb],)
    else:
        views = (gm.at[0, 0 : nb - 1], gm.at[0], gr.at[0, 0 : nb - 1], gr.at[0])
    views += (gp.at[0 : 2 * nb - 1],)
    for i, view in enumerate(views):
        pltpu.make_async_copy(view, view, gs.at[i]).wait()


def solution(mesh):
    nw, nn = mesh.shape["wide"], mesh.shape["narrow"]

    def per_device(mobility, sav_vector, cotangent):
        bx, by, nz = mobility.shape
        b1x, b1y, z1 = bx // 2, by // 2, nz // 2
        x2, y2 = nw * bx // 4, nn * by // 4
        own = (bx, by, nz)
        l0 = (bx + 2 * H0, by + 2 * H0, nz)
        l1 = (b1x + 2 * H1, 3 * b1y, z1)
        l2 = (x2 + 2 * PAD2, y2, z1)
        l3 = (x2 // 2 + 2 * PAD2, y2 // 2, z1)
        l4 = (x2 // 4 + 2 * PAD, 8, z1)
        own2 = (bx // 4 * (by // 4), z1)
        half2 = (bx // 4 * (by // 4) // 2, z1)
        buffers = (
            [own] * 3 + [l0] * 12
            + [(2, 4, by, nz), (2, 7, bx, nz), (2, 7, bx, nz), (4, 5, 1, nz), (4, 5, 1, nz)]
            + [(2, 2, by, nz)] * 2 + [(2, 4, 1, nz)] * 2 + [(2, 2, bx, nz)] * 2 + [(2, 2, by, nz)] * 2
            + [(1, *l1)] + [l1] * 5 + [(2, *l1)] * 3 + [l1] + [(2, 2, 3, b1y, z1), (2, 2, 2, b1y, z1), (2, 2, 2, b1y, z1), (4, *TILE), (4, *TILE), (4, 6, 1, z1), (4, 6, 1, z1), (2, b1x, *TILE), (2, b1x, *TILE)]
            + [l2] * 7 + [l2 if nw <= 16 else (1, *TILE)] + [l3] * 8 + [l4] * 7
            + [(2, 2, b1x * l0[1], nz // 2)]
            + [half2, own2, (1, 128), (2, nn // 2 * nw, *half2), (2, nn // 2 * nw, *own2), (nn * nw, 1, 128)]
            + [(bx // 4 + 4, 2 * y2 + 2 * b1y, z1), (3 * bx * by * nz // 1024, *TILE)]
        )
        size = sum(4 * functools.reduce(lambda p, q: p * q, shape) for shape in buffers)
        dma = lambda n: pltpu.SemaphoreType.DMA((n,))
        scratch = [pltpu.VMEM(shape, F32) for shape in buffers]
        scratch += [dma(n) for n in (1, 8, 2 if nn // 2 * nw <= 16 else 5, 5, 6, 4, 8, 8, 2)]
        steps = (nn // 2 * nw - 1).bit_length() + 1
        scratch.append(pltpu.SemaphoreType.REGULAR((steps,)))
        return pl.pallas_call(
            functools.partial(kernel, nw, nn, bx, by, nz),
            out_shape=jax.ShapeDtypeStruct((bx, by, nz), F32),
            in_specs=[pl.BlockSpec(memory_space=pltpu.HBM)] * 3,
            out_specs=pl.BlockSpec(memory_space=pltpu.VMEM),
            scratch_shapes=scratch,
            compiler_params=pltpu.CompilerParams(
                collective_id=0, has_side_effects=True, vmem_limit_bytes=GRANT if size < GRANT else 67043328
            ),
        )(mobility, sav_vector, cotangent)

    spec = P("wide", "narrow", None)
    return jax.shard_map(per_device, mesh=mesh, in_specs=(spec,) * 3, out_specs=spec, check_vma=False)
```
